32 devices in a mesh: row: 4 (over y, x), col: 8 (over z, core).
Axes of the slice: x: 2, y: 2, z: 4, core: 2. Of those that a mesh axis runs over, the one named last changes fastest.
Arguments:
- anc_inverse: float32 [10240, 10240], P('row', 'col'), may hold values from -0.0625 to 0.0625
- lower_anc: float32 [10240, 3, 384], P('col', None, 'row'), may hold values from -1.5 to 1.5
- upper_anc: float32 [10240, 3, 384], P('row', None, 'col'), may hold values from -0.75 to 0.75
- lower_edge: float32 [2, 384, 384], replicated, may hold values from -0.3125 to 0.3125
- upper_edge: float32 [2, 384, 384], replicated, may hold values from -0.3125 to 0.3125
- diag_inverse: float32 [3, 384, 384], replicated, may hold values from -6 to 6
- tile_mask: int32 [3, 80, 3], replicated, may hold values 0 or 1
Outputs:
- x_blocks: float32 [10240, 3, 384], P(('row', 'col'))
- y_blocks: float32 [8, 4, 320, 3, 384], P('col', 'row')
- z_blocks: float32 [3, 384, 384], P(None, 'row', 'col')
- cross_blocks: float32 [2, 2, 384, 384], P(None, None, 'row', 'col')
The draws below stay inside these ranges and needn't reach their ends.
All inputs are finite; a program needn't handle non-finite values.
Results may differ from the reference program's by a relative error of at most 0.0001.
Values sent between devices are 32-bit elements; how exact they have to be, the bound alone decides.
A program may use at most 128 MiB of HBM per device.

```python
import jax
import jax.numpy as jnp
from jax import lax

ANC = 10240
W = 384
BLK = 128
SUPER = 3
EDGES = 2
NBLK = 80
WB = 3
PROW = 4
PCOL = 8
SLAB = 320


def with_ends(entries, stream_key, smallest, high):
    dims = entries.shape
    spot = [jax.random.randint(jax.random.fold_in(stream_key, axis), (), 0, dims[axis]) for axis in range(len(dims))]
    entries = entries.at[tuple(spot)].set(smallest)
    longest = dims.index(max(dims))
    spot[longest] = (spot[longest] + 1) % dims[longest]
    return entries.at[tuple(spot)].set(high)


def level_of(rng, shape, shards, low, largest):
    loudness = 1.0
    for dim, blocks in shards:
        steps = jax.random.uniform(jax.random.fold_in(jax.random.fold_in(rng, 6), dim), (blocks,), jnp.float32, low / len(shards), largest / len(shards))
        loudness = loudness * jnp.repeat(jnp.exp(steps), shape[dim] // blocks).reshape((-1,) + (1,) * (len(shape) - 1 - dim))
    return loudness


def gaussian(rng, dims, width, most, shards=(), held_as=jnp.bfloat16):
    array = jax.random.normal(rng, dims, jnp.float32) * width
    if len(shards) > 0:
        array = level_of(rng, dims, shards, -0.22, 0.18) * array
    return jnp.clip(array, min=-most, max=most).astype(held_as)


def setup_inputs(seed: int = 0) -> dict:
    seeds = jax.random.split(jax.random.key(seed), 8)
    anc_inverse = gaussian(seeds[0], (ANC, ANC), ANC ** -0.5, 0.0625, ((0, 4), (1, 8)), jnp.float32)
    lower_anc = gaussian(seeds[1], (ANC, SUPER, W), 0.25, 1.5, ((0, 8), (2, 4)), jnp.float32)
    upper_anc = gaussian(seeds[2], (ANC, SUPER, W), 0.125, 0.75, ((0, 4), (2, 8)), jnp.float32)
    lower_edge = gaussian(seeds[3], (EDGES, W, W), W ** -0.5, 0.3125, (), jnp.float32)
    upper_edge = gaussian(seeds[4], (EDGES, W, W), W ** -0.5, 0.3125, (), jnp.float32)
    diag_inverse = gaussian(seeds[5], (SUPER, W, W), 1.0, 6.0, (), jnp.float32)
    tile_mask = with_ends((jax.random.randint(seeds[6], (SUPER, NBLK, WB), 0, 4) < 3).astype(jnp.int32), jax.random.fold_in(seeds[6], 1), 0, 1)
    return {"anc_inverse": anc_inverse, "lower_anc": lower_anc, "upper_anc": upper_anc, "lower_edge": lower_edge, "upper_edge": upper_edge, "diag_inverse": diag_inverse, "tile_mask": tile_mask}


precise = lax.Precision.HIGHEST


def product(left, right):
    return jnp.dot(left, right, precision=precise, preferred_element_type=jnp.float32)


def expand_tiles(mask_rows):
    filled = mask_rows.astype(jnp.float32)
    return jnp.repeat(jnp.repeat(filled, BLK, axis=0), BLK, axis=1)


def reference(anc_inverse, lower_anc, upper_anc, lower_edge, upper_edge, diag_inverse, tile_mask):
    cols_list = []
    rows_list = []
    corner_list = []
    cross_cols = []
    cross_rows = []
    for node_index in range(SUPER):
        pattern = expand_tiles(tile_mask[node_index])
        lower_cur = lower_anc[:, node_index, :] * pattern
        upper_cur = upper_anc[:, node_index, :] * pattern
        inv_cols = -product(anc_inverse, lower_cur)
        inv_rows = -product(upper_cur.T, anc_inverse).T
        if node_index > 0:
            lower_side = lower_edge[node_index - 1]
            upper_side = upper_edge[node_index - 1]
            prev_cols = cols_list[-1]
            prev_rows = rows_list[-1]
            prev_corner = corner_list[-1]
            cross_col = -(product(prev_rows.T, lower_cur) + product(prev_corner, lower_side))
            cross_row = -(product(upper_cur.T, prev_cols) + product(upper_side, prev_corner))
            inv_cols = inv_cols - product(prev_cols, lower_side)
            inv_rows = inv_rows - product(prev_rows, upper_side.T)
            inv_corner = diag_inverse[node_index] - product(upper_cur.T, inv_cols) - product(upper_side, cross_col)
            cross_cols.append(cross_col)
            cross_rows.append(cross_row)
        else:
            inv_corner = diag_inverse[node_index] - product(upper_cur.T, inv_cols)
        cols_list.append(inv_cols)
        rows_list.append(inv_rows)
        corner_list.append(inv_corner)
    x_blocks = jnp.stack(cols_list, axis=1)
    y_blocks = jnp.stack(rows_list, axis=1).reshape(PCOL, PROW, SLAB, SUPER, W)
    z_blocks = jnp.stack(corner_list)
    cross_blocks = jnp.stack([jnp.stack(cross_cols), jnp.stack(cross_rows)])
    return x_blocks, y_blocks, z_blocks, cross_blocks
```

```python
import functools

import jax
import jax.numpy as jnp
from jax import lax
from jax.experimental import pallas as pl
from jax.experimental.pallas import tpu as pltpu
from jax.experimental.layout import Layout, with_layout_constraint
from jax.sharding import PartitionSpec as P


f32 = jnp.float32
bf16 = jnp.bfloat16


def halves(value):
    hi = value.astype(bf16)
    return hi, (value - hi.astype(f32)).astype(bf16)


def dot3(left, right, left_dim, right_dim):
    dims = (((left_dim,), (right_dim,)), ((), ()))

    def one(a, b):
        return lax.dot_general(a, b, dims, preferred_element_type=f32)

    return one(left[0], right[0]) + (one(left[0], right[1]) + one(left[1], right[0]))


def sweep_kernel(
    shape,
    a_ref, l_ref, u_ref, e_ref, f_ref, d_ref, mask_ref,
    xo, yo, zo, co, lbuf, ubuf,
    ah, al, lh, ll, uh, ul, stage, pb, pr, ln, qb, yr, uw_h, uw_l, lw_h, lw_l, win_h, win_l, keep, dbuf,
    late, slate, srs, srr, srs2, srr2,
    a_sem, st_sem, d_sem, l_send, l_recv, u_send, u_recv, up_recv, p_send, p_recv, n_send, n_recv,
    y_send, y_recv, sp_send, sp_recv, sn_send, sn_recv, sr_send, sr_recv, free_up, free_down,
):
    supers, width, blk, prow, nz, rows_here, cols_here, slab = shape
    pcol = 2 * nz
    part_l, part_u = width // prow, width // pcol
    row = lax.axis_index("row")
    col = lax.axis_index("col")
    z, k = col // 2, col % 2
    other = 1 - k
    y, x = row // 2, row % 2
    row_x, row_y, row_d = y * 2 + 1 - x, (1 - y) * 2 + x, (1 - y) * 2 + 1 - x
    to_x, to_y, to_d = {"row": row_x}, {"row": row_y}, {"row": row_d}
    to_pair = {"col": col + 1 - 2 * k}
    up, down = {"col": col + 2}, {"col": col - 2}
    has_up, has_down = z < nz - 1, z > 0

    def when(cond, body):
        pl.when(cond)(body)

    def rc(src, dst, ss, rs, dev):
        return pltpu.make_async_remote_copy(
            src_ref=src, dst_ref=dst, send_sem=ss, recv_sem=rs,
            device_id=dev, device_id_type=pl.DeviceIdType.MESH,
        )

    barrier = pltpu.get_barrier_semaphore()

    def greet(dev):
        pl.semaphore_signal(barrier, inc=1, device_id=dev, device_id_type=pl.DeviceIdType.MESH)

    for dev in (to_x, to_y, to_d, to_pair):
        greet(dev)
    when(has_up, lambda: greet(up))
    when(has_down, lambda: greet(down))
    pl.semaphore_wait(barrier, 4 + has_up.astype(jnp.int32) + has_down.astype(jnp.int32))

    half_l = part_l // 2

    def l_piece(s, r, h=None):
        if h is None:
            return lbuf.at[s, pl.ds(pl.multiple_of(r * part_l, 8), part_l)]
        return lbuf.at[s, pl.ds(pl.multiple_of(r * part_l + h * half_l, 8), half_l)]

    def l_copy(s, i):
        if i == 0:
            return rc(l_ref.at[s], l_piece(s, row), l_send.at[s, 0], l_recv.at[s, 0], to_x)
        if i == 1:
            return rc(l_ref.at[s], l_piece(s, row), l_send.at[s, 1], l_recv.at[s, 1], to_y)
        if i == 2:
            return rc(l_piece(s, row_y, 0), l_piece(s, row_y, 0), l_send.at[s, 2], l_recv.at[s, 2], to_x)
        return rc(l_piece(s, row_x, 1), l_piece(s, row_x, 1), l_send.at[s, 3], l_recv.at[s, 3], to_y)

    def l_start(s):
        l_copy(s, 0).start()
        l_copy(s, 1).start()

    def l_fwd(s):
        rc(l_ref.at[s], l_piece(s, row_x), l_send.at[s, 0], l_recv.at[s, 0], to_x).wait_recv()
        l_copy(s, 3).start()
        rc(l_ref.at[s], l_piece(s, row_y), l_send.at[s, 1], l_recv.at[s, 1], to_y).wait_recv()
        l_copy(s, 2).start()

    def l_done(s):
        rc(l_piece(s, row_d, 0), l_piece(s, row_d, 0), l_send.at[s, 2], l_recv.at[s, 2], to_x).wait_recv()
        rc(l_piece(s, row_d, 1), l_piece(s, row_d, 1), l_send.at[s, 3], l_recv.at[s, 3], to_y).wait_recv()

    def u_piece(s, c):
        return ubuf.at[s, pl.ds(pl.multiple_of(c * part_u, 8), part_u)]

    def u_copy(s, zs, way, own):
        mine = u_piece(s, zs * 2 + k)
        src = u_ref.at[s] if own else mine
        recv = up_recv if way == 2 else u_recv
        return rc(src, mine, u_send.at[s, zs, way], recv.at[s, zs], (up, down, to_pair)[way])

    def u_own(s):
        when(has_up, lambda: u_copy(s, z, 0, True).start())
        when(has_down, lambda: u_copy(s, z, 1, True).start())
        u_copy(s, z, 2, True).start()

    def u_step(s, t):
        @pl.when(z >= t)
        def _():
            u_copy(s, z - t, 1, False).wait_recv()
            when(has_up, lambda: u_copy(s, z - t, 0, False).start())
            u_copy(s, z - t, 2, False).start()

        @pl.when(z + t < nz)
        def _():
            u_copy(s, z + t, 0, False).wait_recv()
            when(has_down, lambda: u_copy(s, z + t, 1, False).start())
            u_copy(s, z + t, 2, False).start()

    def u_done(s):
        for zs in range(nz):
            piece = u_piece(s, zs * 2 + other)
            rc(piece, piece, u_send.at[s, zs, 2], up_recv.at[s, zs], to_pair).wait_recv()

    lanes = stage.shape[2]
    tiles = lanes // blk

    def load(buf, own_ref, s, count, me, part, q):
        here = pl.ds(q * lanes, lanes)

        @pl.loop(0, count)
        def _(p):
            there = stage.at[q % 2, pl.ds(pl.multiple_of(p * part, 8), part)]

            @pl.when(p != me)
            def _():
                pltpu.make_async_copy(
                    buf.at[s, pl.ds(pl.multiple_of(p * part, 8), part), here], there, st_sem.at[q % 2]
                ).start()

            @pl.when(p == me)
            def _():
                pltpu.make_async_copy(own_ref.at[s, :, here], there, st_sem.at[q % 2]).start()

    def convert(buf, own_ref, s, count, me, part, total, first_tile, out_h, out_l):
        load(buf, own_ref, s, count, me, part, 0)
        for q in range(total // lanes):
            if q + 1 < total // lanes:
                load(buf, own_ref, s, count, me, part, q + 1)
            pltpu.make_async_copy(stage.at[q % 2], stage.at[q % 2], st_sem.at[q % 2]).wait()

            @pl.loop(0, tiles)
            def _(t):
                src = pl.ds(pl.multiple_of(t * blk, 128), blk)
                dst = pl.ds(pl.multiple_of(q * lanes + t * blk, 128), blk)
                for j in range(width // blk):
                    keep_it = mask_ref[s, j, first_tile + q * tiles + t].astype(f32)
                    rows = pl.ds(j * blk, blk)
                    hi, lo = halves(stage[q % 2, rows, src] * keep_it)
                    out_h[rows, dst] = hi
                    out_l[rows, dst] = lo

    def window(index):
        start = index * slab
        odd = start % 128
        return pl.ds(pl.multiple_of(start - odd, 128), width), odd

    def l_conv(s):
        convert(lbuf, l_ref, s, prow, row, part_l, cols_here, col * (cols_here // blk), lh, ll)
        if s > 0:
            where, _ = window(row)
            lw_h[s - 1] = lh[:, where]
            lw_l[s - 1] = ll[:, where]

    def u_conv(s):
        convert(ubuf, u_ref, s, pcol, col, part_u, rows_here, row * (rows_here // blk), uh, ul)
        where, _ = window(col)
        uw_h[s] = uh[:, where]
        uw_l[s] = ul[:, where]

    a_lanes = 256
    a_cols = cols_here // a_lanes
    a_slots = 2 * nz

    def a_copy(n, slot):
        i, j = n // a_cols, n % a_cols
        return pltpu.make_async_copy(
            a_ref.at[pl.ds(pl.multiple_of(i * slab, 8), slab), pl.ds(pl.multiple_of(j * a_lanes, 128), a_lanes)],
            pb.at[0, slot // 2, slot % 2, :, pl.ds(0, a_lanes)],
            a_sem.at[slot],
        )

    def a_load():
        count = (rows_here // slab) * a_cols
        for n in range(a_slots - 1):
            a_copy(n, n).start()

        @pl.loop(0, count)
        def _(n):
            slot = n % a_slots

            @pl.when(n + a_slots - 1 < count)
            def _():
                a_copy(n + a_slots - 1, (n + a_slots - 1) % a_slots).start()

            a_copy(n, slot).wait()
            i, j = n // a_cols, n % a_cols
            across = pl.ds(pl.multiple_of(j * a_lanes, 128), a_lanes)
            step = 64
            for b in range(slab // step):
                hi, lo = halves(pb[0, slot // 2, slot % 2, pl.ds(b * step, step), pl.ds(0, a_lanes)])
                down_to = pl.ds(pl.multiple_of(i * slab + b * step, 64), step)
                ah[down_to, across] = hi
                al[down_to, across] = lo

    hz = nz // 2
    h_rows = rows_here // 2

    def far(i):
        flip = (z < hz).astype(jnp.int32)
        return (flip + i) % 2

    def p_copy(s, hh):
        here = pl.ds(pl.multiple_of(hh * hz, hz), hz)
        return rc(pb.at[s % 2, here, other], pr.at[s % 2, here], p_send.at[s, hh], p_recv.at[s, hh], to_pair)

    def p_half(s, i):
        hh = far(i)
        rows = pl.ds(pl.multiple_of(hh * h_rows, 128), h_rows)
        got = dot3((lh[...], ll[...]), (ah[rows], al[rows]), 1, 1).T
        for q in range(2 * hz):
            pb[s % 2, hh * hz + q // 2, q % 2] = got[q * slab : (q + 1) * slab]
        p_copy(s, hh).start()

    def n_copy(s, d, way):
        slot = d + 1 - way
        return rc(pb.at[s % 2, d, k], ln.at[s % 2, slot], n_send.at[s, d], n_recv.at[s, slot], (up, down)[way])

    def line_free(n):
        def tell(sem, dev):
            pl.semaphore_signal(sem.at[n], inc=1, device_id=dev, device_id_type=pl.DeviceIdType.MESH)

        when(has_down, lambda: tell(free_up, down))
        when(has_up, lambda: tell(free_down, up))

    def line_wait(n):
        when(has_up, lambda: pl.semaphore_wait(free_up.at[n], 1))
        when(has_down, lambda: pl.semaphore_wait(free_down.at[n], 1))

    def pair_add(s, i):
        if s == 2 and i == 0:
            line_wait(0)
        hh = far(i)
        p_copy(s, hh).wait_recv()
        for q in range(hz):
            d = hh * hz + q
            pb[s % 2, d, k] = pb[s % 2, d, k] + pr[s % 2, d]
        lo, hi = (1 - i) * hz, (2 - i) * hz

        @pl.when(z == 0)
        def _():
            for d in reversed(range(max(lo, 1), hi)):
                n_copy(s, d, 0).start()

        lo, hi = i * hz, (i + 1) * hz

        @pl.when(z == nz - 1)
        def _():
            for d in range(lo, min(hi, nz - 1)):
                n_copy(s, d, 1).start()

    def line_t(s, t):
        zb = nz - 1 - z

        @pl.when((z >= 1) & (z <= t))
        def _():
            d = z + (nz - 1 - t)
            rc(ln.at[s % 2, d + 1], ln.at[s % 2, d + 1], n_send.at[s, d], n_recv.at[s, d + 1], to_pair).wait_recv()
            pb[s % 2, d, k] = pb[s % 2, d, k] + ln[s % 2, d + 1]
            n_copy(s, d, 0).start()

        @pl.when((zb >= 1) & (zb <= t))
        def _():
            d = z - (nz - 1 - t)
            rc(ln.at[s % 2, d], ln.at[s % 2, d], n_send.at[s, d], n_recv.at[s, d], to_pair).wait_recv()
            pb[s % 2, d, k] = pb[s % 2, d, k] + ln[s % 2, d]
            n_copy(s, d, 1).start()

    def line_end(s):
        @pl.when(has_down)
        def _():
            rc(ln.at[s % 2, z + 1], ln.at[s % 2, z + 1], n_send.at[s, z], n_recv.at[s, z + 1], to_pair).wait_recv()
            pb[s % 2, z, k] = pb[s % 2, z, k] + ln[s % 2, z + 1]

        @pl.when(has_up)
        def _():
            rc(ln.at[s % 2, z], ln.at[s % 2, z], n_send.at[s, z], n_recv.at[s, z], to_pair).wait_recv()
            pb[s % 2, z, k] = pb[s % 2, z, k] + ln[s % 2, z]

        if s < 2:
            line_free(s)
        total = -pb[s % 2, z, k]
        if s > 0:
            total = total - dot3(halves(xo[s - 1]), halves(e_ref[s - 1]), 1, 0)
        xo[s] = total

    def p_sent(s):
        for hh in range(2):
            p_copy(s, hh).wait_send()
        for d in range(nz):
            when(z < d, lambda d=d: n_copy(s, d, 0).wait_send())
            when(z > d, lambda d=d: n_copy(s, d, 1).wait_send())

    half_y = slab // 2
    q_cols = 256

    def q_rows(r, h):
        return pl.ds(pl.multiple_of(r * slab + h * half_y, 8), half_y)

    def q_slab(s, r, h):
        return qb.at[s % 2, q_rows(r, h)]

    def y_copy(s, i):
        src, dev = (
            (q_slab(s, row_x, 0), to_x),
            (q_slab(s, row_d, 0), to_x),
            (q_slab(s, row_y, 1), to_y),
            (q_slab(s, row_d, 1), to_y),
            (q_slab(s, row_y, 0), to_y),
            (q_slab(s, row_x, 1), to_x),
        )[i]
        return rc(src, yr.at[s, i], y_send.at[s, i], y_recv.at[s, i], dev)

    def q_comp(s):
        @pl.loop(0, cols_here // q_cols)
        def _(i):
            across = pl.ds(pl.multiple_of(i * q_cols, 128), q_cols)
            got = dot3((uh[...], ul[...]), (ah[:, across], al[:, across]), 1, 0)
            qb[s % 2, across] = got.T

        for i in (1, 3, 0, 2):
            y_copy(s, i).start()

    def y_relay(s):
        y_copy(s, 1).wait_recv()
        qb[s % 2, q_rows(row_y, 0)] = qb[s % 2, q_rows(row_y, 0)] + yr[s, 1]
        y_copy(s, 4).start()
        y_copy(s, 3).wait_recv()
        qb[s % 2, q_rows(row_x, 1)] = qb[s % 2, q_rows(row_x, 1)] + yr[s, 3]
        y_copy(s, 5).start()

    def y_end(s):
        for i in (0, 2, 4, 5):
            y_copy(s, i).wait_recv()
        for h, (i, j) in enumerate(((0, 4), (2, 5))):
            yo[s, pl.ds(h * half_y, half_y)] = -(qb[s % 2, q_rows(row, h)] + yr[s, i] + yr[s, j])
        if s > 0:
            yo[s] = yo[s] - dot3(halves(yo[s - 1]), halves(f_ref[s - 1]), 1, 1)

    def y_sent(s):
        for i in range(6):
            y_copy(s, i).wait_send()

    first = ((row == 0) & (col == 0)).astype(f32)

    def fill(value, index):
        _, odd = window(index)
        hi, lo = halves(value)
        win_h[...] = jnp.zeros(win_h.shape, bf16)
        win_l[...] = jnp.zeros(win_l.shape, bf16)
        rows = pl.ds(pl.multiple_of(odd, 64), slab)
        win_h[rows] = hi
        win_l[rows] = lo

    def with_upper(s):
        return dot3((uw_h[s], uw_l[s]), (win_h[...], win_l[...]), 1, 0)

    def d_copy(s):
        return pltpu.make_async_copy(d_ref.at[s], dbuf, d_sem)

    def put(value, i):
        turned = value.T
        for d in range(pcol):
            pb[1, d // 2, d % 2, pl.ds(i * part_u, part_u)] = turned[d * part_u : (d + 1) * part_u]

    n_early = 3 * (supers - 1)
    e_rows = n_early * part_u
    e_here = pl.ds(0, e_rows)

    def order(kind, s):
        return kind * (supers - 1) + s

    def corner_first():
        d_copy(0).start()
        fill(xo[0], col)
        got = with_upper(0)
        d_copy(0).wait()
        keep[0] = dbuf[...] * first - got

    def step_sums(s):
        edge_f = halves(f_ref[s - 1])
        corner = keep[0]
        put(corner, order(0, s - 1))
        corner = halves(corner)
        fill(xo[s - 1], col)
        put(-(with_upper(s) + dot3(edge_f, corner, 1, 0)), order(2, s - 1))
        fill(yo[s - 1], row)
        turned = dot3((lw_h[s - 1], lw_l[s - 1]), (win_h[...], win_l[...]), 1, 0)
        keep[1] = -(turned.T + dot3(corner, halves(e_ref[s - 1]), 1, 0))
        put(keep[1], order(1, s - 1))

    def step_corner(s):
        d_copy(s).start()
        fill(xo[s], col)
        got = with_upper(s) + dot3(halves(f_ref[s - 1]), halves(keep[1]), 1, 0)
        d_copy(s).wait()
        keep[0] = dbuf[...] * first - got

    late_in, sln2 = slate.at[pl.ds(0, nz)], slate.at[pl.ds(nz, nz + 1)]

    def parts(g):
        if g == 0:
            return pb.at[1, :, :, e_here], pr.at[1, :, e_here], ln.at[1, :, e_here], srs, srr
        return late, late_in, sln2, srs2, srr2

    def sp_copy(g):
        here, got = parts(g)[:2]
        return rc(here.at[:, other], got, sp_send.at[g], sp_recv.at[g], to_pair)

    def sn_copy(g, d, way):
        slot = d + 1 - way
        here, _, line = parts(g)[:3]
        return rc(here.at[d, k], line.at[slot], sn_send.at[g, d], sn_recv.at[g, slot], (up, down)[way])

    def s_pair(g):
        sp_copy(g).start()

    def s_add(g):
        if g == 0:
            line_wait(1)
        here, got = parts(g)[:2]
        sp_copy(g).wait_recv()
        for d in range(nz):
            here[d, k] = here[d, k] + got[d]

        @pl.when(z == 0)
        def _():
            for d in reversed(range(1, nz)):
                sn_copy(g, d, 0).start()

        @pl.when(z == nz - 1)
        def _():
            for d in range(nz - 1):
                sn_copy(g, d, 1).start()

    def s_take(g, d, slot):
        here, _, line = parts(g)[:3]
        rc(line.at[slot], line.at[slot], sn_send.at[g, d], sn_recv.at[g, slot], to_pair).wait_recv()
        here[d, k] = here[d, k] + line[slot]

    def s_line(g, t):
        zb = nz - 1 - z

        @pl.when((z >= 1) & (z <= t))
        def _():
            d = z + (nz - 1 - t)
            s_take(g, d, d + 1)
            sn_copy(g, d, 0).start()

        @pl.when((zb >= 1) & (zb <= t))
        def _():
            d = z - (nz - 1 - t)
            s_take(g, d, d)
            sn_copy(g, d, 1).start()

    def sr_copy(g, r, me, dev):
        out, into = parts(g)[3:]
        return rc(out.at[r], into.at[me], sr_send.at[g, r], sr_recv.at[g, me], dev)

    rows_to = ((row_x, to_x), (row_y, to_y), (row_d, to_d))

    def s_row(g):
        here, out = parts(g)[0], parts(g)[3]
        when(has_down, lambda: s_take(g, z, z + 1))
        when(has_up, lambda: s_take(g, z, z))
        total = here[z, k]
        for r in range(prow):
            turned = total if r == 0 else pltpu.roll(total, width - r * part_l, 1)
            out[r] = turned[:, :128]
        for r, dev in rows_to:
            sr_copy(g, r, row, dev).start()

    def s_end(g):
        out, into = parts(g)[3:]
        for r, dev in rows_to:
            sr_copy(g, r, r, dev).wait_recv()
        total = out[row]
        for r, _ in rows_to:
            total = total + into[r]
        total = total[:, :part_l]
        if g == 0:
            for s in range(supers - 1):
                for kind in range(3):
                    at = order(kind, s) * part_u
                    value = total[at : at + part_u]
                    if kind == 0:
                        zo[s] = value
                    else:
                        co[kind - 1, s] = value
        else:
            zo[supers - 1] = total

    def s_sent(g):
        sp_copy(g).wait_send()
        for d in range(nz):
            when(z < d, lambda d=d: sn_copy(g, d, 0).wait_send())
            when(z > d, lambda d=d: sn_copy(g, d, 1).wait_send())
        for r, dev in rows_to:
            sr_copy(g, r, row, dev).wait_send()

    def late_put():
        turned = keep[0].T
        for d in range(pcol):
            late[d // 2, d % 2] = turned[d * part_u : (d + 1) * part_u]

    l_start(0)
    u_own(0)
    a_load()
    u_own(1)
    l_fwd(0)
    l_start(1)
    u_step(0, 1)
    l_done(0)
    l_conv(0)
    p_half(0, 0)
    u_own(2)
    p_half(0, 1)
    pair_add(0, 0)
    l_fwd(1)
    l_start(2)
    pair_add(0, 1)
    u_step(0, 2)
    u_step(1, 1)
    l_done(1)
    l_conv(1)
    p_half(1, 0)
    u_step(0, 3)
    line_t(0, 1)
    p_half(1, 1)
    pair_add(1, 0)
    pair_add(1, 1)
    l_fwd(2)
    u_step(1, 2)
    u_step(2, 1)
    u_done(0)
    u_conv(0)
    line_t(0, 2)
    q_comp(0)
    l_done(2)
    l_conv(2)
    u_step(1, 3)
    line_end(0)
    line_t(1, 1)
    y_relay(0)
    corner_first()
    u_done(1)
    u_conv(1)
    p_sent(0)
    p_half(2, 0)
    u_step(2, 2)
    p_half(2, 1)
    line_t(1, 2)
    pair_add(2, 0)
    pair_add(2, 1)
    q_comp(1)
    y_end(0)
    u_step(2, 3)
    line_end(1)
    p_sent(1)
    y_relay(1)
    step_sums(1)
    line_t(2, 1)
    step_corner(1)
    u_done(2)
    u_conv(2)
    y_sent(0)
    line_t(2, 2)
    q_comp(2)
    y_end(1)
    step_sums(2)
    s_pair(0)
    y_relay(2)
    s_add(0)
    s_line(0, 1)
    s_line(0, 2)
    line_end(2)
    step_corner(2)
    late_put()
    s_pair(1)
    s_row(0)
    s_add(1)
    s_line(1, 1)
    y_end(2)
    s_line(1, 2)
    s_end(0)
    s_row(1)
    s_end(1)

    for s in range(supers):
        for i in range(4):
            l_copy(s, i).wait_send()
        for zs in range(nz):
            for own in (True, False):
                mine = (z == zs) if own else (z != zs)

                @pl.when(mine)
                def _(s=s, zs=zs, own=own):
                    u_copy(s, zs, 2, own).wait_send()

            when((z >= zs) & has_up, lambda s=s, zs=zs: u_copy(s, zs, 0, False).wait_send())
            when((z <= zs) & has_down, lambda s=s, zs=zs: u_copy(s, zs, 1, False).wait_send())
    p_sent(2)
    y_sent(1)
    y_sent(2)
    s_sent(0)
    s_sent(1)


def fits(shape):
    supers, width, blk, prow, pcol, rows_here, cols_here, slab = shape
    return (
        supers == 3 and prow == 4 and pcol % 4 == 0 and blk == 128 and width % blk == 0
        and slab % 64 == 0 and width == slab + 64 and slab % 128 == 64
        and rows_here % 640 == 0 and cols_here % 640 == 0
        and width % (8 * pcol) == 0 and width // prow <= 128
        and 2 * (supers - 1) * 3 * width // (2 * pcol) <= slab
    )


def sweep(shape, anc_inverse, lower, upper, lower_edge, upper_edge, diag_inverse, mask):
    supers, width, blk, prow, pcol, rows_here, cols_here, slab = shape
    nz = pcol // 2
    part_u = width // pcol
    n_early = 3 * (supers - 1)
    vmem, dma = pltpu.VMEM, pltpu.SemaphoreType.DMA
    in_vmem = pl.BlockSpec(memory_space=pltpu.VMEM)
    in_hbm = pl.BlockSpec(memory_space=pl.ANY)
    out = [
        ((supers, slab, width), in_vmem),
        ((supers, slab, width), in_vmem),
        ((supers, part_u, width // prow), in_vmem),
        ((2, supers - 1, part_u, width // prow), in_vmem),
        ((supers, width, cols_here), in_hbm),
        ((supers, width, rows_here), in_hbm),
    ]
    return pl.pallas_call(
        functools.partial(sweep_kernel, (supers, width, blk, prow, nz, rows_here, cols_here, slab)),
        name="sweep",
        out_shape=[jax.ShapeDtypeStruct(dims, f32) for dims, _ in out],
        in_specs=[in_hbm, in_hbm, in_hbm, in_vmem, in_vmem, in_hbm, pl.BlockSpec(memory_space=pltpu.SMEM)],
        out_specs=[spec for _, spec in out],
        scratch_shapes=[
            vmem((rows_here, cols_here), bf16),
            vmem((rows_here, cols_here), bf16),
            vmem((width, cols_here), bf16),
            vmem((width, cols_here), bf16),
            vmem((width, rows_here), bf16),
            vmem((width, rows_here), bf16),
            vmem((2, width, cols_here // 2), f32),
            vmem((2, nz, 2, slab, width), f32),
            vmem((2, nz, slab, width), f32),
            vmem((2, nz + 1, slab, width), f32),
            vmem((2, cols_here, width), f32),
            vmem((supers, 6, slab // 2, width), f32),
            vmem((supers, width, width), bf16),
            vmem((supers, width, width), bf16),
            vmem((supers - 1, width, width), bf16),
            vmem((supers - 1, width, width), bf16),
            vmem((width, width), bf16),
            vmem((width, width), bf16),
            vmem((2, width, width), f32),
            vmem((width, width), f32),
            vmem((nz, 2, part_u, width), f32),
            vmem((2 * nz + 1, part_u, width), f32),
            vmem((prow, n_early * part_u, 128), f32),
            vmem((prow, n_early * part_u, 128), f32),
            vmem((prow, part_u, 128), f32),
            vmem((prow, part_u, 128), f32),
            dma((2 * nz,)),
            dma((2,)),
            dma,
            dma((supers, 4)),
            dma((supers, 4)),
            dma((supers, nz, 3)),
            dma((supers, nz)),
            dma((supers, nz)),
            dma((supers, 2)),
            dma((supers, 2)),
            dma((supers, nz)),
            dma((supers, nz + 1)),
            dma((supers, 6)),
            dma((supers, 6)),
            dma((2,)),
            dma((2,)),
            dma((2, nz)),
            dma((2, nz + 1)),
            dma((2, prow)),
            dma((2, prow)),
            pltpu.SemaphoreType.REGULAR((2,)),
            pltpu.SemaphoreType.REGULAR((2,)),
        ],
        compiler_params=pltpu.CompilerParams(
            collective_id=0, has_side_effects=True, vmem_limit_bytes=67043328
        ),
    )(anc_inverse, lower, upper, lower_edge, upper_edge, diag_inverse, mask)


def per_device(anc_inverse, lower_anc, upper_anc, lower_edge, upper_edge, diag_inverse, tile_mask):
    rows_here, cols_here = anc_inverse.shape
    prow, pcol = lax.axis_size("row"), lax.axis_size("col")
    supers, width = diag_inverse.shape[0], diag_inverse.shape[1]
    blk = width // tile_mask.shape[2]
    shape = (supers, width, blk, prow, pcol, rows_here, cols_here, cols_here // prow)
    args = (anc_inverse, lower_anc, upper_anc, lower_edge, upper_edge, diag_inverse, tile_mask)
    if not fits(shape):
        return general(*args)
    x, y, corner, cross, _, _ = sweep(
        shape,
        anc_inverse,
        jnp.transpose(lower_anc, (1, 2, 0)),
        jnp.transpose(upper_anc, (1, 2, 0)),
        lower_edge,
        upper_edge,
        diag_inverse,
        jnp.transpose(tile_mask, (0, 2, 1)),
    )
    return (
        jnp.transpose(x, (1, 0, 2)),
        jnp.transpose(y, (1, 0, 2))[None, None],
        jnp.transpose(corner, (0, 2, 1)),
        jnp.transpose(cross, (0, 1, 3, 2)),
    )


precise = lax.Precision.HIGH


def contract(left, right, left_dim, right_dim):
    return lax.dot_general(
        left,
        right,
        (((left_dim,), (right_dim,)), ((), ())),
        precision=precise,
        preferred_element_type=jnp.float32,
    )


def row_major(array):
    return with_layout_constraint(array, Layout(major_to_minor=(0, 1)))


def partner(index, step, count):
    if count & (count - 1) == 0:
        return index ^ step
    return (step - index) % count


def exchange(piece_for, axis):
    count = lax.axis_size(axis)
    index = lax.axis_index(axis)
    got = []
    for step in range(count):
        peer = partner(index, step, count)
        piece = piece_for(peer)
        pairs = [(i, partner(i, step, count)) for i in range(count)]
        if any(i != j for i, j in pairs):
            piece = lax.ppermute(piece, axis, pairs)
        got.append((peer, piece))
    return got


def mask_factor(factor, tile_mask, first_row, first_col, blk):
    rows, supers, cols = factor.shape
    blocks = rows // blk
    window = lax.dynamic_slice_in_dim(tile_mask, first_row // blk, blocks, 1).astype(jnp.float32)
    tile_cols = window.shape[2]
    tile_of_col = (first_col + jnp.arange(cols)) // blk
    pick = (tile_of_col[None, :] == jnp.arange(tile_cols)[:, None]).astype(jnp.float32)
    chosen = sum(window[:, :, t, None] * pick[t] for t in range(tile_cols))
    chosen = jnp.transpose(chosen, (1, 0, 2))
    masked = factor.reshape(blocks, blk, supers, cols) * chosen[:, None]
    return jnp.transpose(masked.reshape(rows, supers, cols), (1, 2, 0))


def general(anc_inverse, lower_anc, upper_anc, lower_edge, upper_edge, diag_inverse, tile_mask):
    rows_here, cols_here = anc_inverse.shape
    prow = lax.axis_size("row")
    pcol = lax.axis_size("col")
    supers, width = diag_inverse.shape[0], diag_inverse.shape[1]
    blk = width // tile_mask.shape[2]
    row = lax.axis_index("row")
    col = lax.axis_index("col")
    part_lower = width // prow
    part_upper = width // pcol

    upper_t = mask_factor(upper_anc, tile_mask, row * rows_here, col * part_upper, blk)
    lower_t = mask_factor(lower_anc, tile_mask, col * cols_here, row * part_lower, blk)

    upper_t = lax.all_gather(upper_t, "col", axis=0)
    lower_full = jnp.zeros((supers, prow, part_lower, cols_here), jnp.float32)
    for peer, piece in exchange(lambda _: lower_t, "row"):
        lower_full = lax.dynamic_update_slice(lower_full, piece[:, None], (0, peer, 0, 0))
    lower_full = lower_full.reshape(supers, width, cols_here)
    lower_comb = [-lower_full[0]]
    for s in range(1, supers):
        lower_comb.append(-lower_full[s] - contract(lower_edge[s - 1], lower_comb[-1], 0, 0))
    cols_part = [row_major(contract(anc_inverse, one, 1, 1)) for one in lower_comb]
    cols_mine = [lax.psum_scatter(one, "col", scatter_dimension=0, tiled=True) for one in cols_part]

    upper_full = [upper_t[:, s].reshape(width, rows_here) for s in range(supers)]
    upper_comb = [-upper_full[0]]
    for s in range(1, supers):
        upper_comb.append(-upper_full[s] - contract(upper_edge[s - 1], upper_comb[-1], 1, 0))
    rows_part = [row_major(contract(anc_inverse, one, 0, 1)) for one in upper_comb]

    first = jnp.logical_and(row == 0, col == 0)
    corner = []
    cross_cols = []
    cross_rows = []
    for s in range(supers):
        upper_here = contract(upper_full[s], cols_part[s], 1, 0)
        now = jnp.where(first, diag_inverse[s], 0.0) - upper_here
        if s > 0:
            upper_prev = contract(upper_full[s], cols_part[s - 1], 1, 0)
            lower_prev = lax.dot_general(
                rows_part[s - 1],
                lower_full[s],
                (((0,), (1,)), ((), ())),
                precision=precise,
                preferred_element_type=jnp.float32,
            )
            cross_col = -(lower_prev + contract(corner[-1], lower_edge[s - 1], 1, 0))
            cross_row = -(upper_prev + contract(upper_edge[s - 1], corner[-1], 1, 0))
            now = now - contract(upper_edge[s - 1], cross_col, 1, 0)
            cross_cols.append(cross_col)
            cross_rows.append(cross_row)
        corner.append(now)
    sums = jnp.stack(corner + cross_cols + cross_rows)
    count = sums.shape[0]

    row_slab = cols_here // prow
    rows_mine = [
        sum(
            piece
            for _, piece in exchange(
                lambda peer: lax.dynamic_slice_in_dim(one, peer * row_slab, row_slab, 0), "row"
            )
        )
        for one in rows_part
    ]
    sums, rows_mine = lax.optimization_barrier((sums, rows_mine))
    sums = sum(
        piece
        for _, piece in exchange(
            lambda peer: lax.dynamic_slice_in_dim(sums, peer * part_lower, part_lower, 1), "row"
        )
    )
    sums = jnp.transpose(sums.reshape(count * part_lower, width))
    sums, cols_mine = lax.optimization_barrier((sums, cols_mine))
    sums = lax.psum_scatter(sums, "col", scatter_dimension=0, tiled=True)
    sums = jnp.transpose(sums).reshape(count, part_lower, part_upper)

    x_blocks = jnp.stack(cols_mine, axis=1)
    y_blocks = jnp.stack(rows_mine, axis=1)[None, None]
    z_blocks = sums[:supers]
    cross_blocks = sums[supers:].reshape(2, supers - 1, part_lower, part_upper)
    return (x_blocks, y_blocks, z_blocks, cross_blocks)


def solution(mesh):
    return jax.shard_map(
        per_device,
        mesh=mesh,
        in_specs=(
            P("row", "col"),
            P("col", None, "row"),
            P("row", None, "col"),
            P(),
            P(),
            P(),
            P(),
        ),
        out_specs=(
            P(("row", "col"), None, None),
            P("col", "row", None, None, None),
            P(None, "row", "col"),
            P(None, None, "row", "col"),
        ),
        check_vma=False,
    )
```

```python
import functools

import jax
import jax.numpy as jnp
from jax import lax
from jax.experimental import pallas as pl
from jax.experimental.pallas import tpu as pltpu
from jax.experimental.layout import Layout, with_layout_constraint
from jax.sharding import PartitionSpec as P


f32 = jnp.float32
bf16 = jnp.bfloat16


def halves(value):
    hi = value.astype(bf16)
    return hi, (value - hi.astype(f32)).astype(bf16)


def dot3(left, right, left_dim, right_dim):
    dims = (((left_dim,), (right_dim,)), ((), ()))

    def one(a, b):
        return lax.dot_general(a, b, dims, preferred_element_type=f32)

    return one(left[0], right[0]) + (one(left[0], right[1]) + one(left[1], right[0]))


def sweep_kernel(
    shape,
    a_ref, l_ref, u_ref, e_ref, f_ref, d_ref, mask_ref,
    xo, yo, zo, co, lbuf, ubuf,
    ah, al, lh, ll, uh, ul, stage, pb, pr, ln, qb, yr, uw_h, uw_l, lw_h, lw_l, win_h, win_l, keep,
    sp2, sq, tb, zb, zl, zf,
    a_sem, st_sem, d_sem, l_send, l_recv, u_send, u_recv, up_recv, p_send, p_recv, n_send, n_recv,
    y_send, y_recv, sp_send, sp_recv, sq_send, sq_recv, sn_send, sn_recv, sf_send, sf_recv,
    free_up, free_down, free_pair,
):
    supers, width, blk, prow, nz, rows_here, cols_here, slab = shape
    pcol = 2 * nz
    part_l, part_u = width // prow, width // pcol
    row = lax.axis_index("row")
    col = lax.axis_index("col")
    z, k = col // 2, col % 2
    other = 1 - k
    y, x = row // 2, row % 2
    row_x, row_y, row_d = y * 2 + 1 - x, (1 - y) * 2 + x, (1 - y) * 2 + 1 - x
    to_x, to_y, to_d = {"row": row_x}, {"row": row_y}, {"row": row_d}
    to_pair = {"col": col + 1 - 2 * k}
    up, down = {"col": col + 2}, {"col": col - 2}
    has_up, has_down = z < nz - 1, z > 0
    at_end, inside = (z == 0) | (z == nz - 1), (z > 0) & (z < nz - 1)

    def when(cond, body):
        pl.when(cond)(body)

    def rc(src, dst, ss, rs, dev):
        return pltpu.make_async_remote_copy(
            src_ref=src, dst_ref=dst, send_sem=ss, recv_sem=rs,
            device_id=dev, device_id_type=pl.DeviceIdType.MESH,
        )

    barrier = pltpu.get_barrier_semaphore()

    def greet(dev):
        pl.semaphore_signal(barrier, inc=1, device_id=dev, device_id_type=pl.DeviceIdType.MESH)

    for dev in (to_x, to_y, to_d, to_pair):
        greet(dev)
    when(has_up, lambda: greet(up))
    when(has_down, lambda: greet(down))
    pl.semaphore_wait(barrier, 4 + has_up.astype(jnp.int32) + has_down.astype(jnp.int32))

    half_l = part_l // 2

    def l_piece(s, r, h):
        return lbuf.at[s, pl.ds(pl.multiple_of(r * part_l + h * half_l, 8), half_l)]

    def l_own(s, h):
        return l_ref.at[s, pl.ds(h * half_l, half_l)]

    def l_copy(s, i):
        src, dst, dev = (
            (l_own(s, 1), l_piece(s, row, 1), to_x),
            (l_own(s, 0), l_piece(s, row, 0), to_y),
            (l_own(s, 0), l_piece(s, row, 0), to_x),
            (l_own(s, 1), l_piece(s, row, 1), to_y),
            (l_piece(s, row_x, 1), l_piece(s, row_x, 1), to_y),
            (l_piece(s, row_y, 0), l_piece(s, row_y, 0), to_x),
        )[i]
        return rc(src, dst, l_send.at[s, i], l_recv.at[s, i], dev)

    def l_take(s, i):
        r, h = ((row_x, 1), (row_y, 0), (row_x, 0), (row_y, 1), (row_d, 1), (row_d, 0))[i]
        rc(l_piece(s, r, h), l_piece(s, r, h), l_send.at[s, i], l_recv.at[s, i], to_pair).wait_recv()

    def l_start(s):
        for i in range(4):
            l_copy(s, i).start()

    def l_fwd(s):
        l_take(s, 0)
        l_copy(s, 4).start()
        l_take(s, 1)
        l_copy(s, 5).start()

    def l_done(s):
        for i in range(2, 6):
            l_take(s, i)

    def u_piece(s, c):
        return ubuf.at[s, pl.ds(pl.multiple_of(c * part_u, 8), part_u)]

    def u_copy(s, zs, way, own):
        mine = u_piece(s, zs * 2 + k)
        src = u_ref.at[s] if own else mine
        recv = up_recv if way == 2 else u_recv
        return rc(src, mine, u_send.at[s, zs, way], recv.at[s, zs], (up, down, to_pair)[way])

    def u_own(s):
        when(has_up, lambda: u_copy(s, z, 0, True).start())
        when(has_down, lambda: u_copy(s, z, 1, True).start())
        u_copy(s, z, 2, True).start()

    def u_step(s, t):
        @pl.when(z >= t)
        def _():
            u_copy(s, z - t, 1, False).wait_recv()
            when(has_up, lambda: u_copy(s, z - t, 0, False).start())
            u_copy(s, z - t, 2, False).start()

        @pl.when(z + t < nz)
        def _():
            u_copy(s, z + t, 0, False).wait_recv()
            when(has_down, lambda: u_copy(s, z + t, 1, False).start())
            u_copy(s, z + t, 2, False).start()

    def u_done(s):
        for zs in range(nz):
            piece = u_piece(s, zs * 2 + other)
            rc(piece, piece, u_send.at[s, zs, 2], up_recv.at[s, zs], to_pair).wait_recv()

    lanes = stage.shape[2]
    tiles = lanes // blk

    def load(buf, own_ref, s, count, me, part, q):
        here = pl.ds(q * lanes, lanes)

        @pl.loop(0, count)
        def _(p):
            there = stage.at[q % 2, pl.ds(pl.multiple_of(p * part, 8), part)]

            @pl.when(p != me)
            def _():
                pltpu.make_async_copy(
                    buf.at[s, pl.ds(pl.multiple_of(p * part, 8), part), here], there, st_sem.at[q % 2]
                ).start()

            @pl.when(p == me)
            def _():
                pltpu.make_async_copy(own_ref.at[s, :, here], there, st_sem.at[q % 2]).start()

    def convert(buf, own_ref, s, count, me, part, total, first_tile, out_h, out_l):
        load(buf, own_ref, s, count, me, part, 0)
        for q in range(total // lanes):
            if q + 1 < total // lanes:
                load(buf, own_ref, s, count, me, part, q + 1)
            pltpu.make_async_copy(stage.at[q % 2], stage.at[q % 2], st_sem.at[q % 2]).wait()

            @pl.loop(0, tiles)
            def _(t):
                src = pl.ds(pl.multiple_of(t * blk, 128), blk)
                dst = pl.ds(pl.multiple_of(q * lanes + t * blk, 128), blk)
                for j in range(width // blk):
                    keep_it = mask_ref[s, j, first_tile + q * tiles + t].astype(f32)
                    rows = pl.ds(j * blk, blk)
                    hi, lo = halves(stage[q % 2, rows, src] * keep_it)
                    out_h[rows, dst] = hi
                    out_l[rows, dst] = lo

    def window(index):
        start = index * slab
        odd = start % 128
        return pl.ds(pl.multiple_of(start - odd, 128), width), odd

    def l_conv(s):
        convert(lbuf, l_ref, s, prow, row, part_l, cols_here, col * (cols_here // blk), lh, ll)
        if s > 0:
            where, _ = window(row)
            lw_h[s - 1] = lh[:, where]
            lw_l[s - 1] = ll[:, where]

    def u_conv(s):
        convert(ubuf, u_ref, s, pcol, col, part_u, rows_here, row * (rows_here // blk), uh, ul)
        where, _ = window(col)
        uw_h[s] = uh[:, where]
        uw_l[s] = ul[:, where]

    a_lanes = 256
    a_cols = cols_here // a_lanes
    a_slots = 2 * nz

    def a_copy(n, slot):
        i, j = n // a_cols, n % a_cols
        return pltpu.make_async_copy(
            a_ref.at[pl.ds(pl.multiple_of(i * slab, 8), slab), pl.ds(pl.multiple_of(j * a_lanes, 128), a_lanes)],
            pb.at[pl.ds(pl.multiple_of(slot * slab, 64), slab), pl.ds(0, a_lanes)],
            a_sem.at[slot],
        )

    def a_load():
        count = (rows_here // slab) * a_cols
        for n in range(a_slots - 1):
            a_copy(n, n).start()

        @pl.loop(0, count)
        def _(n):
            slot = n % a_slots

            @pl.when(n + a_slots - 1 < count)
            def _():
                a_copy(n + a_slots - 1, (n + a_slots - 1) % a_slots).start()

            a_copy(n, slot).wait()
            i, j = n // a_cols, n % a_cols
            across = pl.ds(pl.multiple_of(j * a_lanes, 128), a_lanes)
            step = 64
            for b in range(slab // step):
                hi, lo = halves(pb[pl.ds(pl.multiple_of(slot * slab + b * step, 64), step), pl.ds(0, a_lanes)])
                down_to = pl.ds(pl.multiple_of(i * slab + b * step, 64), step)
                ah[down_to, across] = hi
                al[down_to, across] = lo

    hz = nz // 2
    h_rows = rows_here // 2

    def far(i):
        flip = (z < hz).astype(jnp.int32)
        return (flip + i) % 2

    def p_rows(s, d, n=1):
        return pl.ds(pl.multiple_of((s * nz + d) * slab, 64), n * slab)

    def p_copy(s, hh):
        return rc(
            pb.at[p_rows(supers, hh * hz, hz)], pr.at[p_rows(0, hh * hz, hz)],
            p_send.at[s, hh], p_recv.at[s, hh], to_pair,
        )

    def p_both(s, middle):
        @pl.loop(0, 2)
        def _(i):
            when(i == 1, middle)
            hh = far(i)
            if s > 0:
                p_copy(s - 1, hh).wait_send()
            rows = pl.ds(pl.multiple_of(hh * h_rows, 128), h_rows)
            got = dot3((lh[...], ll[...]), (ah[rows], al[rows]), 1, 1).T
            for q in range(2 * hz):
                spot = jnp.where(k == q % 2, s, supers)
                pb[p_rows(spot, hh * hz + q // 2)] = got[q * slab : (q + 1) * slab]
            if s > 0:
                when(i == 0, lambda: pl.semaphore_wait(free_pair.at[s - 1], 1))
            p_copy(s, hh).start()

    def n_copy(s, d, way):
        slot = d + 1 - way
        return rc(pb.at[p_rows(s, d)], ln.at[s % 2, slot], n_send.at[s, d], n_recv.at[s, slot], (up, down)[way])

    def n_take(s, d, slot):
        rc(ln.at[s % 2, slot], ln.at[s % 2, slot], n_send.at[s, d], n_recv.at[s, slot], to_pair).wait_recv()
        pb[p_rows(s, d)] = pb[p_rows(s, d)] + ln[s % 2, slot]

    def tell(sem, dev):
        pl.semaphore_signal(sem, inc=1, device_id=dev, device_id_type=pl.DeviceIdType.MESH)

    def line_wait():
        when(has_up, lambda: pl.semaphore_wait(free_up, 1))
        when(has_down, lambda: pl.semaphore_wait(free_down, 1))

    def pair_add(s, i):
        if s == 2 and i == 0:
            when(at_end, line_wait)
        hh = far(i)
        p_copy(s, hh).wait_recv()
        for q in range(hz):
            d = hh * hz + q
            pb[p_rows(s, d)] = pb[p_rows(s, d)] + pr[p_rows(0, d)]
        if i == 1:
            tell(free_pair.at[s], to_pair)
        lo, hi = (1 - i) * hz, (2 - i) * hz

        @pl.when(z == 0)
        def _():
            for d in reversed(range(max(lo, 1), hi)):
                n_copy(s, d, 0).start()

        lo, hi = i * hz, (i + 1) * hz

        @pl.when(z == nz - 1)
        def _():
            for d in range(lo, min(hi, nz - 1)):
                n_copy(s, d, 1).start()

    def line_t(s, t):
        zb_ = nz - 1 - z
        if s == 2 and t == 1:
            when(inside, line_wait)

        @pl.when((z >= 1) & (z <= t))
        def _():
            d = z + (nz - 1 - t)
            n_take(s, d, d + 1)
            n_copy(s, d, 0).start()

        @pl.when((zb_ >= 1) & (zb_ <= t))
        def _():
            d = z - (nz - 1 - t)
            n_take(s, d, d)
            n_copy(s, d, 1).start()

    def line_take(s):
        when(has_down, lambda: n_take(s, z, z + 1))
        when(has_up, lambda: n_take(s, z, z))
        if s == 0:
            when(has_down, lambda: tell(free_up, down))
            when(has_up, lambda: tell(free_down, up))

    def x_out(s):
        total = -pb[p_rows(s, z)]
        if s > 0:
            total = total - dot3(halves(xo[s - 1]), halves(e_ref[s - 1]), 1, 0)
        xo[s] = total

    def n_sent(s):
        for d in range(nz):
            when(z < d, lambda d=d: n_copy(s, d, 0).wait_send())
            when(z > d, lambda d=d: n_copy(s, d, 1).wait_send())

    half_y = slab // 2
    q_cols = 256

    def q_rows(r, h):
        return pl.ds(pl.multiple_of(r * slab + h * half_y, 8), half_y)

    def q_slab(s, r, h):
        return qb.at[s % 2, q_rows(r, h)]

    def y_copy(s, i):
        src, dev = (
            (q_slab(s, row_x, 0), to_x),
            (q_slab(s, row_d, 0), to_x),
            (q_slab(s, row_y, 1), to_y),
            (q_slab(s, row_d, 1), to_y),
            (q_slab(s, row_y, 0), to_y),
            (q_slab(s, row_x, 1), to_x),
        )[i]
        return rc(src, yr.at[s, i], y_send.at[s, i], y_recv.at[s, i], dev)

    def q_comp(s):
        @pl.loop(0, cols_here // q_cols)
        def _(i):
            across = pl.ds(pl.multiple_of(i * q_cols, 128), q_cols)
            got = dot3((uh[...], ul[...]), (ah[:, across], al[:, across]), 1, 0)
            qb[s % 2, across] = got.T

        for i in (1, 3, 0, 2):
            y_copy(s, i).start()

    def y_relay(s):
        y_copy(s, 1).wait_recv()
        qb[s % 2, q_rows(row_y, 0)] = qb[s % 2, q_rows(row_y, 0)] + yr[s, 1]
        y_copy(s, 4).start()
        y_copy(s, 3).wait_recv()
        qb[s % 2, q_rows(row_x, 1)] = qb[s % 2, q_rows(row_x, 1)] + yr[s, 3]
        y_copy(s, 5).start()

    def y_end(s):
        for i in (0, 2, 4, 5):
            y_copy(s, i).wait_recv()
        for h, (i, j) in enumerate(((0, 4), (2, 5))):
            yo[s, pl.ds(h * half_y, half_y)] = -(qb[s % 2, q_rows(row, h)] + yr[s, i] + yr[s, j])
        if s > 0:
            yo[s] = yo[s] - dot3(halves(yo[s - 1]), halves(f_ref[s - 1]), 1, 1)

    def y_sent(s):
        for i in range(6):
            y_copy(s, i).wait_send()

    first = ((row == 0) & (col == 0)).astype(f32)

    def fill(value, index):
        _, odd = window(index)
        hi, lo = halves(value)
        win_h[...] = jnp.zeros(win_h.shape, bf16)
        win_l[...] = jnp.zeros(win_l.shape, bf16)
        rows = pl.ds(pl.multiple_of(odd, 64), slab)
        win_h[rows] = hi
        win_l[rows] = lo

    def with_upper(s):
        return dot3((uw_h[s], uw_l[s]), (win_h[...], win_l[...]), 1, 0)

    def d_copy(s):
        return pltpu.make_async_copy(d_ref.at[s], keep.at[0], d_sem)

    def put(value, g, i):
        n = groups[g]
        for r in range(prow):
            for h in range(2):
                at = base(g) + ((h * prow + r) * n + i) * half_l
                pb[pl.ds(at, half_l)] = value[r * part_l + h * half_l : r * part_l + (h + 1) * half_l]

    groups = (3, 3, 1)
    tiles_of = tuple((n + 1) // 2 for n in groups)
    tile_at = (0, tiles_of[0], tiles_of[0] + tiles_of[1])

    def base(g):
        return (0, nz * slab, supers * nz * slab)[g]

    def corner_first():
        d_copy(0).start()
        fill(xo[0], col)
        got = with_upper(0)
        d_copy(0).wait()
        keep[0] = keep[0] * first - got

    def step_sums(s):
        edge_f = halves(f_ref[s - 1])
        corner = keep[0]
        put(corner, s - 1, 0)
        corner = halves(corner)
        fill(xo[s - 1], col)
        put(-(with_upper(s) + dot3(edge_f, corner, 1, 0)), s - 1, 2)
        fill(yo[s - 1], row)
        turned = dot3((lw_h[s - 1], lw_l[s - 1]), (win_h[...], win_l[...]), 1, 0)
        keep[1] = -(turned.T + dot3(corner, halves(e_ref[s - 1]), 1, 0))
        put(keep[1], s - 1, 1)

    def step_corner(s):
        d_copy(s).start()
        fill(xo[s], col)
        got = with_upper(s) + dot3(halves(f_ref[s - 1]), halves(keep[1]), 1, 0)
        d_copy(s).wait()
        keep[0] = keep[0] * first - got

    def s_rows(g, h, r=0, a=0, count=None):
        n = groups[g]
        at = base(g) + (h * prow + r) * n * half_l + a * n * half_l // 2
        return pl.ds(pl.multiple_of(at, 8), count or n * half_l // 2)

    def sp_copy(g):
        size = prow * groups[g] * half_l
        into = sp2 if g == 2 else pr.at[pl.ds(g * size, size)]
        return rc(pb.at[s_rows(g, other, count=size)], into, sp_send.at[g], sp_recv.at[g], to_pair)

    def s_pair(g):
        if g == 0:
            pl.semaphore_wait(free_pair.at[supers - 1], 1)
        sp_copy(g).start()

    def sq_copy(g, i):
        size = groups[g] * half_l // 2
        r, a, dev = (
            (row_x, 0, to_x), (row_d, 0, to_x), (row_y, 1, to_y), (row_d, 1, to_y), (row_y, 0, to_y), (row_x, 1, to_x),
        )[i]
        into = sq.at[i, pl.ds(sum(groups[:g]) * half_l // 2, size)]
        return rc(pb.at[s_rows(g, k, r, a)], into, sq_send.at[g, i], sq_recv.at[g, i], dev)

    def sq_got(g, i):
        return sq[i, pl.ds(sum(groups[:g]) * half_l // 2, groups[g] * half_l // 2)]

    def s_add(g):
        size = prow * groups[g] * half_l
        sp_copy(g).wait_recv()
        mine = s_rows(g, k, count=size)
        pb[mine] = pb[mine] + (sp2[...] if g == 2 else pr[pl.ds(g * size, size)])
        for i in (1, 3, 0, 2):
            sq_copy(g, i).start()

    def s_relay(g):
        for i, r, a, j in ((1, row_y, 0, 4), (3, row_x, 1, 5)):
            sq_copy(g, i).wait_recv()
            there = s_rows(g, k, r, a)
            pb[there] = pb[there] + sq_got(g, i)
            sq_copy(g, j).start()

    def z_rows(g):
        return pl.ds(tile_at[g] * 2 * half_l, tiles_of[g] * 2 * half_l)

    def sn_copy(g, d, way):
        slot = d + 1 - way
        return rc(
            zb.at[d, z_rows(g)], zl.at[slot, z_rows(g)], sn_send.at[g, d], sn_recv.at[g, slot], (up, down)[way]
        )

    def s_turn(g):
        n = groups[g]
        for i in (0, 2, 4, 5):
            sq_copy(g, i).wait_recv()
        for a, (i, j) in enumerate(((0, 4), (2, 5))):
            there = s_rows(g, k, row, a)
            pb[there] = pb[there] + sq_got(g, i) + sq_got(g, j)
        for m in range(tiles_of[g]):
            size = min(2, n - 2 * m) * half_l
            at = base(g) + (k * prow + row) * n * half_l + m * 2 * half_l
            tb[pl.ds(0, size)] = pb[pl.ds(pl.multiple_of(at, 8), size)]
            turned = tb[...].T
            wide = 2 * part_u
            for d in range(nz):
                zb[d, pl.ds((tile_at[g] + m) * wide, wide)] = turned[d * wide : (d + 1) * wide]

        @pl.when(z == 0)
        def _():
            for d in reversed(range(1, nz)):
                sn_copy(g, d, 0).start()

        @pl.when(z == nz - 1)
        def _():
            for d in range(nz - 1):
                sn_copy(g, d, 1).start()

    def s_take(g, d, slot):
        rows = z_rows(g)
        rc(zl.at[slot, rows], zl.at[slot, rows], sn_send.at[g, d], sn_recv.at[g, slot], to_pair).wait_recv()
        zb[d, rows] = zb[d, rows] + zl[slot, rows]

    def s_line(g, t):
        zb_ = nz - 1 - z

        @pl.when((z >= 1) & (z <= t))
        def _():
            d = z + (nz - 1 - t)
            s_take(g, d, d + 1)
            sn_copy(g, d, 0).start()

        @pl.when((zb_ >= 1) & (zb_ <= t))
        def _():
            d = z - (nz - 1 - t)
            s_take(g, d, d)
            sn_copy(g, d, 1).start()

    def sf_copy(tile):
        rows = pl.ds(pl.multiple_of((tile * 2 + other) * part_u, 8), part_u)
        return rc(zb.at[z, rows], zf.at[tile], sf_send.at[tile], sf_recv.at[tile], to_pair)

    def s_last(g):
        when(has_down, lambda: s_take(g, z, z + 1))
        when(has_up, lambda: s_take(g, z, z))
        for m in range(tiles_of[g]):
            sf_copy(tile_at[g] + m).start()

    def s_out(g):
        n = groups[g]
        left = lax.broadcasted_iota(jnp.int32, (part_u, 128), 1) < half_l
        for m in range(tiles_of[g]):
            tile = tile_at[g] + m
            sf_copy(tile).wait_recv()
            mine = zb[z, pl.ds(pl.multiple_of((tile * 2 + k) * part_u, 8), part_u)]
            theirs = zf[tile]
            a, b = jnp.where(k == 0, mine, theirs), jnp.where(k == 0, theirs, mine)
            for i in range(2 * m, min(2 * m + 2, n)):
                if i % 2 == 0:
                    value = jnp.where(left, a, pltpu.roll(b, half_l, 1))
                else:
                    value = jnp.where(left, pltpu.roll(a, 128 - half_l, 1), b)
                value = value[:, :part_l]
                if i == 0:
                    zo[g] = value
                else:
                    co[i - 1, g] = value

    def s_sent(g):
        sp_copy(g).wait_send()
        for i in range(6):
            sq_copy(g, i).wait_send()
        for d in range(nz):
            when(z < d, lambda d=d: sn_copy(g, d, 0).wait_send())
            when(z > d, lambda d=d: sn_copy(g, d, 1).wait_send())
        for m in range(tiles_of[g]):
            sf_copy(tile_at[g] + m).wait_send()

    def middle_0():
        u_step(0, 2)
        when(inside, lambda: u_own(1))
        l_fwd(1)

    def middle_1():
        l_fwd(2)

    def middle_2():
        u_step(2, 1)
        u_step(1, 3)
        y_relay(0)

    tb[...] = jnp.zeros(tb.shape, f32)
    l_start(0)
    u_own(0)
    a_load()
    when(at_end, lambda: u_own(1))
    l_fwd(0)
    l_start(1)
    u_step(0, 1)
    when(at_end, lambda: u_own(2))
    l_done(0)
    l_conv(0)
    p_both(0, middle_0)
    pair_add(0, 0)
    pair_add(0, 1)
    l_start(2)
    u_step(0, 3)
    u_done(0)
    u_conv(0)
    u_step(1, 1)
    q_comp(0)
    line_t(0, 1)
    u_step(1, 2)
    when(inside, lambda: u_own(2))
    l_done(1)
    l_conv(1)
    p_both(1, middle_1)
    pair_add(1, 0)
    pair_add(1, 1)
    line_t(0, 2)
    l_done(2)
    l_conv(2)
    p_both(2, middle_2)
    y_end(0)
    when(inside, lambda: line_take(0))
    line_t(1, 1)
    u_done(1)
    u_conv(1)
    u_step(2, 2)
    q_comp(1)
    pair_add(2, 0)
    pair_add(2, 1)
    when(at_end, lambda: line_take(0))
    n_sent(0)
    x_out(0)
    corner_first()
    step_sums(1)
    s_pair(0)
    line_t(1, 2)
    u_step(2, 3)
    s_add(0)
    y_relay(1)
    u_done(2)
    u_conv(2)
    y_sent(0)
    line_t(2, 1)
    q_comp(2)
    s_relay(0)
    line_take(1)
    x_out(1)
    y_end(1)
    step_corner(1)
    line_t(2, 2)
    n_sent(1)
    step_sums(2)
    s_pair(1)
    s_turn(0)
    y_relay(2)
    s_add(1)
    s_line(0, 1)
    line_take(2)
    x_out(2)
    step_corner(2)
    for half in range(2):
        p_copy(2, half).wait_send()
    put(keep[0], 2, 0)
    s_pair(2)
    s_line(0, 2)
    s_relay(1)
    s_add(2)
    s_last(0)
    s_turn(1)
    s_relay(2)
    s_line(1, 1)
    y_end(2)
    s_out(0)
    s_turn(2)
    s_line(1, 2)
    s_line(2, 1)
    s_last(1)
    s_line(2, 2)
    s_last(2)
    s_out(1)
    s_out(2)

    for s in range(supers):
        for i in range(6):
            l_copy(s, i).wait_send()
        for zs in range(nz):
            for own in (True, False):
                mine = (z == zs) if own else (z != zs)

                @pl.when(mine)
                def _(s=s, zs=zs, own=own):
                    u_copy(s, zs, 2, own).wait_send()

            when((z >= zs) & has_up, lambda s=s, zs=zs: u_copy(s, zs, 0, False).wait_send())
            when((z <= zs) & has_down, lambda s=s, zs=zs: u_copy(s, zs, 1, False).wait_send())
    n_sent(2)
    y_sent(1)
    y_sent(2)
    s_sent(0)
    s_sent(1)
    s_sent(2)


def part_u_is_half(width, prow, pcol):
    return 2 * (width // pcol) == width // prow and (width // prow) % 48 == 0


def fits(shape):
    supers, width, blk, prow, pcol, rows_here, cols_here, slab = shape
    return (
        supers == 3 and prow == 4 and pcol % 4 == 0 and blk == 128 and width % blk == 0
        and slab % 64 == 0 and width == slab + 64 and slab % 128 == 64
        and rows_here % 640 == 0 and cols_here % 640 == 0
        and width % (8 * pcol) == 0 and width // prow <= 128
        and part_u_is_half(width, prow, pcol) and 3 * width <= (pcol // 2) * slab
    )


def sweep(shape, anc_inverse, lower, upper, lower_edge, upper_edge, diag_inverse, mask):
    supers, width, blk, prow, pcol, rows_here, cols_here, slab = shape
    nz = pcol // 2
    part_u = width // pcol
    sums, sum_tiles = 3 * supers - 2, 2 * supers - 1
    vmem, dma = pltpu.VMEM, pltpu.SemaphoreType.DMA
    in_vmem = pl.BlockSpec(memory_space=pltpu.VMEM)
    in_hbm = pl.BlockSpec(memory_space=pl.ANY)
    out = [
        ((supers, slab, width), in_vmem),
        ((supers, slab, width), in_vmem),
        ((supers, part_u, width // prow), in_vmem),
        ((2, supers - 1, part_u, width // prow), in_vmem),
        ((supers, width, cols_here), in_hbm),
        ((supers, width, rows_here), in_hbm),
    ]
    return pl.pallas_call(
        functools.partial(sweep_kernel, (supers, width, blk, prow, nz, rows_here, cols_here, slab)),
        name="sweep",
        out_shape=[jax.ShapeDtypeStruct(dims, f32) for dims, _ in out],
        in_specs=[in_hbm, in_hbm, in_hbm, in_vmem, in_vmem, in_hbm, pl.BlockSpec(memory_space=pltpu.SMEM)],
        out_specs=[spec for _, spec in out],
        scratch_shapes=[
            vmem((rows_here, cols_here), bf16),
            vmem((rows_here, cols_here), bf16),
            vmem((width, cols_here), bf16),
            vmem((width, cols_here), bf16),
            vmem((width, rows_here), bf16),
            vmem((width, rows_here), bf16),
            vmem((2, width, cols_here // 2), f32),
            vmem(((supers + 1) * nz * slab, width), f32),
            vmem((nz * slab, width), f32),
            vmem((2, nz + 1, slab, width), f32),
            vmem((2, cols_here, width), f32),
            vmem((supers, 6, slab // 2, width), f32),
            vmem((supers, width, width), bf16),
            vmem((supers, width, width), bf16),
            vmem((supers - 1, width, width), bf16),
            vmem((supers - 1, width, width), bf16),
            vmem((width, width), bf16),
            vmem((width, width), bf16),
            vmem((2, width, width), f32),
            vmem((prow * width // (2 * prow), width), f32),
            vmem((6, sums * width // (4 * prow), width), f32),
            vmem((128, width), f32),
            vmem((nz, sum_tiles * 2 * part_u, 128), f32),
            vmem((nz + 1, sum_tiles * 2 * part_u, 128), f32),
            vmem((sum_tiles, part_u, 128), f32),
            dma((2 * nz,)),
            dma((2,)),
            dma,
            dma((supers, 6)),
            dma((supers, 6)),
            dma((supers, nz, 3)),
            dma((supers, nz)),
            dma((supers, nz)),
            dma((supers, 2)),
            dma((supers, 2)),
            dma((supers, nz)),
            dma((supers, nz + 1)),
            dma((supers, 6)),
            dma((supers, 6)),
            dma((supers,)),
            dma((supers,)),
            dma((supers, 6)),
            dma((supers, 6)),
            dma((supers, nz)),
            dma((supers, nz + 1)),
            dma((sum_tiles,)),
            dma((sum_tiles,)),
            pltpu.SemaphoreType.REGULAR,
            pltpu.SemaphoreType.REGULAR,
            pltpu.SemaphoreType.REGULAR((supers,)),
        ],
        compiler_params=pltpu.CompilerParams(
            collective_id=0, has_side_effects=True, vmem_limit_bytes=67043328
        ),
    )(anc_inverse, lower, upper, lower_edge, upper_edge, diag_inverse, mask)


def per_device(anc_inverse, lower_anc, upper_anc, lower_edge, upper_edge, diag_inverse, tile_mask):
    rows_here, cols_here = anc_inverse.shape
    prow, pcol = lax.axis_size("row"), lax.axis_size("col")
    supers, width = diag_inverse.shape[0], diag_inverse.shape[1]
    blk = width // tile_mask.shape[2]
    shape = (supers, width, blk, prow, pcol, rows_here, cols_here, cols_here // prow)
    args = (anc_inverse, lower_anc, upper_anc, lower_edge, upper_edge, diag_inverse, tile_mask)
    if not fits(shape):
        return general(*args)
    x, y, corner, cross, _, _ = sweep(
        shape,
        anc_inverse,
        jnp.transpose(lower_anc, (1, 2, 0)),
        jnp.transpose(upper_anc, (1, 2, 0)),
        lower_edge,
        upper_edge,
        diag_inverse,
        jnp.transpose(tile_mask, (0, 2, 1)),
    )
    return (
        jnp.transpose(x, (1, 0, 2)),
        jnp.transpose(y, (1, 0, 2))[None, None],
        jnp.transpose(corner, (0, 2, 1)),
        jnp.transpose(cross, (0, 1, 3, 2)),
    )


precise = lax.Precision.HIGH


def contract(left, right, left_dim, right_dim):
    return lax.dot_general(
        left,
        right,
        (((left_dim,), (right_dim,)), ((), ())),
        precision=precise,
        preferred_element_type=jnp.float32,
    )


def row_major(array):
    return with_layout_constraint(array, Layout(major_to_minor=(0, 1)))


def partner(index, step, count):
    if count & (count - 1) == 0:
        return index ^ step
    return (step - index) % count


def exchange(piece_for, axis):
    count = lax.axis_size(axis)
    index = lax.axis_index(axis)
    got = []
    for step in range(count):
        peer = partner(index, step, count)
        piece = piece_for(peer)
        pairs = [(i, partner(i, step, count)) for i in range(count)]
        if any(i != j for i, j in pairs):
            piece = lax.ppermute(piece, axis, pairs)
        got.append((peer, piece))
    return got


def mask_factor(factor, tile_mask, first_row, first_col, blk):
    rows, supers, cols = factor.shape
    blocks = rows // blk
    window = lax.dynamic_slice_in_dim(tile_mask, first_row // blk, blocks, 1).astype(jnp.float32)
    tile_cols = window.shape[2]
    tile_of_col = (first_col + jnp.arange(cols)) // blk
    pick = (tile_of_col[None, :] == jnp.arange(tile_cols)[:, None]).astype(jnp.float32)
    chosen = sum(window[:, :, t, None] * pick[t] for t in range(tile_cols))
    chosen = jnp.transpose(chosen, (1, 0, 2))
    masked = factor.reshape(blocks, blk, supers, cols) * chosen[:, None]
    return jnp.transpose(masked.reshape(rows, supers, cols), (1, 2, 0))


def general(anc_inverse, lower_anc, upper_anc, lower_edge, upper_edge, diag_inverse, tile_mask):
    rows_here, cols_here = anc_inverse.shape
    prow = lax.axis_size("row")
    pcol = lax.axis_size("col")
    supers, width = diag_inverse.shape[0], diag_inverse.shape[1]
    blk = width // tile_mask.shape[2]
    row = lax.axis_index("row")
    col = lax.axis_index("col")
    part_lower = width // prow
    part_upper = width // pcol

    upper_t = mask_factor(upper_anc, tile_mask, row * rows_here, col * part_upper, blk)
    lower_t = mask_factor(lower_anc, tile_mask, col * cols_here, row * part_lower, blk)

    upper_t = lax.all_gather(upper_t, "col", axis=0)
    lower_full = jnp.zeros((supers, prow, part_lower, cols_here), jnp.float32)
    for peer, piece in exchange(lambda _: lower_t, "row"):
        lower_full = lax.dynamic_update_slice(lower_full, piece[:, None], (0, peer, 0, 0))
    lower_full = lower_full.reshape(supers, width, cols_here)
    lower_comb = [-lower_full[0]]
    for s in range(1, supers):
        lower_comb.append(-lower_full[s] - contract(lower_edge[s - 1], lower_comb[-1], 0, 0))
    cols_part = [row_major(contract(anc_inverse, one, 1, 1)) for one in lower_comb]
    cols_mine = [lax.psum_scatter(one, "col", scatter_dimension=0, tiled=True) for one in cols_part]

    upper_full = [upper_t[:, s].reshape(width, rows_here) for s in range(supers)]
    upper_comb = [-upper_full[0]]
    for s in range(1, supers):
        upper_comb.append(-upper_full[s] - contract(upper_edge[s - 1], upper_comb[-1], 1, 0))
    rows_part = [row_major(contract(anc_inverse, one, 0, 1)) for one in upper_comb]

    first = jnp.logical_and(row == 0, col == 0)
    corner = []
    cross_cols = []
    cross_rows = []
    for s in range(supers):
        upper_here = contract(upper_full[s], cols_part[s], 1, 0)
        now = jnp.where(first, diag_inverse[s], 0.0) - upper_here
        if s > 0:
            upper_prev = contract(upper_full[s], cols_part[s - 1], 1, 0)
            lower_prev = lax.dot_general(
                rows_part[s - 1],
                lower_full[s],
                (((0,), (1,)), ((), ())),
                precision=precise,
                preferred_element_type=jnp.float32,
            )
            cross_col = -(lower_prev + contract(corner[-1], lower_edge[s - 1], 1, 0))
            cross_row = -(upper_prev + contract(upper_edge[s - 1], corner[-1], 1, 0))
            now = now - contract(upper_edge[s - 1], cross_col, 1, 0)
            cross_cols.append(cross_col)
            cross_rows.append(cross_row)
        corner.append(now)
    sums = jnp.stack(corner + cross_cols + cross_rows)
    count = sums.shape[0]

    row_slab = cols_here // prow
    rows_mine = [
        sum(
            piece
            for _, piece in exchange(
                lambda peer: lax.dynamic_slice_in_dim(one, peer * row_slab, row_slab, 0), "row"
            )
        )
        for one in rows_part
    ]
    sums, rows_mine = lax.optimization_barrier((sums, rows_mine))
    sums = sum(
        piece
        for _, piece in exchange(
            lambda peer: lax.dynamic_slice_in_dim(sums, peer * part_lower, part_lower, 1), "row"
        )
    )
    sums = jnp.transpose(sums.reshape(count * part_lower, width))
    sums, cols_mine = lax.optimization_barrier((sums, cols_mine))
    sums = lax.psum_scatter(sums, "col", scatter_dimension=0, tiled=True)
    sums = jnp.transpose(sums).reshape(count, part_lower, part_upper)

    x_blocks = jnp.stack(cols_mine, axis=1)
    y_blocks = jnp.stack(rows_mine, axis=1)[None, None]
    z_blocks = sums[:supers]
    cross_blocks = sums[supers:].reshape(2, supers - 1, part_lower, part_upper)
    return (x_blocks, y_blocks, z_blocks, cross_blocks)


def solution(mesh):
    return jax.shard_map(
        per_device,
        mesh=mesh,
        in_specs=(
            P("row", "col"),
            P("col", None, "row"),
            P("row", None, "col"),
            P(),
            P(),
            P(),
            P(),
        ),
        out_specs=(
            P(("row", "col"), None, None),
            P("col", "row", None, None, None),
            P(None, "row", "col"),
            P(None, None, "row", "col"),
        ),
        check_vma=False,
    )
```

```python
import functools

import jax
import jax.numpy as jnp
from jax import lax
from jax.experimental import pallas as pl
from jax.experimental.pallas import tpu as pltpu
from jax.experimental.layout import Layout, with_layout_constraint
from jax.sharding import PartitionSpec as P


f32 = jnp.float32
bf16 = jnp.bfloat16


def halves(value):
    hi = value.astype(bf16)
    return hi, (value - hi.astype(f32)).astype(bf16)


def dot3(left, right, left_dim, right_dim):
    dims = (((left_dim,), (right_dim,)), ((), ()))

    def one(a, b):
        return lax.dot_general(a, b, dims, preferred_element_type=f32)

    return one(left[0], right[0]) + (one(left[0], right[1]) + one(left[1], right[0]))


def sweep_kernel(
    shape,
    a_ref, l_ref, u_ref, e_ref, f_ref, d_ref, mask_ref,
    x_hbm, y_hbm, zo, co, lbuf, ubuf,
    ah, al, lh, ll, uh, ul, stage, pb, pr, ln, qb, yr, uw_h, uw_l, lw_h, lw_l, win_h, win_l, keep,
    sp2, sq, sqd, tb, zb, zl, zf, xo, yo,
    a_sem, st_sem, d_sem, l_send, l_recv, u_send, u_recv, up_recv, p_send, p_recv, n_send, n_recv,
    y_send, y_recv, sp_send, sp_recv, sq_send, sq_recv, sn_send, sn_recv, sf_send, sf_recv,
    free_up, free_down, free_pair, o_sem,
):
    supers, width, blk, prow, nz, rows_here, cols_here, slab = shape
    pcol = 2 * nz
    part_l, part_u = width // prow, width // pcol
    row = lax.axis_index("row")
    col = lax.axis_index("col")
    z, k = col // 2, col % 2
    other = 1 - k
    y, x = row // 2, row % 2
    row_x, row_y, row_d = y * 2 + 1 - x, (1 - y) * 2 + x, (1 - y) * 2 + 1 - x
    to_x, to_y, to_d = {"row": row_x}, {"row": row_y}, {"row": row_d}
    to_pair = {"col": col + 1 - 2 * k}
    up, down = {"col": col + 2}, {"col": col - 2}
    has_up, has_down = z < nz - 1, z > 0
    at_end, inside = (z == 0) | (z == nz - 1), (z > 0) & (z < nz - 1)

    def when(cond, body):
        pl.when(cond)(body)

    def rc(src, dst, ss, rs, dev):
        return pltpu.make_async_remote_copy(
            src_ref=src, dst_ref=dst, send_sem=ss, recv_sem=rs,
            device_id=dev, device_id_type=pl.DeviceIdType.MESH,
        )

    barrier = pltpu.get_barrier_semaphore()

    def greet(dev):
        pl.semaphore_signal(barrier, inc=1, device_id=dev, device_id_type=pl.DeviceIdType.MESH)

    for dev in (to_x, to_y, to_d, to_pair):
        greet(dev)
    for there in range(nz):
        when(z != there, lambda: greet({"col": 2 * there + k}))
    pl.semaphore_wait(barrier, 4 + nz - 1)

    half_l = part_l // 2

    def l_piece(s, r, h):
        return lbuf.at[s, pl.ds(pl.multiple_of(r * part_l + h * half_l, 8), half_l)]

    def l_own(s, h):
        return l_ref.at[s, pl.ds(h * half_l, half_l)]

    def l_copy(s, i):
        src, dst, dev = (
            (l_own(s, 1), l_piece(s, row, 1), to_x),
            (l_own(s, 0), l_piece(s, row, 0), to_y),
            (l_own(s, 0), l_piece(s, row, 0), to_x),
            (l_own(s, 1), l_piece(s, row, 1), to_y),
            (l_piece(s, row_x, 1), l_piece(s, row_x, 1), to_y),
            (l_piece(s, row_y, 0), l_piece(s, row_y, 0), to_x),
        )[i]
        return rc(src, dst, l_send.at[s, i], l_recv.at[s, i], dev)

    def l_take(s, i):
        r, h = ((row_x, 1), (row_y, 0), (row_x, 0), (row_y, 1), (row_d, 1), (row_d, 0))[i]
        rc(l_piece(s, r, h), l_piece(s, r, h), l_send.at[s, i], l_recv.at[s, i], to_pair).wait_recv()

    def l_start(s):
        for i in range(4):
            l_copy(s, i).start()

    def l_fwd(s):
        l_take(s, 0)
        l_copy(s, 4).start()
        l_take(s, 1)
        l_copy(s, 5).start()

    def l_done(s):
        for i in range(2, 6):
            l_take(s, i)

    def u_piece(s, c):
        return ubuf.at[s, pl.ds(pl.multiple_of(c * part_u, 8), part_u)]

    def u_copy(s, zs, way, own):
        mine = u_piece(s, zs * 2 + k)
        src = u_ref.at[s] if own else mine
        recv = up_recv if way == 2 else u_recv
        return rc(src, mine, u_send.at[s, zs, way], recv.at[s, zs], (up, down, to_pair)[way])

    def u_own(s):
        when(has_up, lambda: u_copy(s, z, 0, True).start())
        when(has_down, lambda: u_copy(s, z, 1, True).start())
        u_copy(s, z, 2, True).start()

    def u_low(s, t, cond):
        @pl.when((z >= t) & cond)
        def _():
            u_copy(s, z - t, 1, False).wait_recv()
            when(has_up, lambda: u_copy(s, z - t, 0, False).start())
            u_copy(s, z - t, 2, False).start()

    def u_high(s, t, cond):
        @pl.when((z + t < nz) & cond)
        def _():
            u_copy(s, z + t, 0, False).wait_recv()
            when(has_down, lambda: u_copy(s, z + t, 1, False).start())
            u_copy(s, z + t, 2, False).start()

    def u_step(s, t, cond=None):
        cond = z >= 0 if cond is None else cond
        u_low(s, t, cond)
        u_high(s, t, cond)

    def u_from_ends(s):
        u_low(s, 1, inside & (z == 1))
        u_high(s, 1, inside & (z == nz - 2))

    def u_from_inside(s):
        u_low(s, 1, inside & (z > 1))
        u_high(s, 1, inside & (z < nz - 2))

    def u_done(s):
        for zs in range(nz):
            piece = u_piece(s, zs * 2 + other)
            rc(piece, piece, u_send.at[s, zs, 2], up_recv.at[s, zs], to_pair).wait_recv()

    lanes = stage.shape[2]
    tiles = lanes // blk

    def load(buf, own_ref, s, count, me, part, q):
        here = pl.ds(q * lanes, lanes)

        @pl.loop(0, count)
        def _(p):
            there = stage.at[q % 2, pl.ds(pl.multiple_of(p * part, 8), part)]

            @pl.when(p != me)
            def _():
                pltpu.make_async_copy(
                    buf.at[s, pl.ds(pl.multiple_of(p * part, 8), part), here], there, st_sem.at[q % 2]
                ).start()

            @pl.when(p == me)
            def _():
                pltpu.make_async_copy(own_ref.at[s, :, here], there, st_sem.at[q % 2]).start()

    def convert(buf, own_ref, s, count, me, part, total, first_tile, out_h, out_l):
        load(buf, own_ref, s, count, me, part, 0)
        for q in range(total // lanes):
            if q + 1 < total // lanes:
                load(buf, own_ref, s, count, me, part, q + 1)
            pltpu.make_async_copy(stage.at[q % 2], stage.at[q % 2], st_sem.at[q % 2]).wait()

            @pl.loop(0, tiles)
            def _(t):
                src = pl.ds(pl.multiple_of(t * blk, 128), blk)
                dst = pl.ds(pl.multiple_of(q * lanes + t * blk, 128), blk)
                for j in range(width // blk):
                    keep_it = mask_ref[s, j, first_tile + q * tiles + t].astype(f32)
                    rows = pl.ds(j * blk, blk)
                    hi, lo = halves(stage[q % 2, rows, src] * keep_it)
                    out_h[rows, dst] = hi
                    out_l[rows, dst] = lo

    def window(index):
        start = index * slab
        odd = start % 128
        return pl.ds(pl.multiple_of(start - odd, 128), width), odd

    def l_conv(s):
        convert(lbuf, l_ref, s, prow, row, part_l, cols_here, col * (cols_here // blk), lh, ll)
        if s > 0:
            where, _ = window(row)
            lw_h[s - 1] = lh[:, where]
            lw_l[s - 1] = ll[:, where]

    def u_conv(s):
        convert(ubuf, u_ref, s, pcol, col, part_u, rows_here, row * (rows_here // blk), uh, ul)
        where, _ = window(col)
        uw_h[s] = uh[:, where]
        uw_l[s] = ul[:, where]

    a_lanes = 256
    a_cols = cols_here // a_lanes
    a_slots = 2 * nz

    def a_copy(n, slot):
        i, j = n // a_cols, n % a_cols
        return pltpu.make_async_copy(
            a_ref.at[pl.ds(pl.multiple_of(i * slab, 8), slab), pl.ds(pl.multiple_of(j * a_lanes, 128), a_lanes)],
            pb.at[pl.ds(pl.multiple_of(slot * slab, 64), slab), pl.ds(0, a_lanes)],
            a_sem.at[slot],
        )

    def a_load():
        count = (rows_here // slab) * a_cols
        for n in range(a_slots - 1):
            a_copy(n, n).start()

        @pl.loop(0, count)
        def _(n):
            slot = n % a_slots

            @pl.when(n + a_slots - 1 < count)
            def _():
                a_copy(n + a_slots - 1, (n + a_slots - 1) % a_slots).start()

            a_copy(n, slot).wait()
            i, j = n // a_cols, n % a_cols
            across = pl.ds(pl.multiple_of(j * a_lanes, 128), a_lanes)
            step = 64
            for b in range(slab // step):
                hi, lo = halves(pb[pl.ds(pl.multiple_of(slot * slab + b * step, 64), step), pl.ds(0, a_lanes)])
                down_to = pl.ds(pl.multiple_of(i * slab + b * step, 64), step)
                ah[down_to, across] = hi
                al[down_to, across] = lo

    hz = nz // 2
    h_rows = rows_here // 2

    def far(i):
        flip = (z < hz).astype(jnp.int32)
        return (flip + i) % 2

    def p_rows(s, d, n=1):
        return pl.ds(pl.multiple_of((s * nz + d) * slab, 64), n * slab)

    def p_copy(s, hh):
        return rc(
            pb.at[p_rows(supers, hh * hz, hz)], pr.at[p_rows(0, hh * hz, hz)],
            p_send.at[s, hh], p_recv.at[s, hh], to_pair,
        )

    def p_both(s, middle):
        @pl.loop(0, 2)
        def _(i):
            when(i == 1, middle)
            hh = far(i)
            if s > 0:
                p_copy(s - 1, hh).wait_send()
            rows = pl.ds(pl.multiple_of(hh * h_rows, 128), h_rows)
            got = dot3((lh[...], ll[...]), (ah[rows], al[rows]), 1, 1).T
            for q in range(2 * hz):
                spot = jnp.where(k == q % 2, s, supers)
                pb[p_rows(spot, hh * hz + q // 2)] = got[q * slab : (q + 1) * slab]
            if s > 0:
                when(i == 0, lambda: pl.semaphore_wait(free_pair.at[s - 1], 1))
            p_copy(s, hh).start()

    def n_copy(s, d, way):
        slot = d + 1 - way
        return rc(pb.at[p_rows(s, d)], ln.at[s % 2, slot], n_send.at[s, d], n_recv.at[s, slot], (up, down)[way])

    def n_take(s, d, slot):
        rc(ln.at[s % 2, slot], ln.at[s % 2, slot], n_send.at[s, d], n_recv.at[s, slot], to_pair).wait_recv()
        pb[p_rows(s, d)] = pb[p_rows(s, d)] + ln[s % 2, slot]

    def tell(sem, dev):
        pl.semaphore_signal(sem, inc=1, device_id=dev, device_id_type=pl.DeviceIdType.MESH)

    def line_wait():
        when(has_up, lambda: pl.semaphore_wait(free_up, 1))
        when(has_down, lambda: pl.semaphore_wait(free_down, 1))

    def pair_add(s, i):
        if s == 2 and i == 0:
            when(at_end, line_wait)
        hh = far(i)
        p_copy(s, hh).wait_recv()
        for q in range(hz):
            d = hh * hz + q
            pb[p_rows(s, d)] = pb[p_rows(s, d)] + pr[p_rows(0, d)]
        if i == 1:
            tell(free_pair.at[s], to_pair)
        lo, hi = (1 - i) * hz, (2 - i) * hz

        @pl.when(z == 0)
        def _():
            for d in reversed(range(max(lo, 1), hi)):
                n_copy(s, d, 0).start()

        lo, hi = i * hz, (i + 1) * hz

        @pl.when(z == nz - 1)
        def _():
            for d in range(lo, min(hi, nz - 1)):
                n_copy(s, d, 1).start()

    def line_t(s, t):
        zb_ = nz - 1 - z
        if s == 2 and t == 1:
            when(inside, line_wait)

        @pl.when((z >= 1) & (z <= t))
        def _():
            d = z + (nz - 1 - t)
            n_take(s, d, d + 1)
            n_copy(s, d, 0).start()

        @pl.when((zb_ >= 1) & (zb_ <= t))
        def _():
            d = z - (nz - 1 - t)
            n_take(s, d, d)
            n_copy(s, d, 1).start()

    def line_take(s):
        when(has_down, lambda: n_take(s, z, z + 1))
        when(has_up, lambda: n_take(s, z, z))
        if s == 0:
            when(has_down, lambda: tell(free_up, down))
            when(has_up, lambda: tell(free_down, up))

    def x_leave(s):
        return pltpu.make_async_copy(xo.at[s], x_hbm.at[s], o_sem.at[0, s])

    def y_leave(s):
        return pltpu.make_async_copy(yo.at[s], y_hbm.at[s], o_sem.at[1, s])

    def x_out(s):
        total = -pb[p_rows(s, z)]
        if s > 0:
            total = total - dot3(halves(xo[s - 1]), halves(e_ref[s - 1]), 1, 0)
        xo[s] = total
        x_leave(s).start()

    def n_sent(s):
        for d in range(nz):
            when(z < d, lambda d=d: n_copy(s, d, 0).wait_send())
            when(z > d, lambda d=d: n_copy(s, d, 1).wait_send())

    half_y = slab // 2
    q_cols = 256

    def q_rows(r, h):
        return pl.ds(pl.multiple_of(r * slab + h * half_y, 8), half_y)

    def q_slab(s, r, h):
        return qb.at[s % 2, q_rows(r, h)]

    def y_copy(s, i):
        src, dev = (
            (q_slab(s, row_x, 0), to_x),
            (q_slab(s, row_d, 0), to_x),
            (q_slab(s, row_y, 1), to_y),
            (q_slab(s, row_d, 1), to_y),
            (q_slab(s, row_y, 0), to_y),
            (q_slab(s, row_x, 1), to_x),
        )[i]
        return rc(src, yr.at[s, i], y_send.at[s, i], y_recv.at[s, i], dev)

    def q_comp(s, late=None):
        count = cols_here // q_cols

        @pl.loop(0, count)
        def _(i):
            @pl.when(i == 2)
            def _():
                y_copy(s, 1).start()
                y_copy(s, 3).start()

            if late is not None:
                when(i == count - 1, late)
            across = pl.ds(pl.multiple_of((row_d + i) % count * q_cols, 128), q_cols)
            got = dot3((uh[...], ul[...]), (ah[:, across], al[:, across]), 1, 0)
            qb[s % 2, across] = got.T

        if late is None:
            y_own(s)

    def y_own(s):
        y_copy(s, 0).start()
        y_copy(s, 2).start()

    def y_relay(s):
        y_copy(s, 1).wait_recv()
        qb[s % 2, q_rows(row_y, 0)] = qb[s % 2, q_rows(row_y, 0)] + yr[s, 1]
        y_copy(s, 4).start()
        y_copy(s, 3).wait_recv()
        qb[s % 2, q_rows(row_x, 1)] = qb[s % 2, q_rows(row_x, 1)] + yr[s, 3]
        y_copy(s, 5).start()

    def y_end(s):
        for i in (0, 2, 4, 5):
            y_copy(s, i).wait_recv()
        for h, (i, j) in enumerate(((0, 4), (2, 5))):
            yo[s, pl.ds(h * half_y, half_y)] = -(qb[s % 2, q_rows(row, h)] + yr[s, i] + yr[s, j])
        if s > 0:
            yo[s] = yo[s] - dot3(halves(yo[s - 1]), halves(f_ref[s - 1]), 1, 1)
        y_leave(s).start()

    def y_sent(s):
        for i in range(6):
            y_copy(s, i).wait_send()

    first = ((row == 0) & (col == 0)).astype(f32)

    def fill(value, index):
        _, odd = window(index)
        hi, lo = halves(value)
        win_h[...] = jnp.zeros(win_h.shape, bf16)
        win_l[...] = jnp.zeros(win_l.shape, bf16)
        rows = pl.ds(pl.multiple_of(odd, 64), slab)
        win_h[rows] = hi
        win_l[rows] = lo

    def with_upper(s):
        return dot3((uw_h[s], uw_l[s]), (win_h[...], win_l[...]), 1, 0)

    def d_copy(s):
        return pltpu.make_async_copy(d_ref.at[s], keep.at[0], d_sem)

    def put(value, g, i):
        n = groups[g]
        for r in range(prow):
            for h in range(2):
                at = base(g) + ((h * prow + r) * n + i) * half_l
                pb[pl.ds(at, half_l)] = value[r * part_l + h * half_l : r * part_l + (h + 1) * half_l]

    groups = (3, 3, 1)
    tiles_of = tuple((n + 1) // 2 for n in groups)
    tile_at = (0, tiles_of[0], tiles_of[0] + tiles_of[1])

    def base(g):
        return (0, nz * slab, supers * nz * slab)[g]

    def corner_first():
        d_copy(0).start()
        fill(xo[0], col)
        got = with_upper(0)
        d_copy(0).wait()
        keep[0] = keep[0] * first - got

    def step_sums(s):
        edge_f = halves(f_ref[s - 1])
        corner = keep[0]
        put(corner, s - 1, 0)
        corner = halves(corner)
        fill(xo[s - 1], col)
        put(-(with_upper(s) + dot3(edge_f, corner, 1, 0)), s - 1, 2)
        fill(yo[s - 1], row)
        turned = dot3((lw_h[s - 1], lw_l[s - 1]), (win_h[...], win_l[...]), 1, 0)
        keep[1] = -(turned.T + dot3(corner, halves(e_ref[s - 1]), 1, 0))
        put(keep[1], s - 1, 1)

    def step_corner(s):
        d_copy(s).start()
        fill(xo[s], col)
        got = with_upper(s) + dot3(halves(f_ref[s - 1]), halves(keep[1]), 1, 0)
        d_copy(s).wait()
        keep[0] = keep[0] * first - got

    def s_rows(g, h, r=0, a=0, count=None):
        n = groups[g]
        at = base(g) + (h * prow + r) * n * half_l + a * n * half_l // 2
        return pl.ds(pl.multiple_of(at, 8), count or n * half_l // 2)

    def sp_copy(g):
        size = prow * groups[g] * half_l
        into = sp2 if g == 2 else pr.at[pl.ds(g * size, size)]
        return rc(pb.at[s_rows(g, other, count=size)], into, sp_send.at[g], sp_recv.at[g], to_pair)

    def s_pair(g):
        if g == 0:
            pl.semaphore_wait(free_pair.at[supers - 1], 1)
        sp_copy(g).start()

    def sq_copy(g, i):
        size = groups[g] * half_l // 2
        r, a, dev = (
            (row_x, 0, to_x), (row_d, 0, to_x), (row_y, 1, to_y), (row_d, 1, to_y), (row_y, 0, to_y), (row_x, 1, to_x),
        )[i]
        into = sq.at[i, pl.ds(sum(groups[:g]) * half_l // 2, size)]
        return rc(pb.at[s_rows(g, k, r, a)], into, sq_send.at[g, i], sq_recv.at[g, i], dev)

    def sq_got(g, i):
        return sq[i, pl.ds(sum(groups[:g]) * half_l // 2, groups[g] * half_l // 2)]

    def sd_copy(r, me, dev):
        return rc(
            pb.at[s_rows(2, k, r, 0, groups[2] * half_l)], sqd.at[me], sq_send.at[2, r], sq_recv.at[2, me], dev
        )

    rows_to = ((row_x, to_x), (row_y, to_y), (row_d, to_d))

    def s_add(g):
        size = prow * groups[g] * half_l
        sp_copy(g).wait_recv()
        mine = s_rows(g, k, count=size)
        pb[mine] = pb[mine] + (sp2[...] if g == 2 else pr[pl.ds(g * size, size)])
        if g == 2:
            for r, dev in rows_to:
                sd_copy(r, row, dev).start()
        else:
            for i in (1, 3, 0, 2):
                sq_copy(g, i).start()

    def s_relay(g):
        for i, r, a, j in ((1, row_y, 0, 4), (3, row_x, 1, 5)):
            sq_copy(g, i).wait_recv()
            there = s_rows(g, k, r, a)
            pb[there] = pb[there] + sq_got(g, i)
            sq_copy(g, j).start()

    def z_rows(g):
        return pl.ds(tile_at[g] * 2 * half_l, tiles_of[g] * 2 * half_l)

    def sn_copy(g, d, way):
        slot = d + 1 - way
        return rc(
            zb.at[d, z_rows(g)], zl.at[slot, z_rows(g)], sn_send.at[g, d], sn_recv.at[g, slot], (up, down)[way]
        )

    def sz_copy(d):
        rows = z_rows(2)
        return rc(zb.at[d, rows], zl.at[z, rows], sn_send.at[2, d], sn_recv.at[2, z], {"col": 2 * d + k})

    def s_turn(g):
        n = groups[g]
        if g == 2:
            there = s_rows(2, k, row, 0, n * half_l)
            for r, dev in rows_to:
                sd_copy(r, r, dev).wait_recv()
            pb[there] = (pb[there] + sqd[row_x]) + (sqd[row_y] + sqd[row_d])
        else:
            for i in (0, 2, 4, 5):
                sq_copy(g, i).wait_recv()
            for a, (i, j) in enumerate(((0, 4), (2, 5))):
                there = s_rows(g, k, row, a)
                pb[there] = pb[there] + sq_got(g, i) + sq_got(g, j)
        for m in range(tiles_of[g]):
            size = min(2, n - 2 * m) * half_l
            at = base(g) + (k * prow + row) * n * half_l + m * 2 * half_l
            tb[pl.ds(0, size)] = pb[pl.ds(pl.multiple_of(at, 8), size)]
            turned = tb[...].T
            wide = 2 * part_u
            for d in range(nz):
                zb[d, pl.ds((tile_at[g] + m) * wide, wide)] = turned[d * wide : (d + 1) * wide]
        if g == 2:
            for d in range(nz):
                when(z != d, lambda: sz_copy(d).start())
            return

        @pl.when(z == 0)
        def _():
            for d in reversed(range(1, nz)):
                sn_copy(g, d, 0).start()

        @pl.when(z == nz - 1)
        def _():
            for d in range(nz - 1):
                sn_copy(g, d, 1).start()

    def s_take(g, d, slot):
        rows = z_rows(g)
        rc(zl.at[slot, rows], zl.at[slot, rows], sn_send.at[g, d], sn_recv.at[g, slot], to_pair).wait_recv()
        zb[d, rows] = zb[d, rows] + zl[slot, rows]

    def s_line(g, t):
        zb_ = nz - 1 - z

        @pl.when((z >= 1) & (z <= t))
        def _():
            d = z + (nz - 1 - t)
            s_take(g, d, d + 1)
            sn_copy(g, d, 0).start()

        @pl.when((zb_ >= 1) & (zb_ <= t))
        def _():
            d = z - (nz - 1 - t)
            s_take(g, d, d)
            sn_copy(g, d, 1).start()

    def sf_copy(tile):
        rows = pl.ds(pl.multiple_of((tile * 2 + other) * part_u, 8), part_u)
        return rc(zb.at[z, rows], zf.at[tile], sf_send.at[tile], sf_recv.at[tile], to_pair)

    def s_last(g):
        if g == 2:
            for there in range(nz):
                when(z != there, lambda: s_take(g, z, there))
        else:
            when(has_down, lambda: s_take(g, z, z + 1))
            when(has_up, lambda: s_take(g, z, z))
        for m in range(tiles_of[g]):
            sf_copy(tile_at[g] + m).start()

    def s_out(g):
        n = groups[g]
        left = lax.broadcasted_iota(jnp.int32, (part_u, 128), 1) < half_l
        for m in range(tiles_of[g]):
            tile = tile_at[g] + m
            sf_copy(tile).wait_recv()
            mine = zb[z, pl.ds(pl.multiple_of((tile * 2 + k) * part_u, 8), part_u)]
            theirs = zf[tile]
            a, b = jnp.where(k == 0, mine, theirs), jnp.where(k == 0, theirs, mine)
            for i in range(2 * m, min(2 * m + 2, n)):
                if i % 2 == 0:
                    value = jnp.where(left, a, pltpu.roll(b, half_l, 1))
                else:
                    value = jnp.where(left, pltpu.roll(a, 128 - half_l, 1), b)
                value = value[:, :part_l]
                if i == 0:
                    zo[g] = value
                else:
                    co[i - 1, g] = value

    def s_sent(g):
        sp_copy(g).wait_send()
        if g == 2:
            for r, dev in rows_to:
                sd_copy(r, row, dev).wait_send()
            for d in range(nz):
                when(z != d, lambda: sz_copy(d).wait_send())
        else:
            for i in range(6):
                sq_copy(g, i).wait_send()
            for d in range(nz):
                when(z < d, lambda: sn_copy(g, d, 0).wait_send())
                when(z > d, lambda: sn_copy(g, d, 1).wait_send())
        for m in range(tiles_of[g]):
            sf_copy(tile_at[g] + m).wait_send()

    def middle_0():
        u_step(0, 2)
        when(inside, lambda: u_own(1))
        l_fwd(1)

    def middle_1():
        u_step(1, 1, inside)
        l_fwd(2)

    def middle_2():
        u_step(1, 1, at_end)
        u_from_ends(2)
        y_relay(0)

    tb[...] = jnp.zeros(tb.shape, f32)
    l_start(0)
    u_own(0)
    a_load()
    when(at_end, lambda: u_own(1))
    l_fwd(0)
    l_start(1)
    u_step(0, 1)
    when(at_end, lambda: u_own(2))
    l_done(0)
    l_conv(0)
    p_both(0, middle_0)
    pair_add(0, 0)
    pair_add(0, 1)
    l_start(2)
    l_done(1)
    l_conv(1)
    p_both(1, middle_1)
    pair_add(1, 0)
    pair_add(1, 1)
    line_t(0, 1)
    u_step(0, 3)
    u_done(0)
    u_conv(0)
    q_comp(0)
    u_step(1, 2, inside)
    line_t(0, 2)
    when(inside, lambda: u_own(2))
    l_done(2)
    l_conv(2)
    p_both(2, middle_2)
    u_step(1, 2, at_end)
    u_step(1, 3)
    u_done(1)
    u_conv(1)
    y_end(0)
    when(inside, lambda: line_take(0))
    line_t(1, 1)
    q_comp(1)
    pair_add(2, 0)
    pair_add(2, 1)
    u_from_inside(2)
    when(at_end, lambda: line_take(0))
    n_sent(0)
    x_out(0)
    corner_first()
    step_sums(1)
    s_pair(0)
    u_step(2, 2, inside)
    s_add(0)
    y_relay(1)
    line_t(1, 2)
    s_relay(0)
    line_t(2, 1)
    u_step(2, 1, at_end)
    u_step(2, 2, at_end)
    u_step(2, 3)
    u_done(2)
    u_conv(2)
    y_sent(0)
    s_turn(0)
    line_take(1)
    x_out(1)
    y_end(1)
    step_corner(1)
    n_sent(1)
    step_sums(2)
    s_pair(1)
    line_t(2, 2)
    s_add(1)
    q_comp(2, lambda: s_relay(1))
    line_take(2)
    x_out(2)
    step_corner(2)
    p_copy(2, 0).wait_send()
    p_copy(2, 1).wait_send()
    put(keep[0], 2, 0)
    s_pair(2)
    s_line(0, 1)
    s_add(2)
    y_relay(2)
    y_own(2)
    s_turn(1)
    s_line(0, 2)
    s_turn(2)
    s_line(1, 1)
    s_last(0)
    s_line(1, 2)
    s_out(0)
    s_last(1)
    s_last(2)
    y_end(2)
    s_out(1)
    s_out(2)

    for s in range(supers):
        x_leave(s).wait()
        y_leave(s).wait()
        for i in range(6):
            l_copy(s, i).wait_send()
        for zs in range(nz):
            for own in (True, False):
                mine = (z == zs) if own else (z != zs)

                @pl.when(mine)
                def _(s=s, zs=zs, own=own):
                    u_copy(s, zs, 2, own).wait_send()

            when((z >= zs) & has_up, lambda s=s, zs=zs: u_copy(s, zs, 0, False).wait_send())
            when((z <= zs) & has_down, lambda s=s, zs=zs: u_copy(s, zs, 1, False).wait_send())
    n_sent(2)
    y_sent(1)
    y_sent(2)
    s_sent(0)
    s_sent(1)
    s_sent(2)


def part_u_is_half(width, prow, pcol):
    return 2 * (width // pcol) == width // prow and (width // prow) % 48 == 0


def fits(shape):
    supers, width, blk, prow, pcol, rows_here, cols_here, slab = shape
    return (
        supers == 3 and prow == 4 and pcol % 4 == 0 and blk == 128 and width % blk == 0
        and slab % 64 == 0 and width == slab + 64 and slab % 128 == 64
        and rows_here % 640 == 0 and cols_here % 640 == 0
        and width % (8 * pcol) == 0 and width // prow <= 128
        and part_u_is_half(width, prow, pcol) and 3 * width <= (pcol // 2) * slab
    )


def sweep(shape, anc_inverse, lower, upper, lower_edge, upper_edge, diag_inverse, mask):
    supers, width, blk, prow, pcol, rows_here, cols_here, slab = shape
    nz = pcol // 2
    part_u = width // pcol
    sums, sum_tiles = 3 * supers - 2, 2 * supers - 1
    vmem, dma = pltpu.VMEM, pltpu.SemaphoreType.DMA
    in_vmem = pl.BlockSpec(memory_space=pltpu.VMEM)
    in_hbm = pl.BlockSpec(memory_space=pl.ANY)
    out = [
        ((supers, slab, width), in_hbm),
        ((supers, slab, width), in_hbm),
        ((supers, part_u, width // prow), in_vmem),
        ((2, supers - 1, part_u, width // prow), in_vmem),
        ((supers, width, cols_here), in_hbm),
        ((supers, width, rows_here), in_hbm),
    ]
    return pl.pallas_call(
        functools.partial(sweep_kernel, (supers, width, blk, prow, nz, rows_here, cols_here, slab)),
        name="sweep",
        out_shape=[jax.ShapeDtypeStruct(dims, f32) for dims, _ in out],
        in_specs=[in_hbm, in_hbm, in_hbm, in_vmem, in_vmem, in_hbm, pl.BlockSpec(memory_space=pltpu.SMEM)],
        out_specs=[spec for _, spec in out],
        scratch_shapes=[
            vmem((rows_here, cols_here), bf16),
            vmem((rows_here, cols_here), bf16),
            vmem((width, cols_here), bf16),
            vmem((width, cols_here), bf16),
            vmem((width, rows_here), bf16),
            vmem((width, rows_here), bf16),
            vmem((2, width, cols_here // 2), f32),
            vmem(((supers + 1) * nz * slab, width), f32),
            vmem((nz * slab, width), f32),
            vmem((2, nz + 1, slab, width), f32),
            vmem((2, cols_here, width), f32),
            vmem((supers, 6, slab // 2, width), f32),
            vmem((supers, width, width), bf16),
            vmem((supers, width, width), bf16),
            vmem((supers - 1, width, width), bf16),
            vmem((supers - 1, width, width), bf16),
            vmem((width, width), bf16),
            vmem((width, width), bf16),
            vmem((2, width, width), f32),
            vmem((prow * width // (2 * prow), width), f32),
            vmem((6, (sums - 1) * width // (4 * prow), width), f32),
            vmem((prow, width // (2 * prow), width), f32),
            vmem((128, width), f32),
            vmem((nz, sum_tiles * 2 * part_u, 128), f32),
            vmem((nz + 1, sum_tiles * 2 * part_u, 128), f32),
            vmem((sum_tiles, part_u, 128), f32),
            vmem((supers, slab, width), f32),
            vmem((supers, slab, width), f32),
            dma((2 * nz,)),
            dma((2,)),
            dma,
            dma((supers, 6)),
            dma((supers, 6)),
            dma((supers, nz, 3)),
            dma((supers, nz)),
            dma((supers, nz)),
            dma((supers, 2)),
            dma((supers, 2)),
            dma((supers, nz)),
            dma((supers, nz + 1)),
            dma((supers, 6)),
            dma((supers, 6)),
            dma((supers,)),
            dma((supers,)),
            dma((supers, 6)),
            dma((supers, 6)),
            dma((supers, nz)),
            dma((supers, nz + 1)),
            dma((sum_tiles,)),
            dma((sum_tiles,)),
            pltpu.SemaphoreType.REGULAR,
            pltpu.SemaphoreType.REGULAR,
            pltpu.SemaphoreType.REGULAR((supers,)),
            dma((2, supers)),
        ],
        compiler_params=pltpu.CompilerParams(
            collective_id=0, has_side_effects=True, vmem_limit_bytes=67043328
        ),
    )(anc_inverse, lower, upper, lower_edge, upper_edge, diag_inverse, mask)


def place(x, y, corner, cross):
    supers, slab, width = x.shape

    def body(*refs):
        for src, dst in zip(refs[:4], refs[4:]):
            dst[...] = src[...]

    slabs = pl.BlockSpec((1, slab, width), lambda i: (i, 0, 0))

    def whole(array):
        return pl.BlockSpec(array.shape, lambda i: (0,) * array.ndim)

    specs = [slabs, slabs, whole(corner), whole(cross)]
    return pl.pallas_call(
        body,
        name="place",
        grid=(supers,),
        out_shape=[jax.ShapeDtypeStruct(one.shape, f32) for one in (x, y, corner, cross)],
        in_specs=specs,
        out_specs=specs,
    )(x, y, corner, cross)


def per_device(anc_inverse, lower_anc, upper_anc, lower_edge, upper_edge, diag_inverse, tile_mask):
    rows_here, cols_here = anc_inverse.shape
    prow, pcol = lax.axis_size("row"), lax.axis_size("col")
    supers, width = diag_inverse.shape[0], diag_inverse.shape[1]
    blk = width // tile_mask.shape[2]
    shape = (supers, width, blk, prow, pcol, rows_here, cols_here, cols_here // prow)
    args = (anc_inverse, lower_anc, upper_anc, lower_edge, upper_edge, diag_inverse, tile_mask)
    if not fits(shape):
        return general(*args)
    x, y, corner, cross, _, _ = sweep(
        shape,
        anc_inverse,
        jnp.transpose(lower_anc, (1, 2, 0)),
        jnp.transpose(upper_anc, (1, 2, 0)),
        lower_edge,
        upper_edge,
        diag_inverse,
        jnp.transpose(tile_mask, (0, 2, 1)),
    )
    x, y, corner, cross = place(x, y, corner, cross)
    return (
        jnp.transpose(x, (1, 0, 2)),
        jnp.transpose(y, (1, 0, 2))[None, None],
        jnp.transpose(corner, (0, 2, 1)),
        jnp.transpose(cross, (0, 1, 3, 2)),
    )


precise = lax.Precision.HIGH


def contract(left, right, left_dim, right_dim):
    return lax.dot_general(
        left,
        right,
        (((left_dim,), (right_dim,)), ((), ())),
        precision=precise,
        preferred_element_type=jnp.float32,
    )


def row_major(array):
    return with_layout_constraint(array, Layout(major_to_minor=(0, 1)))


def partner(index, step, count):
    if count & (count - 1) == 0:
        return index ^ step
    return (step - index) % count


def exchange(piece_for, axis):
    count = lax.axis_size(axis)
    index = lax.axis_index(axis)
    got = []
    for step in range(count):
        peer = partner(index, step, count)
        piece = piece_for(peer)
        pairs = [(i, partner(i, step, count)) for i in range(count)]
        if any(i != j for i, j in pairs):
            piece = lax.ppermute(piece, axis, pairs)
        got.append((peer, piece))
    return got


def mask_factor(factor, tile_mask, first_row, first_col, blk):
    rows, supers, cols = factor.shape
    blocks = rows // blk
    window = lax.dynamic_slice_in_dim(tile_mask, first_row // blk, blocks, 1).astype(jnp.float32)
    tile_cols = window.shape[2]
    tile_of_col = (first_col + jnp.arange(cols)) // blk
    pick = (tile_of_col[None, :] == jnp.arange(tile_cols)[:, None]).astype(jnp.float32)
    chosen = sum(window[:, :, t, None] * pick[t] for t in range(tile_cols))
    chosen = jnp.transpose(chosen, (1, 0, 2))
    masked = factor.reshape(blocks, blk, supers, cols) * chosen[:, None]
    return jnp.transpose(masked.reshape(rows, supers, cols), (1, 2, 0))


def general(anc_inverse, lower_anc, upper_anc, lower_edge, upper_edge, diag_inverse, tile_mask):
    rows_here, cols_here = anc_inverse.shape
    prow = lax.axis_size("row")
    pcol = lax.axis_size("col")
    supers, width = diag_inverse.shape[0], diag_inverse.shape[1]
    blk = width // tile_mask.shape[2]
    row = lax.axis_index("row")
    col = lax.axis_index("col")
    part_lower = width // prow
    part_upper = width // pcol

    upper_t = mask_factor(upper_anc, tile_mask, row * rows_here, col * part_upper, blk)
    lower_t = mask_factor(lower_anc, tile_mask, col * cols_here, row * part_lower, blk)

    upper_t = lax.all_gather(upper_t, "col", axis=0)
    lower_full = jnp.zeros((supers, prow, part_lower, cols_here), jnp.float32)
    for peer, piece in exchange(lambda _: lower_t, "row"):
        lower_full = lax.dynamic_update_slice(lower_full, piece[:, None], (0, peer, 0, 0))
    lower_full = lower_full.reshape(supers, width, cols_here)
    lower_comb = [-lower_full[0]]
    for s in range(1, supers):
        lower_comb.append(-lower_full[s] - contract(lower_edge[s - 1], lower_comb[-1], 0, 0))
    cols_part = [row_major(contract(anc_inverse, one, 1, 1)) for one in lower_comb]
    cols_mine = [lax.psum_scatter(one, "col", scatter_dimension=0, tiled=True) for one in cols_part]

    upper_full = [upper_t[:, s].reshape(width, rows_here) for s in range(supers)]
    upper_comb = [-upper_full[0]]
    for s in range(1, supers):
        upper_comb.append(-upper_full[s] - contract(upper_edge[s - 1], upper_comb[-1], 1, 0))
    rows_part = [row_major(contract(anc_inverse, one, 0, 1)) for one in upper_comb]

    first = jnp.logical_and(row == 0, col == 0)
    corner = []
    cross_cols = []
    cross_rows = []
    for s in range(supers):
        upper_here = contract(upper_full[s], cols_part[s], 1, 0)
        now = jnp.where(first, diag_inverse[s], 0.0) - upper_here
        if s > 0:
            upper_prev = contract(upper_full[s], cols_part[s - 1], 1, 0)
            lower_prev = lax.dot_general(
                rows_part[s - 1],
                lower_full[s],
                (((0,), (1,)), ((), ())),
                precision=precise,
                preferred_element_type=jnp.float32,
            )
            cross_col = -(lower_prev + contract(corner[-1], lower_edge[s - 1], 1, 0))
            cross_row = -(upper_prev + contract(upper_edge[s - 1], corner[-1], 1, 0))
            now = now - contract(upper_edge[s - 1], cross_col, 1, 0)
            cross_cols.append(cross_col)
            cross_rows.append(cross_row)
        corner.append(now)
    sums = jnp.stack(corner + cross_cols + cross_rows)
    count = sums.shape[0]

    row_slab = cols_here // prow
    rows_mine = [
        sum(
            piece
            for _, piece in exchange(
                lambda peer: lax.dynamic_slice_in_dim(one, peer * row_slab, row_slab, 0), "row"
            )
        )
        for one in rows_part
    ]
    sums, rows_mine = lax.optimization_barrier((sums, rows_mine))
    sums = sum(
        piece
        for _, piece in exchange(
            lambda peer: lax.dynamic_slice_in_dim(sums, peer * part_lower, part_lower, 1), "row"
        )
    )
    sums = jnp.transpose(sums.reshape(count * part_lower, width))
    sums, cols_mine = lax.optimization_barrier((sums, cols_mine))
    sums = lax.psum_scatter(sums, "col", scatter_dimension=0, tiled=True)
    sums = jnp.transpose(sums).reshape(count, part_lower, part_upper)

    x_blocks = jnp.stack(cols_mine, axis=1)
    y_blocks = jnp.stack(rows_mine, axis=1)[None, None]
    z_blocks = sums[:supers]
    cross_blocks = sums[supers:].reshape(2, supers - 1, part_lower, part_upper)
    return (x_blocks, y_blocks, z_blocks, cross_blocks)


def solution(mesh):
    return jax.shard_map(
        per_device,
        mesh=mesh,
        in_specs=(
            P("row", "col"),
            P("col", None, "row"),
            P("row", None, "col"),
            P(),
            P(),
            P(),
            P(),
        ),
        out_specs=(
            P(("row", "col"), None, None),
            P("col", "row", None, None, None),
            P(None, "row", "col"),
            P(None, None, "row", "col"),
        ),
        check_vma=False,
    )
```

```python
import functools

import jax
import jax.numpy as jnp
from jax import lax
from jax.experimental import pallas as pl
from jax.experimental.pallas import tpu as pltpu
from jax.experimental.layout import Layout, with_layout_constraint
from jax.sharding import PartitionSpec as P


f32 = jnp.float32
bf16 = jnp.bfloat16


def halves(value):
    hi = value.astype(bf16)
    return hi, (value - hi.astype(f32)).astype(bf16)


def dot3(left, right, left_dim, right_dim):
    dims = (((left_dim,), (right_dim,)), ((), ()))

    def one(a, b):
        return lax.dot_general(a, b, dims, preferred_element_type=f32)

    return one(left[0], right[0]) + (one(left[0], right[1]) + one(left[1], right[0]))


def sweep_kernel(
    shape,
    a_ref, l_ref, u_ref, e_ref, f_ref, d_ref, mask_ref,
    x_hbm, y_hbm, zo, co, lbuf, ubuf,
    ah, al, lh, ll, uh, ul, stage, pb, pr, ln, qb, yr, uw_h, uw_l, lw_h, lw_l, win_h, win_l, keep,
    sp2, sq, sqd, tb, zb, zl, zf, xo, yo,
    a_sem, st_sem, d_sem, l_send, l_recv, u_send, u_recv, up_recv, p_send, p_recv, n_send, n_recv,
    y_send, y_recv, sp_send, sp_recv, sq_send, sq_recv, sn_send, sn_recv, sf_send, sf_recv,
    free_up, free_down, free_pair, o_sem,
):
    supers, width, blk, prow, nz, rows_here, cols_here, slab = shape
    pcol = 2 * nz
    part_l, part_u = width // prow, width // pcol
    row = lax.axis_index("row")
    col = lax.axis_index("col")
    z, k = col // 2, col % 2
    other = 1 - k
    y, x = row // 2, row % 2
    row_x, row_y, row_d = y * 2 + 1 - x, (1 - y) * 2 + x, (1 - y) * 2 + 1 - x
    to_x, to_y, to_d = {"row": row_x}, {"row": row_y}, {"row": row_d}
    to_pair = {"col": col + 1 - 2 * k}
    up, down = {"col": col + 2}, {"col": col - 2}
    has_up, has_down = z < nz - 1, z > 0
    at_end, inside = (z == 0) | (z == nz - 1), (z > 0) & (z < nz - 1)

    def when(cond, body):
        pl.when(cond)(body)

    def rc(src, dst, ss, rs, dev):
        return pltpu.make_async_remote_copy(
            src_ref=src, dst_ref=dst, send_sem=ss, recv_sem=rs,
            device_id=dev, device_id_type=pl.DeviceIdType.MESH,
        )

    barrier = pltpu.get_barrier_semaphore()

    def greet(dev):
        pl.semaphore_signal(barrier, inc=1, device_id=dev, device_id_type=pl.DeviceIdType.MESH)

    for dev in (to_x, to_y, to_d, to_pair):
        greet(dev)
    for there in range(nz):
        when(z != there, lambda: greet({"col": 2 * there + k}))
    pl.semaphore_wait(barrier, 4 + nz - 1)

    half_l = part_l // 2

    def l_piece(s, r, h):
        return lbuf.at[s, pl.ds(pl.multiple_of(r * part_l + h * half_l, 8), half_l)]

    def l_own(s, h):
        return l_ref.at[s, pl.ds(h * half_l, half_l)]

    def l_copy(s, i):
        src, dst, dev = (
            (l_own(s, 1), l_piece(s, row, 1), to_x),
            (l_own(s, 0), l_piece(s, row, 0), to_y),
            (l_own(s, 0), l_piece(s, row, 0), to_x),
            (l_own(s, 1), l_piece(s, row, 1), to_y),
            (l_piece(s, row_x, 1), l_piece(s, row_x, 1), to_y),
            (l_piece(s, row_y, 0), l_piece(s, row_y, 0), to_x),
        )[i]
        return rc(src, dst, l_send.at[s, i], l_recv.at[s, i], dev)

    def l_take(s, i):
        r, h = ((row_x, 1), (row_y, 0), (row_x, 0), (row_y, 1), (row_d, 1), (row_d, 0))[i]
        rc(l_piece(s, r, h), l_piece(s, r, h), l_send.at[s, i], l_recv.at[s, i], to_pair).wait_recv()

    def l_start(s):
        for i in range(4):
            l_copy(s, i).start()

    def l_fwd(s):
        l_take(s, 0)
        l_copy(s, 4).start()
        l_take(s, 1)
        l_copy(s, 5).start()

    def l_done(s):
        for i in range(2, 6):
            l_take(s, i)

    def u_piece(s, c):
        return ubuf.at[s, pl.ds(pl.multiple_of(c * part_u, 8), part_u)]

    def u_copy(s, zs, way, own):
        mine = u_piece(s, zs * 2 + k)
        src = u_ref.at[s] if own else mine
        recv = up_recv if way == 2 else u_recv
        return rc(src, mine, u_send.at[s, zs, way], recv.at[s, zs], (up, down, to_pair)[way])

    def u_own(s):
        when(has_up, lambda: u_copy(s, z, 0, True).start())
        when(has_down, lambda: u_copy(s, z, 1, True).start())
        u_copy(s, z, 2, True).start()

    def u_low(s, t, cond):
        @pl.when((z >= t) & cond)
        def _():
            u_copy(s, z - t, 1, False).wait_recv()
            when(has_up, lambda: u_copy(s, z - t, 0, False).start())
            u_copy(s, z - t, 2, False).start()

    def u_high(s, t, cond):
        @pl.when((z + t < nz) & cond)
        def _():
            u_copy(s, z + t, 0, False).wait_recv()
            when(has_down, lambda: u_copy(s, z + t, 1, False).start())
            u_copy(s, z + t, 2, False).start()

    def u_step(s, t, cond=None):
        cond = z >= 0 if cond is None else cond
        u_low(s, t, cond)
        u_high(s, t, cond)

    def u_from_ends(s):
        u_low(s, 1, inside & (z == 1))
        u_high(s, 1, inside & (z == nz - 2))

    def u_from_inside(s):
        u_low(s, 1, inside & (z > 1))
        u_high(s, 1, inside & (z < nz - 2))

    def u_done(s):
        for zs in range(nz):
            piece = u_piece(s, zs * 2 + other)
            rc(piece, piece, u_send.at[s, zs, 2], up_recv.at[s, zs], to_pair).wait_recv()

    lanes = stage.shape[2]
    tiles = lanes // blk

    def load(buf, own_ref, s, count, me, part, q):
        here = pl.ds(q * lanes, lanes)

        @pl.loop(0, count)
        def _(p):
            there = stage.at[q % 2, pl.ds(pl.multiple_of(p * part, 8), part)]

            @pl.when(p != me)
            def _():
                pltpu.make_async_copy(
                    buf.at[s, pl.ds(pl.multiple_of(p * part, 8), part), here], there, st_sem.at[q % 2]
                ).start()

            @pl.when(p == me)
            def _():
                pltpu.make_async_copy(own_ref.at[s, :, here], there, st_sem.at[q % 2]).start()

    def convert(buf, own_ref, s, count, me, part, total, first_tile, out_h, out_l):
        load(buf, own_ref, s, count, me, part, 0)
        for q in range(total // lanes):
            if q + 1 < total // lanes:
                load(buf, own_ref, s, count, me, part, q + 1)
            pltpu.make_async_copy(stage.at[q % 2], stage.at[q % 2], st_sem.at[q % 2]).wait()

            @pl.loop(0, tiles)
            def _(t):
                src = pl.ds(pl.multiple_of(t * blk, 128), blk)
                dst = pl.ds(pl.multiple_of(q * lanes + t * blk, 128), blk)
                for j in range(width // blk):
                    keep_it = mask_ref[s, j, first_tile + q * tiles + t].astype(f32)
                    rows = pl.ds(j * blk, blk)
                    hi, lo = halves(stage[q % 2, rows, src] * keep_it)
                    out_h[rows, dst] = hi
                    out_l[rows, dst] = lo

    def window(index):
        start = index * slab
        odd = start % 128
        return pl.ds(pl.multiple_of(start - odd, 128), width), odd

    def l_conv(s):
        convert(lbuf, l_ref, s, prow, row, part_l, cols_here, col * (cols_here // blk), lh, ll)
        if s > 0:
            where, _ = window(row)
            lw_h[s - 1] = lh[:, where]
            lw_l[s - 1] = ll[:, where]

    def u_conv(s):
        convert(ubuf, u_ref, s, pcol, col, part_u, rows_here, row * (rows_here // blk), uh, ul)
        where, _ = window(col)
        uw_h[s] = uh[:, where]
        uw_l[s] = ul[:, where]

    a_lanes = 256
    a_cols = cols_here // a_lanes
    a_slots = 2 * nz

    def a_copy(n, slot):
        i, j = n // a_cols, n % a_cols
        return pltpu.make_async_copy(
            a_ref.at[pl.ds(pl.multiple_of(i * slab, 8), slab), pl.ds(pl.multiple_of(j * a_lanes, 128), a_lanes)],
            pb.at[pl.ds(pl.multiple_of(slot * slab, 64), slab), pl.ds(0, a_lanes)],
            a_sem.at[slot],
        )

    def a_load():
        count = (rows_here // slab) * a_cols
        for n in range(a_slots - 1):
            a_copy(n, n).start()

        @pl.loop(0, count)
        def _(n):
            slot = n % a_slots

            @pl.when(n + a_slots - 1 < count)
            def _():
                a_copy(n + a_slots - 1, (n + a_slots - 1) % a_slots).start()

            a_copy(n, slot).wait()
            i, j = n // a_cols, n % a_cols
            across = pl.ds(pl.multiple_of(j * a_lanes, 128), a_lanes)
            step = 64
            for b in range(slab // step):
                hi, lo = halves(pb[pl.ds(pl.multiple_of(slot * slab + b * step, 64), step), pl.ds(0, a_lanes)])
                down_to = pl.ds(pl.multiple_of(i * slab + b * step, 64), step)
                ah[down_to, across] = hi
                al[down_to, across] = lo

    hz = nz // 2
    h_rows = rows_here // 2

    def far(i):
        flip = (z < hz).astype(jnp.int32)
        return (flip + i) % 2

    def p_rows(s, d, n=1):
        return pl.ds(pl.multiple_of((s * nz + d) * slab, 64), n * slab)

    def p_copy(s, hh):
        return rc(
            pb.at[p_rows(supers, hh * hz, hz)], pr.at[p_rows(0, hh * hz, hz)],
            p_send.at[s, hh], p_recv.at[s, hh], to_pair,
        )

    def p_both(s, middle):
        @pl.loop(0, 2)
        def _(i):
            when(i == 1, middle)
            hh = far(i)
            if s > 0:
                p_copy(s - 1, hh).wait_send()
            rows = pl.ds(pl.multiple_of(hh * h_rows, 128), h_rows)
            got = dot3((lh[...], ll[...]), (ah[rows], al[rows]), 1, 1).T
            for q in range(2 * hz):
                spot = jnp.where(k == q % 2, s, supers)
                pb[p_rows(spot, hh * hz + q // 2)] = got[q * slab : (q + 1) * slab]
            if s > 0:
                when(i == 0, lambda: pl.semaphore_wait(free_pair.at[s - 1], 1))
            p_copy(s, hh).start()

    def n_copy(s, d, way):
        slot = d + 1 - way
        return rc(pb.at[p_rows(s, d)], ln.at[s % 2, slot], n_send.at[s, d], n_recv.at[s, slot], (up, down)[way])

    def n_take(s, d, slot):
        rc(ln.at[s % 2, slot], ln.at[s % 2, slot], n_send.at[s, d], n_recv.at[s, slot], to_pair).wait_recv()
        pb[p_rows(s, d)] = pb[p_rows(s, d)] + ln[s % 2, slot]

    def tell(sem, dev):
        pl.semaphore_signal(sem, inc=1, device_id=dev, device_id_type=pl.DeviceIdType.MESH)

    def line_wait():
        when(has_up, lambda: pl.semaphore_wait(free_up, 1))
        when(has_down, lambda: pl.semaphore_wait(free_down, 1))

    def pair_add(s, i):
        if s == 2 and i == 0:
            when(at_end, line_wait)
        hh = far(i)
        p_copy(s, hh).wait_recv()
        for q in range(hz):
            d = hh * hz + q
            pb[p_rows(s, d)] = pb[p_rows(s, d)] + pr[p_rows(0, d)]
        if i == 1:
            tell(free_pair.at[s], to_pair)
        lo, hi = (1 - i) * hz, (2 - i) * hz

        @pl.when(z == 0)
        def _():
            for d in reversed(range(max(lo, 1), hi)):
                n_copy(s, d, 0).start()

        lo, hi = i * hz, (i + 1) * hz

        @pl.when(z == nz - 1)
        def _():
            for d in range(lo, min(hi, nz - 1)):
                n_copy(s, d, 1).start()

    def line_t(s, t):
        zb_ = nz - 1 - z
        if s == 2 and t == 1:
            when(inside, line_wait)

        @pl.when((z >= 1) & (z <= t))
        def _():
            d = z + (nz - 1 - t)
            n_take(s, d, d + 1)
            n_copy(s, d, 0).start()

        @pl.when((zb_ >= 1) & (zb_ <= t))
        def _():
            d = z - (nz - 1 - t)
            n_take(s, d, d)
            n_copy(s, d, 1).start()

    def line_take(s):
        when(has_down, lambda: n_take(s, z, z + 1))
        when(has_up, lambda: n_take(s, z, z))
        if s == 0:
            when(has_down, lambda: tell(free_up, down))
            when(has_up, lambda: tell(free_down, up))

    def x_leave(s):
        return pltpu.make_async_copy(xo.at[s], x_hbm.at[s], o_sem.at[0, s])

    def y_leave(s):
        return pltpu.make_async_copy(yo.at[s], y_hbm.at[s], o_sem.at[1, s])

    def x_out(s):
        total = -pb[p_rows(s, z)]
        if s > 0:
            total = total - dot3(halves(xo[s - 1]), halves(e_ref[s - 1]), 1, 0)
        xo[s] = total
        x_leave(s).start()

    def n_sent(s):
        for d in range(nz):
            when(z < d, lambda d=d: n_copy(s, d, 0).wait_send())
            when(z > d, lambda d=d: n_copy(s, d, 1).wait_send())

    half_y = slab // 2
    q_cols = 256

    def q_rows(r, h):
        return pl.ds(pl.multiple_of(r * slab + h * half_y, 8), half_y)

    def q_slab(s, r, h):
        return qb.at[s % 2, q_rows(r, h)]

    def y_copy(s, i):
        src, dev = (
            (q_slab(s, row_x, 0), to_x),
            (q_slab(s, row_d, 0), to_x),
            (q_slab(s, row_y, 1), to_y),
            (q_slab(s, row_d, 1), to_y),
            (q_slab(s, row_y, 0), to_y),
            (q_slab(s, row_x, 1), to_x),
        )[i]
        return rc(src, yr.at[s, i], y_send.at[s, i], y_recv.at[s, i], dev)

    def q_comp(s, late=None):
        count = cols_here // q_cols

        @pl.loop(0, count)
        def _(i):
            @pl.when(i == 2)
            def _():
                y_copy(s, 1).start()
                y_copy(s, 3).start()

            if late is not None:
                when(i == count - 1, late)
            across = pl.ds(pl.multiple_of((row_d + i) % count * q_cols, 128), q_cols)
            got = dot3((uh[...], ul[...]), (ah[:, across], al[:, across]), 1, 0)
            qb[s % 2, across] = got.T

        if late is None:
            y_own(s)

    def y_own(s):
        y_copy(s, 0).start()
        y_copy(s, 2).start()

    def y_relay(s):
        y_copy(s, 1).wait_recv()
        qb[s % 2, q_rows(row_y, 0)] = qb[s % 2, q_rows(row_y, 0)] + yr[s, 1]
        y_copy(s, 4).start()
        y_copy(s, 3).wait_recv()
        qb[s % 2, q_rows(row_x, 1)] = qb[s % 2, q_rows(row_x, 1)] + yr[s, 3]
        y_copy(s, 5).start()

    def y_end(s):
        for i in (0, 2, 4, 5):
            y_copy(s, i).wait_recv()
        for h, (i, j) in enumerate(((0, 4), (2, 5))):
            yo[s, pl.ds(h * half_y, half_y)] = -(qb[s % 2, q_rows(row, h)] + yr[s, i] + yr[s, j])
        if s > 0:
            yo[s] = yo[s] - dot3(halves(yo[s - 1]), halves(f_ref[s - 1]), 1, 1)
        y_leave(s).start()

    def y_sent(s):
        for i in range(6):
            y_copy(s, i).wait_send()

    first = ((row == 0) & (col == 0)).astype(f32)

    def fill(value, index):
        _, odd = window(index)
        hi, lo = halves(value)
        win_h[...] = jnp.zeros(win_h.shape, bf16)
        win_l[...] = jnp.zeros(win_l.shape, bf16)
        rows = pl.ds(pl.multiple_of(odd, 64), slab)
        win_h[rows] = hi
        win_l[rows] = lo

    def with_upper(s):
        return dot3((uw_h[s], uw_l[s]), (win_h[...], win_l[...]), 1, 0)

    def d_copy(s):
        return pltpu.make_async_copy(d_ref.at[s], keep.at[0], d_sem)

    def put(value, g, i):
        n = groups[g]
        for r in range(prow):
            for h in range(2):
                at = base(g) + ((h * prow + r) * n + i) * half_l
                pb[pl.ds(at, half_l)] = value[r * part_l + h * half_l : r * part_l + (h + 1) * half_l]

    groups = (3, 3, 1)

    def base(g):
        return (0, nz * slab, supers * nz * slab)[g]

    def corner_first():
        d_copy(0).start()
        fill(xo[0], col)
        got = with_upper(0)
        d_copy(0).wait()
        keep[0] = keep[0] * first - got

    def step_sums(s):
        edge_f = halves(f_ref[s - 1])
        corner = keep[0]
        put(corner, s - 1, 0)
        corner = halves(corner)
        fill(xo[s - 1], col)
        put(-(with_upper(s) + dot3(edge_f, corner, 1, 0)), s - 1, 2)
        fill(yo[s - 1], row)
        turned = dot3((lw_h[s - 1], lw_l[s - 1]), (win_h[...], win_l[...]), 1, 0)
        keep[1] = -(turned.T + dot3(corner, halves(e_ref[s - 1]), 1, 0))
        put(keep[1], s - 1, 1)

    def step_corner(s):
        d_copy(s).start()
        fill(xo[s], col)
        got = with_upper(s) + dot3(halves(f_ref[s - 1]), halves(keep[1]), 1, 0)
        d_copy(s).wait()
        keep[0] = keep[0] * first - got

    def s_rows(g, h, r=0, a=0, count=None):
        n = groups[g]
        at = base(g) + (h * prow + r) * n * half_l + a * n * half_l // 2
        return pl.ds(pl.multiple_of(at, 8), count or n * half_l // 2)

    def sp_copy(g):
        size = prow * groups[g] * half_l
        into = sp2 if g == 2 else pr.at[pl.ds(g * size, size)]
        return rc(pb.at[s_rows(g, other, count=size)], into, sp_send.at[g], sp_recv.at[g], to_pair)

    def s_pair(g):
        if g == 0:
            pl.semaphore_wait(free_pair.at[supers - 1], 1)
        sp_copy(g).start()

    def sq_copy(g, i):
        size = groups[g] * half_l // 2
        r, a, dev = (
            (row_x, 0, to_x), (row_d, 0, to_x), (row_y, 1, to_y), (row_d, 1, to_y), (row_y, 0, to_y), (row_x, 1, to_x),
        )[i]
        into = sq.at[i, pl.ds(sum(groups[:g]) * half_l // 2, size)]
        return rc(pb.at[s_rows(g, k, r, a)], into, sq_send.at[g, i], sq_recv.at[g, i], dev)

    def sq_got(g, i):
        return sq[i, pl.ds(sum(groups[:g]) * half_l // 2, groups[g] * half_l // 2)]

    def sd_copy(r, me, dev):
        return rc(
            pb.at[s_rows(2, k, r, 0, groups[2] * half_l)], sqd.at[me], sq_send.at[2, r], sq_recv.at[2, me], dev
        )

    rows_to = ((row_x, to_x), (row_y, to_y), (row_d, to_d))

    def s_add(g):
        size = prow * groups[g] * half_l
        sp_copy(g).wait_recv()
        mine = s_rows(g, k, count=size)
        pb[mine] = pb[mine] + (sp2[...] if g == 2 else pr[pl.ds(g * size, size)])
        if g == 2:
            for r, dev in rows_to:
                sd_copy(r, row, dev).start()
        else:
            for i in (1, 3, 0, 2):
                sq_copy(g, i).start()

    def s_relay(g):
        for i, r, a, j in ((1, row_y, 0, 4), (3, row_x, 1, 5)):
            sq_copy(g, i).wait_recv()
            there = s_rows(g, k, r, a)
            pb[there] = pb[there] + sq_got(g, i)
            sq_copy(g, j).start()

    def z_rows(g):
        return pl.ds(sum(groups[:g]) * half_l, groups[g] * half_l)

    def sn_copy(g, d, way):
        slot = d + 1 - way
        return rc(
            zb.at[d, z_rows(g)], zl.at[slot, z_rows(g)], sn_send.at[g, d], sn_recv.at[g, slot], (up, down)[way]
        )

    def sz_copy(d):
        rows = z_rows(2)
        return rc(zb.at[d, rows], zl.at[z, rows], sn_send.at[2, d], sn_recv.at[2, z], {"col": 2 * d + k})

    def s_turn(g):
        n = groups[g]
        if g == 2:
            there = s_rows(2, k, row, 0, n * half_l)
            for r, dev in rows_to:
                sd_copy(r, r, dev).wait_recv()
            pb[there] = (pb[there] + sqd[row_x]) + (sqd[row_y] + sqd[row_d])
        else:
            for i in (0, 2, 4, 5):
                sq_copy(g, i).wait_recv()
            for a, (i, j) in enumerate(((0, 4), (2, 5))):
                there = s_rows(g, k, row, a)
                pb[there] = pb[there] + sq_got(g, i) + sq_got(g, j)
        at = base(g) + (k * prow + row) * n * half_l
        total = pb[pl.ds(pl.multiple_of(at, 8), n * half_l)]
        wide = 2 * part_u
        for d in range(nz):
            turned = total if d == 0 else pltpu.roll(total, width - d * wide, 1)
            zb[d, z_rows(g)] = turned[:, :128]
        if g == 2:
            for d in range(nz):
                when(z != d, lambda: sz_copy(d).start())
            return

        @pl.when(z == 0)
        def _():
            for d in reversed(range(1, nz)):
                sn_copy(g, d, 0).start()

        @pl.when(z == nz - 1)
        def _():
            for d in range(nz - 1):
                sn_copy(g, d, 1).start()

    def s_take(g, d, slot):
        rows = z_rows(g)
        rc(zl.at[slot, rows], zl.at[slot, rows], sn_send.at[g, d], sn_recv.at[g, slot], to_pair).wait_recv()
        zb[d, rows] = zb[d, rows] + zl[slot, rows]

    def s_line(g, t):
        zb_ = nz - 1 - z

        @pl.when((z >= 1) & (z <= t))
        def _():
            d = z + (nz - 1 - t)
            s_take(g, d, d + 1)
            sn_copy(g, d, 0).start()

        @pl.when((zb_ >= 1) & (zb_ <= t))
        def _():
            d = z - (nz - 1 - t)
            s_take(g, d, d)
            sn_copy(g, d, 1).start()

    def sf_copy(g):
        return rc(zb.at[z, z_rows(g)], zf.at[z_rows(g)], sf_send.at[g], sf_recv.at[g], to_pair)

    def s_last(g):
        if g == 2:
            for there in range(nz):
                when(z != there, lambda: s_take(g, z, there))
        else:
            when(has_down, lambda: s_take(g, z, z + 1))
            when(has_up, lambda: s_take(g, z, z))
        sf_copy(g).start()

    def s_out(g):
        sf_copy(g).wait_recv()
        mine, theirs = zb[z, z_rows(g)], zf[z_rows(g)]
        for h, both in enumerate((jnp.where(k == 0, mine, theirs), jnp.where(k == 0, theirs, mine))):
            both = jnp.where(k == 0, both, pltpu.roll(both, 128 - part_u, 1))
            for i in range(groups[g]):
                tb[i, pl.ds(h * half_l, half_l)] = both[i * half_l : (i + 1) * half_l]
        for i in range(groups[g]):
            value = tb[i].T[:part_u, :part_l]
            if i == 0:
                zo[g] = value
            else:
                co[i - 1, g] = value

    def s_sent(g):
        sp_copy(g).wait_send()
        if g == 2:
            for r, dev in rows_to:
                sd_copy(r, row, dev).wait_send()
            for d in range(nz):
                when(z != d, lambda: sz_copy(d).wait_send())
        else:
            for i in range(6):
                sq_copy(g, i).wait_send()
            for d in range(nz):
                when(z < d, lambda: sn_copy(g, d, 0).wait_send())
                when(z > d, lambda: sn_copy(g, d, 1).wait_send())
        sf_copy(g).wait_send()

    def middle_0():
        u_step(1, 1, inside)
        l_fwd(1)

    def middle_1():
        when(inside, lambda: u_own(2))
        l_fwd(2)

    def middle_2():
        u_step(0, 2, at_end)

    tb[...] = jnp.zeros(tb.shape, f32)
    l_start(0)
    u_own(0)
    a_load()
    u_own(1)
    l_fwd(0)
    l_start(1)
    u_step(0, 1)
    when(at_end, lambda: u_own(2))
    l_done(0)
    l_conv(0)
    p_both(0, middle_0)
    pair_add(0, 0)
    pair_add(0, 1)
    l_start(2)
    l_done(1)
    l_conv(1)
    u_step(0, 2, inside)
    p_both(1, middle_1)
    pair_add(1, 0)
    pair_add(1, 1)
    line_t(0, 1)
    u_step(1, 2, inside)
    l_done(2)
    l_conv(2)
    p_both(2, middle_2)
    u_from_ends(2)
    u_step(0, 3)
    u_done(0)
    u_conv(0)
    q_comp(0)
    line_t(0, 2)
    u_from_inside(2)
    u_step(1, 1, at_end)
    u_step(1, 2, at_end)
    u_step(1, 3)
    u_done(1)
    u_conv(1)
    y_relay(0)
    line_t(1, 1)
    q_comp(1)
    when(inside, lambda: line_take(0))
    u_step(2, 2, inside)
    pair_add(2, 0)
    pair_add(2, 1)
    when(at_end, lambda: line_take(0))
    n_sent(0)
    x_out(0)
    y_end(0)
    corner_first()
    step_sums(1)
    s_pair(0)
    y_relay(1)
    s_add(0)
    line_t(1, 2)
    s_relay(0)
    u_step(2, 1, at_end)
    u_step(2, 2, at_end)
    u_step(2, 3)
    u_done(2)
    u_conv(2)
    y_sent(0)
    line_t(2, 1)
    s_turn(0)
    line_take(1)
    x_out(1)
    y_end(1)
    step_corner(1)
    n_sent(1)
    step_sums(2)
    s_pair(1)
    line_t(2, 2)
    s_add(1)
    q_comp(2, lambda: s_relay(1))
    line_take(2)
    x_out(2)
    step_corner(2)
    p_copy(2, 0).wait_send()
    p_copy(2, 1).wait_send()
    put(keep[0], 2, 0)
    s_pair(2)
    s_line(0, 1)
    s_add(2)
    y_relay(2)
    y_own(2)
    s_turn(1)
    s_line(0, 2)
    s_turn(2)
    s_line(1, 1)
    s_last(0)
    s_line(1, 2)
    s_out(0)
    s_last(1)
    s_last(2)
    y_end(2)
    s_out(1)
    s_out(2)

    for s in range(supers):
        x_leave(s).wait()
        y_leave(s).wait()
        for i in range(6):
            l_copy(s, i).wait_send()
        for zs in range(nz):
            for own in (True, False):
                mine = (z == zs) if own else (z != zs)

                @pl.when(mine)
                def _(s=s, zs=zs, own=own):
                    u_copy(s, zs, 2, own).wait_send()

            when((z >= zs) & has_up, lambda s=s, zs=zs: u_copy(s, zs, 0, False).wait_send())
            when((z <= zs) & has_down, lambda s=s, zs=zs: u_copy(s, zs, 1, False).wait_send())
    n_sent(2)
    y_sent(1)
    y_sent(2)
    s_sent(0)
    s_sent(1)
    s_sent(2)


def part_u_is_half(width, prow, pcol):
    return 2 * (width // pcol) == width // prow and (width // prow) % 48 == 0


def fits(shape):
    supers, width, blk, prow, pcol, rows_here, cols_here, slab = shape
    return (
        supers == 3 and prow == 4 and pcol % 4 == 0 and blk == 128 and width % blk == 0
        and slab % 64 == 0 and width == slab + 64 and slab % 128 == 64
        and rows_here % 640 == 0 and cols_here % 640 == 0
        and width % (8 * pcol) == 0 and width // prow <= 128
        and part_u_is_half(width, prow, pcol) and 3 * width <= (pcol // 2) * slab
    )


def sweep(shape, anc_inverse, lower, upper, lower_edge, upper_edge, diag_inverse, mask):
    supers, width, blk, prow, pcol, rows_here, cols_here, slab = shape
    nz = pcol // 2
    part_u = width // pcol
    sums = 3 * supers - 2
    vmem, dma = pltpu.VMEM, pltpu.SemaphoreType.DMA
    in_vmem = pl.BlockSpec(memory_space=pltpu.VMEM)
    in_hbm = pl.BlockSpec(memory_space=pl.ANY)
    out = [
        ((supers, slab, width), in_hbm),
        ((supers, slab, width), in_hbm),
        ((supers, part_u, width // prow), in_vmem),
        ((2, supers - 1, part_u, width // prow), in_vmem),
        ((supers, width, cols_here), in_hbm),
        ((supers, width, rows_here), in_hbm),
    ]
    return pl.pallas_call(
        functools.partial(sweep_kernel, (supers, width, blk, prow, nz, rows_here, cols_here, slab)),
        name="sweep",
        out_shape=[jax.ShapeDtypeStruct(dims, f32) for dims, _ in out],
        in_specs=[in_hbm, in_hbm, in_hbm, in_vmem, in_vmem, in_hbm, pl.BlockSpec(memory_space=pltpu.SMEM)],
        out_specs=[spec for _, spec in out],
        scratch_shapes=[
            vmem((rows_here, cols_here), bf16),
            vmem((rows_here, cols_here), bf16),
            vmem((width, cols_here), bf16),
            vmem((width, cols_here), bf16),
            vmem((width, rows_here), bf16),
            vmem((width, rows_here), bf16),
            vmem((2, width, cols_here // 2), f32),
            vmem(((supers + 1) * nz * slab, width), f32),
            vmem((nz * slab, width), f32),
            vmem((2, nz + 1, slab, width), f32),
            vmem((2, cols_here, width), f32),
            vmem((supers, 6, slab // 2, width), f32),
            vmem((supers, width, width), bf16),
            vmem((supers, width, width), bf16),
            vmem((supers - 1, width, width), bf16),
            vmem((supers - 1, width, width), bf16),
            vmem((width, width), bf16),
            vmem((width, width), bf16),
            vmem((2, width, width), f32),
            vmem((prow * width // (2 * prow), width), f32),
            vmem((6, (sums - 1) * width // (4 * prow), width), f32),
            vmem((prow, width // (2 * prow), width), f32),
            vmem((supers, 128, 128), f32),
            vmem((nz, sums * part_u, 128), f32),
            vmem((nz + 1, sums * part_u, 128), f32),
            vmem((sums * part_u, 128), f32),
            vmem((supers, slab, width), f32),
            vmem((supers, slab, width), f32),
            dma((2 * nz,)),
            dma((2,)),
            dma,
            dma((supers, 6)),
            dma((supers, 6)),
            dma((supers, nz, 3)),
            dma((supers, nz)),
            dma((supers, nz)),
            dma((supers, 2)),
            dma((supers, 2)),
            dma((supers, nz)),
            dma((supers, nz + 1)),
            dma((supers, 6)),
            dma((supers, 6)),
            dma((supers,)),
            dma((supers,)),
            dma((supers, 6)),
            dma((supers, 6)),
            dma((supers, nz)),
            dma((supers, nz + 1)),
            dma((supers,)),
            dma((supers,)),
            pltpu.SemaphoreType.REGULAR,
            pltpu.SemaphoreType.REGULAR,
            pltpu.SemaphoreType.REGULAR((supers,)),
            dma((2, supers)),
        ],
        compiler_params=pltpu.CompilerParams(
            collective_id=0, has_side_effects=True, vmem_limit_bytes=67043328
        ),
    )(anc_inverse, lower, upper, lower_edge, upper_edge, diag_inverse, mask)


def place(x, y, corner, cross):
    arrays = (x, y, corner, cross)
    pieces = [(a, i) for a, array in enumerate(arrays[:2]) for i in range(array.shape[0])] + [(2, None), (3, None)]

    def body(*refs):
        srcs, dsts, kept, (get, put) = refs[:4], refs[4:8], refs[8:12], refs[12:]

        def view(ref, i):
            return ref if i is None else ref.at[i]

        def copies(n):
            a, i = pieces[n]
            src, mid, dst = (view(r[a], i) for r in (srcs, kept, dsts))
            return pltpu.make_async_copy(src, mid, get.at[n]), pltpu.make_async_copy(mid, dst, put.at[n])

        for n in range(len(pieces)):
            copies(n)[0].start()
        for n in range(len(pieces)):
            copies(n)[0].wait()
            copies(n)[1].start()
        for n in range(len(pieces)):
            copies(n)[1].wait()

    return pl.pallas_call(
        body,
        name="place",
        out_shape=[jax.ShapeDtypeStruct(one.shape, f32) for one in arrays],
        in_specs=[pl.BlockSpec(memory_space=pl.ANY)] * 4,
        out_specs=[pl.BlockSpec(memory_space=pl.ANY)] * 4,
        scratch_shapes=[pltpu.VMEM(one.shape, f32) for one in arrays]
        + [pltpu.SemaphoreType.DMA((len(pieces),))] * 2,
    )(*arrays)


def per_device(anc_inverse, lower_anc, upper_anc, lower_edge, upper_edge, diag_inverse, tile_mask):
    rows_here, cols_here = anc_inverse.shape
    prow, pcol = lax.axis_size("row"), lax.axis_size("col")
    supers, width = diag_inverse.shape[0], diag_inverse.shape[1]
    blk = width // tile_mask.shape[2]
    shape = (supers, width, blk, prow, pcol, rows_here, cols_here, cols_here // prow)
    args = (anc_inverse, lower_anc, upper_anc, lower_edge, upper_edge, diag_inverse, tile_mask)
    if not fits(shape):
        return general(*args)
    x, y, corner, cross, _, _ = sweep(
        shape,
        anc_inverse,
        jnp.transpose(lower_anc, (1, 2, 0)),
        jnp.transpose(upper_anc, (1, 2, 0)),
        lower_edge,
        upper_edge,
        diag_inverse,
        jnp.transpose(tile_mask, (0, 2, 1)),
    )
    x, y, corner, cross = place(x, y, corner, cross)
    return (
        jnp.transpose(x, (1, 0, 2)),
        jnp.transpose(y, (1, 0, 2))[None, None],
        jnp.transpose(corner, (0, 2, 1)),
        jnp.transpose(cross, (0, 1, 3, 2)),
    )


precise = lax.Precision.HIGH


def contract(left, right, left_dim, right_dim):
    return lax.dot_general(
        left,
        right,
        (((left_dim,), (right_dim,)), ((), ())),
        precision=precise,
        preferred_element_type=jnp.float32,
    )


def row_major(array):
    return with_layout_constraint(array, Layout(major_to_minor=(0, 1)))


def partner(index, step, count):
    if count & (count - 1) == 0:
        return index ^ step
    return (step - index) % count


def exchange(piece_for, axis):
    count = lax.axis_size(axis)
    index = lax.axis_index(axis)
    got = []
    for step in range(count):
        peer = partner(index, step, count)
        piece = piece_for(peer)
        pairs = [(i, partner(i, step, count)) for i in range(count)]
        if any(i != j for i, j in pairs):
            piece = lax.ppermute(piece, axis, pairs)
        got.append((peer, piece))
    return got


def mask_factor(factor, tile_mask, first_row, first_col, blk):
    rows, supers, cols = factor.shape
    blocks = rows // blk
    window = lax.dynamic_slice_in_dim(tile_mask, first_row // blk, blocks, 1).astype(jnp.float32)
    tile_cols = window.shape[2]
    tile_of_col = (first_col + jnp.arange(cols)) // blk
    pick = (tile_of_col[None, :] == jnp.arange(tile_cols)[:, None]).astype(jnp.float32)
    chosen = sum(window[:, :, t, None] * pick[t] for t in range(tile_cols))
    chosen = jnp.transpose(chosen, (1, 0, 2))
    masked = factor.reshape(blocks, blk, supers, cols) * chosen[:, None]
    return jnp.transpose(masked.reshape(rows, supers, cols), (1, 2, 0))


def general(anc_inverse, lower_anc, upper_anc, lower_edge, upper_edge, diag_inverse, tile_mask):
    rows_here, cols_here = anc_inverse.shape
    prow = lax.axis_size("row")
    pcol = lax.axis_size("col")
    supers, width = diag_inverse.shape[0], diag_inverse.shape[1]
    blk = width // tile_mask.shape[2]
    row = lax.axis_index("row")
    col = lax.axis_index("col")
    part_lower = width // prow
    part_upper = width // pcol

    upper_t = mask_factor(upper_anc, tile_mask, row * rows_here, col * part_upper, blk)
    lower_t = mask_factor(lower_anc, tile_mask, col * cols_here, row * part_lower, blk)

    upper_t = lax.all_gather(upper_t, "col", axis=0)
    lower_full = jnp.zeros((supers, prow, part_lower, cols_here), jnp.float32)
    for peer, piece in exchange(lambda _: lower_t, "row"):
        lower_full = lax.dynamic_update_slice(lower_full, piece[:, None], (0, peer, 0, 0))
    lower_full = lower_full.reshape(supers, width, cols_here)
    lower_comb = [-lower_full[0]]
    for s in range(1, supers):
        lower_comb.append(-lower_full[s] - contract(lower_edge[s - 1], lower_comb[-1], 0, 0))
    cols_part = [row_major(contract(anc_inverse, one, 1, 1)) for one in lower_comb]
    cols_mine = [lax.psum_scatter(one, "col", scatter_dimension=0, tiled=True) for one in cols_part]

    upper_full = [upper_t[:, s].reshape(width, rows_here) for s in range(supers)]
    upper_comb = [-upper_full[0]]
    for s in range(1, supers):
        upper_comb.append(-upper_full[s] - contract(upper_edge[s - 1], upper_comb[-1], 1, 0))
    rows_part = [row_major(contract(anc_inverse, one, 0, 1)) for one in upper_comb]

    first = jnp.logical_and(row == 0, col == 0)
    corner = []
    cross_cols = []
    cross_rows = []
    for s in range(supers):
        upper_here = contract(upper_full[s], cols_part[s], 1, 0)
        now = jnp.where(first, diag_inverse[s], 0.0) - upper_here
        if s > 0:
            upper_prev = contract(upper_full[s], cols_part[s - 1], 1, 0)
            lower_prev = lax.dot_general(
                rows_part[s - 1],
                lower_full[s],
                (((0,), (1,)), ((), ())),
                precision=precise,
                preferred_element_type=jnp.float32,
            )
            cross_col = -(lower_prev + contract(corner[-1], lower_edge[s - 1], 1, 0))
            cross_row = -(upper_prev + contract(upper_edge[s - 1], corner[-1], 1, 0))
            now = now - contract(upper_edge[s - 1], cross_col, 1, 0)
            cross_cols.append(cross_col)
            cross_rows.append(cross_row)
        corner.append(now)
    sums = jnp.stack(corner + cross_cols + cross_rows)
    count = sums.shape[0]

    row_slab = cols_here // prow
    rows_mine = [
        sum(
            piece
            for _, piece in exchange(
                lambda peer: lax.dynamic_slice_in_dim(one, peer * row_slab, row_slab, 0), "row"
            )
        )
        for one in rows_part
    ]
    sums, rows_mine = lax.optimization_barrier((sums, rows_mine))
    sums = sum(
        piece
        for _, piece in exchange(
            lambda peer: lax.dynamic_slice_in_dim(sums, peer * part_lower, part_lower, 1), "row"
        )
    )
    sums = jnp.transpose(sums.reshape(count * part_lower, width))
    sums, cols_mine = lax.optimization_barrier((sums, cols_mine))
    sums = lax.psum_scatter(sums, "col", scatter_dimension=0, tiled=True)
    sums = jnp.transpose(sums).reshape(count, part_lower, part_upper)

    x_blocks = jnp.stack(cols_mine, axis=1)
    y_blocks = jnp.stack(rows_mine, axis=1)[None, None]
    z_blocks = sums[:supers]
    cross_blocks = sums[supers:].reshape(2, supers - 1, part_lower, part_upper)
    return (x_blocks, y_blocks, z_blocks, cross_blocks)


def solution(mesh):
    return jax.shard_map(
        per_device,
        mesh=mesh,
        in_specs=(
            P("row", "col"),
            P("col", None, "row"),
            P("row", None, "col"),
            P(),
            P(),
            P(),
            P(),
        ),
        out_specs=(
            P(("row", "col"), None, None),
            P("col", "row", None, None, None),
            P(None, "row", "col"),
            P(None, None, "row", "col"),
        ),
        check_vma=False,
    )
```

```python
import functools

import jax
import jax.numpy as jnp
from jax import lax
from jax.experimental import pallas as pl
from jax.experimental.pallas import tpu as pltpu
from jax.experimental.layout import Layout, with_layout_constraint
from jax.sharding import PartitionSpec as P


f32 = jnp.float32
bf16 = jnp.bfloat16


def halves(value):
    hi = value.astype(bf16)
    return hi, (value - hi.astype(f32)).astype(bf16)


def dot3(left, right, left_dim, right_dim):
    dims = (((left_dim,), (right_dim,)), ((), ()))

    def one(a, b):
        return lax.dot_general(a, b, dims, preferred_element_type=f32)

    return one(left[0], right[0]) + (one(left[0], right[1]) + one(left[1], right[0]))


def sweep_kernel(
    shape,
    a_ref, l_ref, u_ref, e_ref, f_ref, d_ref, mask_ref,
    x_hbm, y_hbm, zo, co, lbuf, ubuf,
    ah, al, lh, ll, uh, ul, stage, pb, pr, ln, qb, yr, uw_h, uw_l, lw_h, lw_l, win_h, win_l, keep,
    sp2, sq, sqd, tb, zb, zl, zf, xo, yo,
    a_sem, st_sem, d_sem, l_send, l_recv, u_send, u_recv, up_recv, p_send, p_recv, n_send, n_recv,
    y_send, y_recv, sp_send, sp_recv, sq_send, sq_recv, sn_send, sn_recv, sf_send, sf_recv,
    free_up, free_down, free_pair, o_sem,
):
    supers, width, blk, prow, nz, rows_here, cols_here, slab = shape
    pcol = 2 * nz
    part_l, part_u = width // prow, width // pcol
    row = lax.axis_index("row")
    col = lax.axis_index("col")
    z, k = col // 2, col % 2
    other = 1 - k
    y, x = row // 2, row % 2
    row_x, row_y, row_d = y * 2 + 1 - x, (1 - y) * 2 + x, (1 - y) * 2 + 1 - x
    to_x, to_y, to_d = {"row": row_x}, {"row": row_y}, {"row": row_d}
    to_pair = {"col": col + 1 - 2 * k}
    up, down = {"col": col + 2}, {"col": col - 2}
    has_up, has_down = z < nz - 1, z > 0
    at_end, inside = (z == 0) | (z == nz - 1), (z > 0) & (z < nz - 1)

    def when(cond, body):
        pl.when(cond)(body)

    def rc(src, dst, ss, rs, dev):
        return pltpu.make_async_remote_copy(
            src_ref=src, dst_ref=dst, send_sem=ss, recv_sem=rs,
            device_id=dev, device_id_type=pl.DeviceIdType.MESH,
        )

    barrier = pltpu.get_barrier_semaphore()

    def greet(dev):
        pl.semaphore_signal(barrier, inc=1, device_id=dev, device_id_type=pl.DeviceIdType.MESH)

    for dev in (to_x, to_y, to_d, to_pair):
        greet(dev)
    for there in range(nz):
        when(z != there, lambda: greet({"col": 2 * there + k}))
    pl.semaphore_wait(barrier, 4 + nz - 1)

    half_l = part_l // 2

    def l_piece(s, r, h):
        return lbuf.at[s, pl.ds(pl.multiple_of(r * part_l + h * half_l, 8), half_l)]

    def l_own(s, h):
        return l_ref.at[s, pl.ds(h * half_l, half_l)]

    def l_copy(s, i):
        src, dst, dev = (
            (l_own(s, 1), l_piece(s, row, 1), to_x),
            (l_own(s, 0), l_piece(s, row, 0), to_y),
            (l_own(s, 0), l_piece(s, row, 0), to_x),
            (l_own(s, 1), l_piece(s, row, 1), to_y),
            (l_piece(s, row_x, 1), l_piece(s, row_x, 1), to_y),
            (l_piece(s, row_y, 0), l_piece(s, row_y, 0), to_x),
        )[i]
        return rc(src, dst, l_send.at[s, i], l_recv.at[s, i], dev)

    def l_take(s, i):
        r, h = ((row_x, 1), (row_y, 0), (row_x, 0), (row_y, 1), (row_d, 1), (row_d, 0))[i]
        rc(l_piece(s, r, h), l_piece(s, r, h), l_send.at[s, i], l_recv.at[s, i], to_pair).wait_recv()

    def l_start(s):
        for i in range(4):
            l_copy(s, i).start()

    def l_fwd(s):
        l_take(s, 0)
        l_copy(s, 4).start()
        l_take(s, 1)
        l_copy(s, 5).start()

    def l_done(s):
        for i in range(2, 6):
            l_take(s, i)

    def u_piece(s, c):
        return ubuf.at[s, pl.ds(pl.multiple_of(c * part_u, 8), part_u)]

    def u_copy(s, zs, way, own):
        mine = u_piece(s, zs * 2 + k)
        src = u_ref.at[s] if own else mine
        recv = up_recv if way == 2 else u_recv
        return rc(src, mine, u_send.at[s, zs, way], recv.at[s, zs], (up, down, to_pair)[way])

    def u_own(s):
        when(has_up, lambda: u_copy(s, z, 0, True).start())
        when(has_down, lambda: u_copy(s, z, 1, True).start())
        u_copy(s, z, 2, True).start()

    def u_low(s, t, cond):
        @pl.when((z >= t) & cond)
        def _():
            u_copy(s, z - t, 1, False).wait_recv()
            when(has_up, lambda: u_copy(s, z - t, 0, False).start())
            u_copy(s, z - t, 2, False).start()

    def u_high(s, t, cond):
        @pl.when((z + t < nz) & cond)
        def _():
            u_copy(s, z + t, 0, False).wait_recv()
            when(has_down, lambda: u_copy(s, z + t, 1, False).start())
            u_copy(s, z + t, 2, False).start()

    def u_step(s, t, cond=None):
        cond = z >= 0 if cond is None else cond
        u_low(s, t, cond)
        u_high(s, t, cond)

    def u_from_ends(s):
        u_low(s, 1, inside & (z == 1))
        u_high(s, 1, inside & (z == nz - 2))

    def u_from_inside(s):
        u_low(s, 1, inside & (z > 1))
        u_high(s, 1, inside & (z < nz - 2))

    def u_done(s):
        for zs in range(nz):
            piece = u_piece(s, zs * 2 + other)
            rc(piece, piece, u_send.at[s, zs, 2], up_recv.at[s, zs], to_pair).wait_recv()

    lanes = stage.shape[2]
    tiles = lanes // blk

    def load(buf, own_ref, s, count, me, part, q):
        here = pl.ds(q * lanes, lanes)

        @pl.loop(0, count)
        def _(p):
            there = stage.at[q % 2, pl.ds(pl.multiple_of(p * part, 8), part)]

            @pl.when(p != me)
            def _():
                pltpu.make_async_copy(
                    buf.at[s, pl.ds(pl.multiple_of(p * part, 8), part), here], there, st_sem.at[q % 2]
                ).start()

            @pl.when(p == me)
            def _():
                pltpu.make_async_copy(own_ref.at[s, :, here], there, st_sem.at[q % 2]).start()

    def convert(buf, own_ref, s, count, me, part, total, first_tile, out_h, out_l):
        load(buf, own_ref, s, count, me, part, 0)
        for q in range(total // lanes):
            if q + 1 < total // lanes:
                load(buf, own_ref, s, count, me, part, q + 1)
            pltpu.make_async_copy(stage.at[q % 2], stage.at[q % 2], st_sem.at[q % 2]).wait()

            @pl.loop(0, tiles)
            def _(t):
                src = pl.ds(pl.multiple_of(t * blk, 128), blk)
                dst = pl.ds(pl.multiple_of(q * lanes + t * blk, 128), blk)
                for j in range(width // blk):
                    keep_it = mask_ref[s, j, first_tile + q * tiles + t].astype(f32)
                    rows = pl.ds(j * blk, blk)
                    hi, lo = halves(stage[q % 2, rows, src] * keep_it)
                    out_h[rows, dst] = hi
                    out_l[rows, dst] = lo

    def window(index):
        start = index * slab
        odd = start % 128
        return pl.ds(pl.multiple_of(start - odd, 128), width), odd

    def l_conv(s):
        convert(lbuf, l_ref, s, prow, row, part_l, cols_here, col * (cols_here // blk), lh, ll)
        if s > 0:
            where, _ = window(row)
            lw_h[s - 1] = lh[:, where]
            lw_l[s - 1] = ll[:, where]

    def u_conv(s):
        convert(ubuf, u_ref, s, pcol, col, part_u, rows_here, row * (rows_here // blk), uh, ul)
        where, _ = window(col)
        uw_h[s] = uh[:, where]
        uw_l[s] = ul[:, where]

    a_lanes = 256
    a_cols = cols_here // a_lanes
    a_slots = 2 * nz

    def a_copy(n, slot):
        i, j = n // a_cols, n % a_cols
        return pltpu.make_async_copy(
            a_ref.at[pl.ds(pl.multiple_of(i * slab, 8), slab), pl.ds(pl.multiple_of(j * a_lanes, 128), a_lanes)],
            pb.at[pl.ds(pl.multiple_of(slot * slab, 64), slab), pl.ds(0, a_lanes)],
            a_sem.at[slot],
        )

    def a_load():
        count = (rows_here // slab) * a_cols
        for n in range(a_slots - 1):
            a_copy(n, n).start()

        @pl.loop(0, count)
        def _(n):
            slot = n % a_slots

            @pl.when(n + a_slots - 1 < count)
            def _():
                a_copy(n + a_slots - 1, (n + a_slots - 1) % a_slots).start()

            a_copy(n, slot).wait()
            i, j = n // a_cols, n % a_cols
            across = pl.ds(pl.multiple_of(j * a_lanes, 128), a_lanes)
            step = 64
            for b in range(slab // step):
                hi, lo = halves(pb[pl.ds(pl.multiple_of(slot * slab + b * step, 64), step), pl.ds(0, a_lanes)])
                down_to = pl.ds(pl.multiple_of(i * slab + b * step, 64), step)
                ah[down_to, across] = hi
                al[down_to, across] = lo

    hz = nz // 2
    h_rows = rows_here // 2

    def far(i):
        flip = (z < hz).astype(jnp.int32)
        return (flip + i) % 2

    def p_rows(s, d, n=1):
        return pl.ds(pl.multiple_of((s * nz + d) * slab, 64), n * slab)

    def p_copy(s, hh):
        return rc(
            pb.at[p_rows(supers, hh * hz, hz)], pr.at[p_rows(0, hh * hz, hz)],
            p_send.at[s, hh], p_recv.at[s, hh], to_pair,
        )

    def p_both(s, middle):
        @pl.loop(0, 2)
        def _(i):
            when(i == 1, middle)
            hh = far(i)
            if s > 0:
                p_copy(s - 1, hh).wait_send()
            rows = pl.ds(pl.multiple_of(hh * h_rows, 128), h_rows)
            got = dot3((lh[...], ll[...]), (ah[rows], al[rows]), 1, 1).T
            for q in range(2 * hz):
                spot = jnp.where(k == q % 2, s, supers)
                pb[p_rows(spot, hh * hz + q // 2)] = got[q * slab : (q + 1) * slab]
            if s > 0:
                when(i == 0, lambda: pl.semaphore_wait(free_pair.at[s - 1], 1))
            p_copy(s, hh).start()

    def n_copy(s, d, way):
        slot = d + 1 - way
        return rc(pb.at[p_rows(s, d)], ln.at[s % 2, slot], n_send.at[s, d], n_recv.at[s, slot], (up, down)[way])

    def n_take(s, d, slot):
        rc(ln.at[s % 2, slot], ln.at[s % 2, slot], n_send.at[s, d], n_recv.at[s, slot], to_pair).wait_recv()
        pb[p_rows(s, d)] = pb[p_rows(s, d)] + ln[s % 2, slot]

    def tell(sem, dev):
        pl.semaphore_signal(sem, inc=1, device_id=dev, device_id_type=pl.DeviceIdType.MESH)

    def line_wait():
        when(has_up, lambda: pl.semaphore_wait(free_up, 1))
        when(has_down, lambda: pl.semaphore_wait(free_down, 1))

    def pair_add(s, i):
        if s == 2 and i == 0:
            when(at_end, line_wait)
        hh = far(i)
        p_copy(s, hh).wait_recv()
        for q in range(hz):
            d = hh * hz + q
            pb[p_rows(s, d)] = pb[p_rows(s, d)] + pr[p_rows(0, d)]
        if i == 1:
            tell(free_pair.at[s], to_pair)
        lo, hi = (1 - i) * hz, (2 - i) * hz

        @pl.when(z == 0)
        def _():
            for d in reversed(range(max(lo, 1), hi)):
                n_copy(s, d, 0).start()

        lo, hi = i * hz, (i + 1) * hz

        @pl.when(z == nz - 1)
        def _():
            for d in range(lo, min(hi, nz - 1)):
                n_copy(s, d, 1).start()

    def line_t(s, t):
        zb_ = nz - 1 - z
        if s == 2 and t == 1:
            when(inside, line_wait)

        @pl.when((z >= 1) & (z <= t))
        def _():
            d = z + (nz - 1 - t)
            n_take(s, d, d + 1)
            n_copy(s, d, 0).start()

        @pl.when((zb_ >= 1) & (zb_ <= t))
        def _():
            d = z - (nz - 1 - t)
            n_take(s, d, d)
            n_copy(s, d, 1).start()

    def line_take(s):
        when(has_down, lambda: n_take(s, z, z + 1))
        when(has_up, lambda: n_take(s, z, z))
        if s == 0:
            when(has_down, lambda: tell(free_up, down))
            when(has_up, lambda: tell(free_down, up))

    def x_leave(s):
        return pltpu.make_async_copy(xo.at[s], x_hbm.at[s], o_sem.at[0, s])

    def y_leave(s):
        return pltpu.make_async_copy(yo.at[s], y_hbm.at[s], o_sem.at[1, s])

    def x_out(s):
        total = -pb[p_rows(s, z)]
        if s > 0:
            total = total - dot3(halves(xo[s - 1]), halves(e_ref[s - 1]), 1, 0)
        xo[s] = total
        x_leave(s).start()

    def n_sent(s):
        for d in range(nz):
            when(z < d, lambda d=d: n_copy(s, d, 0).wait_send())
            when(z > d, lambda d=d: n_copy(s, d, 1).wait_send())

    half_y = slab // 2
    q_cols = 256

    def q_rows(r, h):
        return pl.ds(pl.multiple_of(r * slab + h * half_y, 8), half_y)

    def q_slab(s, r, h):
        return qb.at[s % 2, q_rows(r, h)]

    def y_copy(s, i):
        src, dev = (
            (q_slab(s, row_x, 0), to_x),
            (q_slab(s, row_d, 0), to_x),
            (q_slab(s, row_y, 1), to_y),
            (q_slab(s, row_d, 1), to_y),
            (q_slab(s, row_y, 0), to_y),
            (q_slab(s, row_x, 1), to_x),
        )[i]
        return rc(src, yr.at[s, i], y_send.at[s, i], y_recv.at[s, i], dev)

    q_count = cols_here // q_cols

    def q_part(s, start, stop):
        @pl.loop(start, stop)
        def _(i):
            @pl.when(i == 2)
            def _():
                y_copy(s, 1).start()
                y_copy(s, 3).start()

            across = pl.ds(pl.multiple_of((row_d + i) % q_count * q_cols, 128), q_cols)
            got = dot3((uh[...], ul[...]), (ah[:, across], al[:, across]), 1, 0)
            qb[s % 2, across] = got.T

    def y_own(s):
        y_copy(s, 0).start()
        y_copy(s, 2).start()

    def q_comp(s):
        q_part(s, 0, q_count)
        y_own(s)

    def y_relay(s):
        y_copy(s, 1).wait_recv()
        qb[s % 2, q_rows(row_y, 0)] = qb[s % 2, q_rows(row_y, 0)] + yr[s, 1]
        y_copy(s, 4).start()
        y_copy(s, 3).wait_recv()
        qb[s % 2, q_rows(row_x, 1)] = qb[s % 2, q_rows(row_x, 1)] + yr[s, 3]
        y_copy(s, 5).start()

    def y_end(s):
        for i in (0, 2, 4, 5):
            y_copy(s, i).wait_recv()
        for h, (i, j) in enumerate(((0, 4), (2, 5))):
            yo[s, pl.ds(h * half_y, half_y)] = -(qb[s % 2, q_rows(row, h)] + yr[s, i] + yr[s, j])
        if s > 0:
            yo[s] = yo[s] - dot3(halves(yo[s - 1]), halves(f_ref[s - 1]), 1, 1)
        y_leave(s).start()

    def y_sent(s):
        for i in range(6):
            y_copy(s, i).wait_send()

    first = ((row == 0) & (col == 0)).astype(f32)

    def fill(value, index):
        _, odd = window(index)
        hi, lo = halves(value)
        win_h[...] = jnp.zeros(win_h.shape, bf16)
        win_l[...] = jnp.zeros(win_l.shape, bf16)
        rows = pl.ds(pl.multiple_of(odd, 64), slab)
        win_h[rows] = hi
        win_l[rows] = lo

    def with_upper(s):
        return dot3((uw_h[s], uw_l[s]), (win_h[...], win_l[...]), 1, 0)

    def d_copy(s):
        return pltpu.make_async_copy(d_ref.at[s], keep.at[0], d_sem)

    def put(value, g, i):
        n = groups[g]
        for r in range(prow):
            for h in range(2):
                at = base(g) + ((h * prow + r) * n + i) * half_l
                pb[pl.ds(at, half_l)] = value[r * part_l + h * half_l : r * part_l + (h + 1) * half_l]

    groups = (3, 3, 1)

    def base(g):
        return (0, nz * slab, supers * nz * slab)[g]

    def corner_first():
        d_copy(0).start()
        fill(xo[0], col)
        got = with_upper(0)
        d_copy(0).wait()
        keep[0] = keep[0] * first - got

    def step_sums(s):
        edge_f = halves(f_ref[s - 1])
        corner = keep[0]
        put(corner, s - 1, 0)
        corner = halves(corner)
        fill(xo[s - 1], col)
        put(-(with_upper(s) + dot3(edge_f, corner, 1, 0)), s - 1, 2)
        fill(yo[s - 1], row)
        turned = dot3((lw_h[s - 1], lw_l[s - 1]), (win_h[...], win_l[...]), 1, 0)
        keep[1] = -(turned.T + dot3(corner, halves(e_ref[s - 1]), 1, 0))
        put(keep[1], s - 1, 1)

    def step_corner(s):
        d_copy(s).start()
        fill(xo[s], col)
        got = with_upper(s) + dot3(halves(f_ref[s - 1]), halves(keep[1]), 1, 0)
        d_copy(s).wait()
        keep[0] = keep[0] * first - got

    def s_rows(g, h, r=0, a=0, count=None):
        n = groups[g]
        at = base(g) + (h * prow + r) * n * half_l + a * n * half_l // 2
        return pl.ds(pl.multiple_of(at, 8), count or n * half_l // 2)

    def sp_copy(g):
        size = prow * groups[g] * half_l
        into = sp2 if g == 2 else pr.at[pl.ds(g * size, size)]
        return rc(pb.at[s_rows(g, other, count=size)], into, sp_send.at[g], sp_recv.at[g], to_pair)

    def s_pair(g):
        if g == 0:
            pl.semaphore_wait(free_pair.at[supers - 1], 1)
        sp_copy(g).start()

    def sq_copy(g, i):
        size = groups[g] * half_l // 2
        r, a, dev = (
            (row_x, 0, to_x), (row_d, 0, to_x), (row_y, 1, to_y), (row_d, 1, to_y), (row_y, 0, to_y), (row_x, 1, to_x),
        )[i]
        into = sq.at[i, pl.ds(sum(groups[:g]) * half_l // 2, size)]
        return rc(pb.at[s_rows(g, k, r, a)], into, sq_send.at[g, i], sq_recv.at[g, i], dev)

    def sq_got(g, i):
        return sq[i, pl.ds(sum(groups[:g]) * half_l // 2, groups[g] * half_l // 2)]

    def sd_copy(r, me, dev):
        return rc(
            pb.at[s_rows(2, k, r, 0, groups[2] * half_l)], sqd.at[me], sq_send.at[2, r], sq_recv.at[2, me], dev
        )

    rows_to = ((row_x, to_x), (row_y, to_y), (row_d, to_d))

    def s_add(g):
        size = prow * groups[g] * half_l
        sp_copy(g).wait_recv()
        mine = s_rows(g, k, count=size)
        pb[mine] = pb[mine] + (sp2[...] if g == 2 else pr[pl.ds(g * size, size)])
        if g == 2:
            for r, dev in rows_to:
                sd_copy(r, row, dev).start()
        else:
            for i in (1, 3, 0, 2):
                sq_copy(g, i).start()

    def s_relay(g):
        for i, r, a, j in ((1, row_y, 0, 4), (3, row_x, 1, 5)):
            sq_copy(g, i).wait_recv()
            there = s_rows(g, k, r, a)
            pb[there] = pb[there] + sq_got(g, i)
            sq_copy(g, j).start()

    def z_rows(g):
        return pl.ds(sum(groups[:g]) * half_l, groups[g] * half_l)

    def sn_copy(g, d, way):
        slot = d + 1 - way
        return rc(
            zb.at[d, z_rows(g)], zl.at[slot, z_rows(g)], sn_send.at[g, d], sn_recv.at[g, slot], (up, down)[way]
        )

    def sz_copy(d):
        rows = z_rows(2)
        return rc(zb.at[d, rows], zl.at[z, rows], sn_send.at[2, d], sn_recv.at[2, z], {"col": 2 * d + k})

    def s_turn(g):
        n = groups[g]
        if g == 2:
            there = s_rows(2, k, row, 0, n * half_l)
            for r, dev in rows_to:
                sd_copy(r, r, dev).wait_recv()
            pb[there] = (pb[there] + sqd[row_x]) + (sqd[row_y] + sqd[row_d])
        else:
            for i in (0, 2, 4, 5):
                sq_copy(g, i).wait_recv()
            for a, (i, j) in enumerate(((0, 4), (2, 5))):
                there = s_rows(g, k, row, a)
                pb[there] = pb[there] + sq_got(g, i) + sq_got(g, j)
        at = base(g) + (k * prow + row) * n * half_l
        total = pb[pl.ds(pl.multiple_of(at, 8), n * half_l)]
        wide = 2 * part_u
        for d in range(nz):
            turned = total if d == 0 else pltpu.roll(total, width - d * wide, 1)
            zb[d, z_rows(g)] = turned[:, :128]
        if g == 2:
            for d in range(nz):
                when(z != d, lambda: sz_copy(d).start())
            return

        @pl.when(z == 0)
        def _():
            for d in reversed(range(1, nz)):
                sn_copy(g, d, 0).start()

        @pl.when(z == nz - 1)
        def _():
            for d in range(nz - 1):
                sn_copy(g, d, 1).start()

    def s_take(g, d, slot):
        rows = z_rows(g)
        rc(zl.at[slot, rows], zl.at[slot, rows], sn_send.at[g, d], sn_recv.at[g, slot], to_pair).wait_recv()
        zb[d, rows] = zb[d, rows] + zl[slot, rows]

    def s_line(g, t):
        zb_ = nz - 1 - z

        @pl.when((z >= 1) & (z <= t))
        def _():
            d = z + (nz - 1 - t)
            s_take(g, d, d + 1)
            sn_copy(g, d, 0).start()

        @pl.when((zb_ >= 1) & (zb_ <= t))
        def _():
            d = z - (nz - 1 - t)
            s_take(g, d, d)
            sn_copy(g, d, 1).start()

    def sf_copy(g):
        return rc(zb.at[z, z_rows(g)], zf.at[z_rows(g)], sf_send.at[g], sf_recv.at[g], to_pair)

    def s_last(g):
        if g == 2:
            for there in range(nz):
                when(z != there, lambda: s_take(g, z, there))
        else:
            when(has_down, lambda: s_take(g, z, z + 1))
            when(has_up, lambda: s_take(g, z, z))
        sf_copy(g).start()

    def s_out(g):
        sf_copy(g).wait_recv()
        mine, theirs = zb[z, z_rows(g)], zf[z_rows(g)]
        for h, both in enumerate((jnp.where(k == 0, mine, theirs), jnp.where(k == 0, theirs, mine))):
            both = jnp.where(k == 0, both, pltpu.roll(both, 128 - part_u, 1))
            for i in range(groups[g]):
                tb[i, pl.ds(h * half_l, half_l)] = both[i * half_l : (i + 1) * half_l]
        for i in range(groups[g]):
            value = tb[i].T[:part_u, :part_l]
            if i == 0:
                zo[g] = value
            else:
                co[i - 1, g] = value

    def s_sent(g):
        sp_copy(g).wait_send()
        if g == 2:
            for r, dev in rows_to:
                sd_copy(r, row, dev).wait_send()
            for d in range(nz):
                when(z != d, lambda: sz_copy(d).wait_send())
        else:
            for i in range(6):
                sq_copy(g, i).wait_send()
            for d in range(nz):
                when(z < d, lambda: sn_copy(g, d, 0).wait_send())
                when(z > d, lambda: sn_copy(g, d, 1).wait_send())
        sf_copy(g).wait_send()

    def middle_0():
        u_step(1, 1, inside)
        l_fwd(1)

    def middle_1():
        when(inside, lambda: u_own(2))
        l_fwd(2)

    def middle_2():
        u_step(0, 2, at_end)

    tb[...] = jnp.zeros(tb.shape, f32)
    l_start(0)
    u_own(0)
    a_load()
    u_own(1)
    l_fwd(0)
    l_start(1)
    u_step(0, 1)
    when(at_end, lambda: u_own(2))
    l_done(0)
    l_conv(0)
    p_both(0, middle_0)
    pair_add(0, 0)
    pair_add(0, 1)
    l_start(2)
    l_done(1)
    l_conv(1)
    u_step(0, 2, inside)
    p_both(1, middle_1)
    pair_add(1, 0)
    pair_add(1, 1)
    line_t(0, 1)
    u_step(1, 2, inside)
    l_done(2)
    l_conv(2)
    p_both(2, middle_2)
    u_from_ends(2)
    u_step(0, 3)
    u_done(0)
    u_conv(0)
    q_comp(0)
    line_t(0, 2)
    u_from_inside(2)
    u_step(1, 1, at_end)
    u_step(1, 2, at_end)
    u_step(1, 3)
    u_done(1)
    u_conv(1)
    y_relay(0)
    line_t(1, 1)
    q_comp(1)
    when(inside, lambda: line_take(0))
    u_step(2, 2, inside)
    pair_add(2, 0)
    pair_add(2, 1)
    when(at_end, lambda: line_take(0))
    n_sent(0)
    x_out(0)
    y_end(0)
    corner_first()
    step_sums(1)
    s_pair(0)
    y_relay(1)
    s_add(0)
    line_t(1, 2)
    u_step(2, 1, at_end)
    u_step(2, 2, at_end)
    u_step(2, 3)
    u_done(2)
    u_conv(2)
    y_sent(0)
    q_part(2, 0, 3)
    line_t(2, 1)
    s_relay(0)
    line_take(1)
    x_out(1)
    y_end(1)
    step_corner(1)
    n_sent(1)
    step_sums(2)
    s_pair(1)
    line_t(2, 2)
    s_add(1)
    s_turn(0)
    q_part(2, 3, q_count)
    y_relay(2)
    s_relay(1)
    line_take(2)
    x_out(2)
    step_corner(2)
    p_copy(2, 0).wait_send()
    p_copy(2, 1).wait_send()
    put(keep[0], 2, 0)
    s_pair(2)
    s_line(0, 1)
    s_add(2)
    y_own(2)
    s_turn(1)
    s_line(0, 2)
    s_turn(2)
    s_line(1, 1)
    s_last(0)
    s_line(1, 2)
    s_last(1)
    s_last(2)
    s_out(0)
    y_end(2)
    s_out(1)
    s_out(2)

    for s in range(supers):
        x_leave(s).wait()
        y_leave(s).wait()
        for i in range(6):
            l_copy(s, i).wait_send()
        for zs in range(nz):
            for own in (True, False):
                mine = (z == zs) if own else (z != zs)

                @pl.when(mine)
                def _(s=s, zs=zs, own=own):
                    u_copy(s, zs, 2, own).wait_send()

            when((z >= zs) & has_up, lambda s=s, zs=zs: u_copy(s, zs, 0, False).wait_send())
            when((z <= zs) & has_down, lambda s=s, zs=zs: u_copy(s, zs, 1, False).wait_send())
    n_sent(2)
    y_sent(1)
    y_sent(2)
    s_sent(0)
    s_sent(1)
    s_sent(2)


def part_u_is_half(width, prow, pcol):
    return 2 * (width // pcol) == width // prow and (width // prow) % 48 == 0


def fits(shape):
    supers, width, blk, prow, pcol, rows_here, cols_here, slab = shape
    return (
        supers == 3 and prow == 4 and pcol % 4 == 0 and blk == 128 and width % blk == 0
        and slab % 64 == 0 and width == slab + 64 and slab % 128 == 64
        and rows_here % 640 == 0 and cols_here % 640 == 0
        and width % (8 * pcol) == 0 and width // prow <= 128
        and part_u_is_half(width, prow, pcol) and 3 * width <= (pcol // 2) * slab
    )


def sweep(shape, anc_inverse, lower, upper, lower_edge, upper_edge, diag_inverse, mask):
    supers, width, blk, prow, pcol, rows_here, cols_here, slab = shape
    nz = pcol // 2
    part_u = width // pcol
    sums = 3 * supers - 2
    vmem, dma = pltpu.VMEM, pltpu.SemaphoreType.DMA
    in_vmem = pl.BlockSpec(memory_space=pltpu.VMEM)
    in_hbm = pl.BlockSpec(memory_space=pl.ANY)
    out = [
        ((supers, slab, width), in_hbm),
        ((supers, slab, width), in_hbm),
        ((supers, part_u, width // prow), in_vmem),
        ((2, supers - 1, part_u, width // prow), in_vmem),
        ((supers, width, cols_here), in_hbm),
        ((supers, width, rows_here), in_hbm),
    ]
    return pl.pallas_call(
        functools.partial(sweep_kernel, (supers, width, blk, prow, nz, rows_here, cols_here, slab)),
        name="sweep",
        out_shape=[jax.ShapeDtypeStruct(dims, f32) for dims, _ in out],
        in_specs=[in_hbm, in_hbm, in_hbm, in_vmem, in_vmem, in_hbm, pl.BlockSpec(memory_space=pltpu.SMEM)],
        out_specs=[spec for _, spec in out],
        scratch_shapes=[
            vmem((rows_here, cols_here), bf16),
            vmem((rows_here, cols_here), bf16),
            vmem((width, cols_here), bf16),
            vmem((width, cols_here), bf16),
            vmem((width, rows_here), bf16),
            vmem((width, rows_here), bf16),
            vmem((2, width, cols_here // 2), f32),
            vmem(((supers + 1) * nz * slab, width), f32),
            vmem((nz * slab, width), f32),
            vmem((2, nz + 1, slab, width), f32),
            vmem((2, cols_here, width), f32),
            vmem((supers, 6, slab // 2, width), f32),
            vmem((supers, width, width), bf16),
            vmem((supers, width, width), bf16),
            vmem((supers - 1, width, width), bf16),
            vmem((supers - 1, width, width), bf16),
            vmem((width, width), bf16),
            vmem((width, width), bf16),
            vmem((2, width, width), f32),
            vmem((prow * width // (2 * prow), width), f32),
            vmem((6, (sums - 1) * width // (4 * prow), width), f32),
            vmem((prow, width // (2 * prow), width), f32),
            vmem((supers, 128, 128), f32),
            vmem((nz, sums * part_u, 128), f32),
            vmem((nz + 1, sums * part_u, 128), f32),
            vmem((sums * part_u, 128), f32),
            vmem((supers, slab, width), f32),
            vmem((supers, slab, width), f32),
            dma((2 * nz,)),
            dma((2,)),
            dma,
            dma((supers, 6)),
            dma((supers, 6)),
            dma((supers, nz, 3)),
            dma((supers, nz)),
            dma((supers, nz)),
            dma((supers, 2)),
            dma((supers, 2)),
            dma((supers, nz)),
            dma((supers, nz + 1)),
            dma((supers, 6)),
            dma((supers, 6)),
            dma((supers,)),
            dma((supers,)),
            dma((supers, 6)),
            dma((supers, 6)),
            dma((supers, nz)),
            dma((supers, nz + 1)),
            dma((supers,)),
            dma((supers,)),
            pltpu.SemaphoreType.REGULAR,
            pltpu.SemaphoreType.REGULAR,
            pltpu.SemaphoreType.REGULAR((supers,)),
            dma((2, supers)),
        ],
        compiler_params=pltpu.CompilerParams(
            collective_id=0, has_side_effects=True, vmem_limit_bytes=67043328
        ),
    )(anc_inverse, lower, upper, lower_edge, upper_edge, diag_inverse, mask)


def place(x, y, corner, cross):
    arrays = (x, y, corner, cross)
    pieces = [(a, i) for a, array in enumerate(arrays[:2]) for i in range(array.shape[0])] + [(2, None), (3, None)]

    def body(*refs):
        srcs, dsts, kept, (get, put) = refs[:4], refs[4:8], refs[8:12], refs[12:]

        def view(ref, i):
            return ref if i is None else ref.at[i]

        def copies(n):
            a, i = pieces[n]
            src, mid, dst = (view(r[a], i) for r in (srcs, kept, dsts))
            return pltpu.make_async_copy(src, mid, get.at[n]), pltpu.make_async_copy(mid, dst, put.at[n])

        for n in range(len(pieces)):
            copies(n)[0].start()
        for n in range(len(pieces)):
            copies(n)[0].wait()
            copies(n)[1].start()
        for n in range(len(pieces)):
            copies(n)[1].wait()

    return pl.pallas_call(
        body,
        name="place",
        out_shape=[jax.ShapeDtypeStruct(one.shape, f32) for one in arrays],
        in_specs=[pl.BlockSpec(memory_space=pl.ANY)] * 4,
        out_specs=[pl.BlockSpec(memory_space=pl.ANY)] * 4,
        scratch_shapes=[pltpu.VMEM(one.shape, f32) for one in arrays]
        + [pltpu.SemaphoreType.DMA((len(pieces),))] * 2,
    )(*arrays)


def per_device(anc_inverse, lower_anc, upper_anc, lower_edge, upper_edge, diag_inverse, tile_mask):
    rows_here, cols_here = anc_inverse.shape
    prow, pcol = lax.axis_size("row"), lax.axis_size("col")
    supers, width = diag_inverse.shape[0], diag_inverse.shape[1]
    blk = width // tile_mask.shape[2]
    shape = (supers, width, blk, prow, pcol, rows_here, cols_here, cols_here // prow)
    args = (anc_inverse, lower_anc, upper_anc, lower_edge, upper_edge, diag_inverse, tile_mask)
    if not fits(shape):
        return general(*args)
    x, y, corner, cross, _, _ = sweep(
        shape,
        anc_inverse,
        jnp.transpose(lower_anc, (1, 2, 0)),
        jnp.transpose(upper_anc, (1, 2, 0)),
        lower_edge,
        upper_edge,
        diag_inverse,
        jnp.transpose(tile_mask, (0, 2, 1)),
    )
    x, y, corner, cross = place(x, y, corner, cross)
    return (
        jnp.transpose(x, (1, 0, 2)),
        jnp.transpose(y, (1, 0, 2))[None, None],
        jnp.transpose(corner, (0, 2, 1)),
        jnp.transpose(cross, (0, 1, 3, 2)),
    )


precise = lax.Precision.HIGH


def contract(left, right, left_dim, right_dim):
    return lax.dot_general(
        left,
        right,
        (((left_dim,), (right_dim,)), ((), ())),
        precision=precise,
        preferred_element_type=jnp.float32,
    )


def row_major(array):
    return with_layout_constraint(array, Layout(major_to_minor=(0, 1)))


def partner(index, step, count):
    if count & (count - 1) == 0:
        return index ^ step
    return (step - index) % count


def exchange(piece_for, axis):
    count = lax.axis_size(axis)
    index = lax.axis_index(axis)
    got = []
    for step in range(count):
        peer = partner(index, step, count)
        piece = piece_for(peer)
        pairs = [(i, partner(i, step, count)) for i in range(count)]
        if any(i != j for i, j in pairs):
            piece = lax.ppermute(piece, axis, pairs)
        got.append((peer, piece))
    return got


def mask_factor(factor, tile_mask, first_row, first_col, blk):
    rows, supers, cols = factor.shape
    blocks = rows // blk
    window = lax.dynamic_slice_in_dim(tile_mask, first_row // blk, blocks, 1).astype(jnp.float32)
    tile_cols = window.shape[2]
    tile_of_col = (first_col + jnp.arange(cols)) // blk
    pick = (tile_of_col[None, :] == jnp.arange(tile_cols)[:, None]).astype(jnp.float32)
    chosen = sum(window[:, :, t, None] * pick[t] for t in range(tile_cols))
    chosen = jnp.transpose(chosen, (1, 0, 2))
    masked = factor.reshape(blocks, blk, supers, cols) * chosen[:, None]
    return jnp.transpose(masked.reshape(rows, supers, cols), (1, 2, 0))


def general(anc_inverse, lower_anc, upper_anc, lower_edge, upper_edge, diag_inverse, tile_mask):
    rows_here, cols_here = anc_inverse.shape
    prow = lax.axis_size("row")
    pcol = lax.axis_size("col")
    supers, width = diag_inverse.shape[0], diag_inverse.shape[1]
    blk = width // tile_mask.shape[2]
    row = lax.axis_index("row")
    col = lax.axis_index("col")
    part_lower = width // prow
    part_upper = width // pcol

    upper_t = mask_factor(upper_anc, tile_mask, row * rows_here, col * part_upper, blk)
    lower_t = mask_factor(lower_anc, tile_mask, col * cols_here, row * part_lower, blk)

    upper_t = lax.all_gather(upper_t, "col", axis=0)
    lower_full = jnp.zeros((supers, prow, part_lower, cols_here), jnp.float32)
    for peer, piece in exchange(lambda _: lower_t, "row"):
        lower_full = lax.dynamic_update_slice(lower_full, piece[:, None], (0, peer, 0, 0))
    lower_full = lower_full.reshape(supers, width, cols_here)
    lower_comb = [-lower_full[0]]
    for s in range(1, supers):
        lower_comb.append(-lower_full[s] - contract(lower_edge[s - 1], lower_comb[-1], 0, 0))
    cols_part = [row_major(contract(anc_inverse, one, 1, 1)) for one in lower_comb]
    cols_mine = [lax.psum_scatter(one, "col", scatter_dimension=0, tiled=True) for one in cols_part]

    upper_full = [upper_t[:, s].reshape(width, rows_here) for s in range(supers)]
    upper_comb = [-upper_full[0]]
    for s in range(1, supers):
        upper_comb.append(-upper_full[s] - contract(upper_edge[s - 1], upper_comb[-1], 1, 0))
    rows_part = [row_major(contract(anc_inverse, one, 0, 1)) for one in upper_comb]

    first = jnp.logical_and(row == 0, col == 0)
    corner = []
    cross_cols = []
    cross_rows = []
    for s in range(supers):
        upper_here = contract(upper_full[s], cols_part[s], 1, 0)
        now = jnp.where(first, diag_inverse[s], 0.0) - upper_here
        if s > 0:
            upper_prev = contract(upper_full[s], cols_part[s - 1], 1, 0)
            lower_prev = lax.dot_general(
                rows_part[s - 1],
                lower_full[s],
                (((0,), (1,)), ((), ())),
                precision=precise,
                preferred_element_type=jnp.float32,
            )
            cross_col = -(lower_prev + contract(corner[-1], lower_edge[s - 1], 1, 0))
            cross_row = -(upper_prev + contract(upper_edge[s - 1], corner[-1], 1, 0))
            now = now - contract(upper_edge[s - 1], cross_col, 1, 0)
            cross_cols.append(cross_col)
            cross_rows.append(cross_row)
        corner.append(now)
    sums = jnp.stack(corner + cross_cols + cross_rows)
    count = sums.shape[0]

    row_slab = cols_here // prow
    rows_mine = [
        sum(
            piece
            for _, piece in exchange(
                lambda peer: lax.dynamic_slice_in_dim(one, peer * row_slab, row_slab, 0), "row"
            )
        )
        for one in rows_part
    ]
    sums, rows_mine = lax.optimization_barrier((sums, rows_mine))
    sums = sum(
        piece
        for _, piece in exchange(
            lambda peer: lax.dynamic_slice_in_dim(sums, peer * part_lower, part_lower, 1), "row"
        )
    )
    sums = jnp.transpose(sums.reshape(count * part_lower, width))
    sums, cols_mine = lax.optimization_barrier((sums, cols_mine))
    sums = lax.psum_scatter(sums, "col", scatter_dimension=0, tiled=True)
    sums = jnp.transpose(sums).reshape(count, part_lower, part_upper)

    x_blocks = jnp.stack(cols_mine, axis=1)
    y_blocks = jnp.stack(rows_mine, axis=1)[None, None]
    z_blocks = sums[:supers]
    cross_blocks = sums[supers:].reshape(2, supers - 1, part_lower, part_upper)
    return (x_blocks, y_blocks, z_blocks, cross_blocks)


def solution(mesh):
    return jax.shard_map(
        per_device,
        mesh=mesh,
        in_specs=(
            P("row", "col"),
            P("col", None, "row"),
            P("row", None, "col"),
            P(),
            P(),
            P(),
            P(),
        ),
        out_specs=(
            P(("row", "col"), None, None),
            P("col", "row", None, None, None),
            P(None, "row", "col"),
            P(None, None, "row", "col"),
        ),
        check_vma=False,
    )
```

```python
import functools

import jax
import jax.numpy as jnp
from jax import lax
from jax.experimental import pallas as pl
from jax.experimental.pallas import tpu as pltpu
from jax.experimental.layout import Layout, with_layout_constraint
from jax.sharding import PartitionSpec as P


f32 = jnp.float32
bf16 = jnp.bfloat16


def halves(value):
    hi = value.astype(bf16)
    return hi, (value - hi.astype(f32)).astype(bf16)


def dot3(left, right, left_dim, right_dim):
    dims = (((left_dim,), (right_dim,)), ((), ()))

    def one(a, b):
        return lax.dot_general(a, b, dims, preferred_element_type=f32)

    return one(left[0], right[0]) + (one(left[0], right[1]) + one(left[1], right[0]))


def sweep_kernel(
    shape,
    a_ref, l_ref, u_ref, e_ref, f_ref, d_ref, mask_ref,
    x_hbm, y_hbm, z_hbm, c_hbm, lbuf, ubuf,
    ah, al, lh, ll, uh, ul, stage, pb, pr, ln, qb, yr, uw_h, uw_l, lw_h, lw_l, win_h, win_l, keep,
    sp2, sq, sqd, tb, zb, zl, zf, xo, yo, zo, co,
    a_sem, st_sem, d_sem, l_send, l_recv, u_send, u_recv, up_recv, p_send, p_recv, n_send, n_recv,
    y_send, y_recv, sp_send, sp_recv, sq_send, sq_recv, sn_send, sn_recv, sf_send, sf_recv,
    free_up, free_down, free_pair, o_sem, c_sem,
):
    supers, width, blk, prow, nz, rows_here, cols_here, slab = shape
    pcol = 2 * nz
    part_l, part_u = width // prow, width // pcol
    row = lax.axis_index("row")
    col = lax.axis_index("col")
    z, k = col // 2, col % 2
    other = 1 - k
    y, x = row // 2, row % 2
    row_x, row_y, row_d = y * 2 + 1 - x, (1 - y) * 2 + x, (1 - y) * 2 + 1 - x
    to_x, to_y, to_d = {"row": row_x}, {"row": row_y}, {"row": row_d}
    to_pair = {"col": col + 1 - 2 * k}
    up, down = {"col": col + 2}, {"col": col - 2}
    has_up, has_down = z < nz - 1, z > 0
    at_end, inside = (z == 0) | (z == nz - 1), (z > 0) & (z < nz - 1)

    def when(cond, body):
        pl.when(cond)(body)

    def rc(src, dst, ss, rs, dev):
        return pltpu.make_async_remote_copy(
            src_ref=src, dst_ref=dst, send_sem=ss, recv_sem=rs,
            device_id=dev, device_id_type=pl.DeviceIdType.MESH,
        )

    barrier = pltpu.get_barrier_semaphore()

    def greet(dev):
        pl.semaphore_signal(barrier, inc=1, device_id=dev, device_id_type=pl.DeviceIdType.MESH)

    for dev in (to_x, to_y, to_d, to_pair):
        greet(dev)
    for there in range(nz):
        when(z != there, lambda: greet({"col": 2 * there + k}))
    pl.semaphore_wait(barrier, 4 + nz - 1)

    half_l = part_l // 2

    def l_piece(s, r, h):
        return lbuf.at[s, pl.ds(pl.multiple_of(r * part_l + h * half_l, 8), half_l)]

    def l_own(s, h):
        return l_ref.at[s, pl.ds(h * half_l, half_l)]

    def l_copy(s, i):
        src, dst, dev = (
            (l_own(s, 1), l_piece(s, row, 1), to_x),
            (l_own(s, 0), l_piece(s, row, 0), to_y),
            (l_own(s, 0), l_piece(s, row, 0), to_x),
            (l_own(s, 1), l_piece(s, row, 1), to_y),
            (l_piece(s, row_x, 1), l_piece(s, row_x, 1), to_y),
            (l_piece(s, row_y, 0), l_piece(s, row_y, 0), to_x),
        )[i]
        return rc(src, dst, l_send.at[s, i], l_recv.at[s, i], dev)

    def l_take(s, i):
        r, h = ((row_x, 1), (row_y, 0), (row_x, 0), (row_y, 1), (row_d, 1), (row_d, 0))[i]
        rc(l_piece(s, r, h), l_piece(s, r, h), l_send.at[s, i], l_recv.at[s, i], to_pair).wait_recv()

    def l_start(s):
        for i in range(4):
            l_copy(s, i).start()

    def l_fwd(s):
        l_take(s, 0)
        l_copy(s, 4).start()
        l_take(s, 1)
        l_copy(s, 5).start()

    def l_done(s):
        for i in range(2, 6):
            l_take(s, i)

    def u_piece(s, c):
        return ubuf.at[s, pl.ds(pl.multiple_of(c * part_u, 8), part_u)]

    def u_copy(s, zs, way, own):
        mine = u_piece(s, zs * 2 + k)
        src = u_ref.at[s] if own else mine
        recv = up_recv if way == 2 else u_recv
        return rc(src, mine, u_send.at[s, zs, way], recv.at[s, zs], (up, down, to_pair)[way])

    def u_own(s):
        when(has_up, lambda: u_copy(s, z, 0, True).start())
        when(has_down, lambda: u_copy(s, z, 1, True).start())
        u_copy(s, z, 2, True).start()

    def u_low(s, t, cond):
        @pl.when((z >= t) & cond)
        def _():
            u_copy(s, z - t, 1, False).wait_recv()
            when(has_up, lambda: u_copy(s, z - t, 0, False).start())
            u_copy(s, z - t, 2, False).start()

    def u_high(s, t, cond):
        @pl.when((z + t < nz) & cond)
        def _():
            u_copy(s, z + t, 0, False).wait_recv()
            when(has_down, lambda: u_copy(s, z + t, 1, False).start())
            u_copy(s, z + t, 2, False).start()

    def u_step(s, t, cond=None):
        cond = z >= 0 if cond is None else cond
        u_low(s, t, cond)
        u_high(s, t, cond)

    def u_from_ends(s):
        u_low(s, 1, inside & (z == 1))
        u_high(s, 1, inside & (z == nz - 2))

    def u_from_inside(s):
        u_low(s, 1, inside & (z > 1))
        u_high(s, 1, inside & (z < nz - 2))

    def u_done(s):
        for zs in range(nz):
            piece = u_piece(s, zs * 2 + other)
            rc(piece, piece, u_send.at[s, zs, 2], up_recv.at[s, zs], to_pair).wait_recv()

    lanes = stage.shape[2]
    tiles = lanes // blk

    def load(buf, own_ref, s, count, me, part, q):
        here = pl.ds(q * lanes, lanes)

        @pl.loop(0, count)
        def _(p):
            there = stage.at[q % 2, pl.ds(pl.multiple_of(p * part, 8), part)]

            @pl.when(p != me)
            def _():
                pltpu.make_async_copy(
                    buf.at[s, pl.ds(pl.multiple_of(p * part, 8), part), here], there, st_sem.at[q % 2]
                ).start()

            @pl.when(p == me)
            def _():
                pltpu.make_async_copy(own_ref.at[s, :, here], there, st_sem.at[q % 2]).start()

    def convert(buf, own_ref, s, count, me, part, total, first_tile, out_h, out_l):
        load(buf, own_ref, s, count, me, part, 0)
        for q in range(total // lanes):
            if q + 1 < total // lanes:
                load(buf, own_ref, s, count, me, part, q + 1)
            pltpu.make_async_copy(stage.at[q % 2], stage.at[q % 2], st_sem.at[q % 2]).wait()

            @pl.loop(0, tiles)
            def _(t):
                src = pl.ds(pl.multiple_of(t * blk, 128), blk)
                dst = pl.ds(pl.multiple_of(q * lanes + t * blk, 128), blk)
                for j in range(width // blk):
                    keep_it = mask_ref[s, j, first_tile + q * tiles + t].astype(f32)
                    rows = pl.ds(j * blk, blk)
                    hi, lo = halves(stage[q % 2, rows, src] * keep_it)
                    out_h[rows, dst] = hi
                    out_l[rows, dst] = lo

    def window(index):
        start = index * slab
        odd = start % 128
        return pl.ds(pl.multiple_of(start - odd, 128), width), odd

    def l_conv(s):
        convert(lbuf, l_ref, s, prow, row, part_l, cols_here, col * (cols_here // blk), lh, ll)
        if s > 0:
            where, _ = window(row)
            lw_h[s - 1] = lh[:, where]
            lw_l[s - 1] = ll[:, where]

    def u_conv(s):
        convert(ubuf, u_ref, s, pcol, col, part_u, rows_here, row * (rows_here // blk), uh, ul)
        where, _ = window(col)
        uw_h[s] = uh[:, where]
        uw_l[s] = ul[:, where]

    a_lanes = 256
    a_cols = cols_here // a_lanes
    a_slots = 2 * nz

    def a_copy(n, slot):
        i, j = n // a_cols, n % a_cols
        return pltpu.make_async_copy(
            a_ref.at[pl.ds(pl.multiple_of(i * slab, 8), slab), pl.ds(pl.multiple_of(j * a_lanes, 128), a_lanes)],
            pb.at[pl.ds(pl.multiple_of(slot * slab, 64), slab), pl.ds(0, a_lanes)],
            a_sem.at[slot],
        )

    def a_load():
        count = (rows_here // slab) * a_cols
        for n in range(a_slots - 1):
            a_copy(n, n).start()

        @pl.loop(0, count)
        def _(n):
            slot = n % a_slots

            @pl.when(n + a_slots - 1 < count)
            def _():
                a_copy(n + a_slots - 1, (n + a_slots - 1) % a_slots).start()

            a_copy(n, slot).wait()
            i, j = n // a_cols, n % a_cols
            across = pl.ds(pl.multiple_of(j * a_lanes, 128), a_lanes)
            step = 64
            for b in range(slab // step):
                hi, lo = halves(pb[pl.ds(pl.multiple_of(slot * slab + b * step, 64), step), pl.ds(0, a_lanes)])
                down_to = pl.ds(pl.multiple_of(i * slab + b * step, 64), step)
                ah[down_to, across] = hi
                al[down_to, across] = lo

    hz = nz // 2
    h_rows = rows_here // 2

    def far(i):
        flip = (z < hz).astype(jnp.int32)
        return (flip + i) % 2

    def p_rows(s, d, n=1):
        return pl.ds(pl.multiple_of((s * nz + d) * slab, 64), n * slab)

    def p_copy(s, hh):
        return rc(
            pb.at[p_rows(supers, hh * hz, hz)], pr.at[p_rows(0, hh * hz, hz)],
            p_send.at[s, hh], p_recv.at[s, hh], to_pair,
        )

    def p_both(s, middle):
        @pl.loop(0, 2)
        def _(i):
            when(i == 1, middle)
            hh = far(i)
            if s > 0:
                p_copy(s - 1, hh).wait_send()
            rows = pl.ds(pl.multiple_of(hh * h_rows, 128), h_rows)
            got = dot3((lh[...], ll[...]), (ah[rows], al[rows]), 1, 1).T
            for q in range(2 * hz):
                spot = jnp.where(k == q % 2, s, supers)
                pb[p_rows(spot, hh * hz + q // 2)] = got[q * slab : (q + 1) * slab]
            if s > 0:
                when(i == 0, lambda: pl.semaphore_wait(free_pair.at[s - 1], 1))
            p_copy(s, hh).start()

    def n_copy(s, d, way):
        slot = d + 1 - way
        return rc(pb.at[p_rows(s, d)], ln.at[s % 2, slot], n_send.at[s, d], n_recv.at[s, slot], (up, down)[way])

    def n_take(s, d, slot):
        rc(ln.at[s % 2, slot], ln.at[s % 2, slot], n_send.at[s, d], n_recv.at[s, slot], to_pair).wait_recv()
        pb[p_rows(s, d)] = pb[p_rows(s, d)] + ln[s % 2, slot]

    def tell(sem, dev):
        pl.semaphore_signal(sem, inc=1, device_id=dev, device_id_type=pl.DeviceIdType.MESH)

    def line_wait():
        when(has_up, lambda: pl.semaphore_wait(free_up, 1))
        when(has_down, lambda: pl.semaphore_wait(free_down, 1))

    def pair_add(s, i):
        if s == 2 and i == 0:
            when(at_end, line_wait)
        hh = far(i)
        p_copy(s, hh).wait_recv()
        for q in range(hz):
            d = hh * hz + q
            pb[p_rows(s, d)] = pb[p_rows(s, d)] + pr[p_rows(0, d)]
        if i == 1:
            tell(free_pair.at[s], to_pair)
        lo, hi = (1 - i) * hz, (2 - i) * hz

        @pl.when(z == 0)
        def _():
            for d in reversed(range(max(lo, 1), hi)):
                n_copy(s, d, 0).start()

        lo, hi = i * hz, (i + 1) * hz

        @pl.when(z == nz - 1)
        def _():
            for d in range(lo, min(hi, nz - 1)):
                n_copy(s, d, 1).start()

    def line_t(s, t):
        zb_ = nz - 1 - z
        if s == 2 and t == 1:
            when(inside, line_wait)

        @pl.when((z >= 1) & (z <= t))
        def _():
            d = z + (nz - 1 - t)
            n_take(s, d, d + 1)
            n_copy(s, d, 0).start()

        @pl.when((zb_ >= 1) & (zb_ <= t))
        def _():
            d = z - (nz - 1 - t)
            n_take(s, d, d)
            n_copy(s, d, 1).start()

    def line_take(s):
        when(has_down, lambda: n_take(s, z, z + 1))
        when(has_up, lambda: n_take(s, z, z))
        if s == 0:
            when(has_down, lambda: tell(free_up, down))
            when(has_up, lambda: tell(free_down, up))

    def x_leave(s):
        return pltpu.make_async_copy(xo.at[s], x_hbm.at[s], o_sem.at[0, s])

    def y_leave(s):
        return pltpu.make_async_copy(yo.at[s], y_hbm.at[s], o_sem.at[1, s])

    def x_out(s):
        total = -pb[p_rows(s, z)]
        if s > 0:
            total = total - dot3(halves(xo[s - 1]), halves(e_ref[s - 1]), 1, 0)
        xo[s] = total
        x_leave(s).start()

    def n_sent(s):
        for d in range(nz):
            when(z < d, lambda d=d: n_copy(s, d, 0).wait_send())
            when(z > d, lambda d=d: n_copy(s, d, 1).wait_send())

    half_y = slab // 2
    q_cols = 256

    def q_rows(r, h):
        return pl.ds(pl.multiple_of(r * slab + h * half_y, 8), half_y)

    def q_slab(s, r, h):
        return qb.at[s % 2, q_rows(r, h)]

    def y_copy(s, i):
        src, dev = (
            (q_slab(s, row_x, 0), to_x),
            (q_slab(s, row_d, 0), to_x),
            (q_slab(s, row_y, 1), to_y),
            (q_slab(s, row_d, 1), to_y),
            (q_slab(s, row_y, 0), to_y),
            (q_slab(s, row_x, 1), to_x),
        )[i]
        return rc(src, yr.at[s, i], y_send.at[s, i], y_recv.at[s, i], dev)

    q_count = cols_here // q_cols

    def q_part(s, start, stop):
        @pl.loop(start, stop)
        def _(i):
            @pl.when(i == 2)
            def _():
                y_copy(s, 1).start()
                y_copy(s, 3).start()

            across = pl.ds(pl.multiple_of((row_d + i) % q_count * q_cols, 128), q_cols)
            got = dot3((uh[...], ul[...]), (ah[:, across], al[:, across]), 1, 0)
            qb[s % 2, across] = got.T

    def y_own(s):
        y_copy(s, 0).start()
        y_copy(s, 2).start()

    def q_comp(s):
        q_part(s, 0, q_count)
        y_own(s)

    def y_relay(s):
        y_copy(s, 1).wait_recv()
        qb[s % 2, q_rows(row_y, 0)] = qb[s % 2, q_rows(row_y, 0)] + yr[s, 1]
        y_copy(s, 4).start()
        y_copy(s, 3).wait_recv()
        qb[s % 2, q_rows(row_x, 1)] = qb[s % 2, q_rows(row_x, 1)] + yr[s, 3]
        y_copy(s, 5).start()

    def y_end(s):
        for i in (0, 2, 4, 5):
            y_copy(s, i).wait_recv()
        for h, (i, j) in enumerate(((0, 4), (2, 5))):
            yo[s, pl.ds(h * half_y, half_y)] = -(qb[s % 2, q_rows(row, h)] + yr[s, i] + yr[s, j])
        if s > 0:
            yo[s] = yo[s] - dot3(halves(yo[s - 1]), halves(f_ref[s - 1]), 1, 1)
        y_leave(s).start()

    def y_sent(s):
        for i in range(6):
            y_copy(s, i).wait_send()

    first = ((row == 0) & (col == 0)).astype(f32)

    def fill(value, index):
        _, odd = window(index)
        hi, lo = halves(value)
        win_h[...] = jnp.zeros(win_h.shape, bf16)
        win_l[...] = jnp.zeros(win_l.shape, bf16)
        rows = pl.ds(pl.multiple_of(odd, 64), slab)
        win_h[rows] = hi
        win_l[rows] = lo

    def with_upper(s):
        return dot3((uw_h[s], uw_l[s]), (win_h[...], win_l[...]), 1, 0)

    def d_copy(s):
        return pltpu.make_async_copy(d_ref.at[s], keep.at[0], d_sem)

    def put(value, g, i):
        n = groups[g]
        for r in range(prow):
            for h in range(2):
                at = base(g) + ((h * prow + r) * n + i) * half_l
                pb[pl.ds(at, half_l)] = value[r * part_l + h * half_l : r * part_l + (h + 1) * half_l]

    groups = (3, 3, 1)

    def base(g):
        return (0, nz * slab, supers * nz * slab)[g]

    def corner_first():
        d_copy(0).start()
        fill(xo[0], col)
        got = with_upper(0)
        d_copy(0).wait()
        keep[0] = keep[0] * first - got

    def step_sums(s):
        edge_f = halves(f_ref[s - 1])
        corner = keep[0]
        put(corner, s - 1, 0)
        corner = halves(corner)
        fill(xo[s - 1], col)
        put(-(with_upper(s) + dot3(edge_f, corner, 1, 0)), s - 1, 2)
        fill(yo[s - 1], row)
        turned = dot3((lw_h[s - 1], lw_l[s - 1]), (win_h[...], win_l[...]), 1, 0)
        keep[1] = -(turned.T + dot3(corner, halves(e_ref[s - 1]), 1, 0))
        put(keep[1], s - 1, 1)

    def step_corner(s):
        d_copy(s).start()
        fill(xo[s], col)
        got = with_upper(s) + dot3(halves(f_ref[s - 1]), halves(keep[1]), 1, 0)
        d_copy(s).wait()
        keep[0] = keep[0] * first - got

    def s_rows(g, h, r=0, a=0, count=None):
        n = groups[g]
        at = base(g) + (h * prow + r) * n * half_l + a * n * half_l // 2
        return pl.ds(pl.multiple_of(at, 8), count or n * half_l // 2)

    def sp_copy(g):
        size = prow * groups[g] * half_l
        into = sp2 if g == 2 else pr.at[pl.ds(g * size, size)]
        return rc(pb.at[s_rows(g, other, count=size)], into, sp_send.at[g], sp_recv.at[g], to_pair)

    def s_pair(g):
        if g == 0:
            pl.semaphore_wait(free_pair.at[supers - 1], 1)
        sp_copy(g).start()

    def sq_copy(g, i):
        size = groups[g] * half_l // 2
        r, a, dev = (
            (row_x, 0, to_x), (row_d, 0, to_x), (row_y, 1, to_y), (row_d, 1, to_y), (row_y, 0, to_y), (row_x, 1, to_x),
        )[i]
        into = sq.at[i, pl.ds(sum(groups[:g]) * half_l // 2, size)]
        return rc(pb.at[s_rows(g, k, r, a)], into, sq_send.at[g, i], sq_recv.at[g, i], dev)

    def sq_got(g, i):
        return sq[i, pl.ds(sum(groups[:g]) * half_l // 2, groups[g] * half_l // 2)]

    def sd_copy(r, me, dev):
        return rc(
            pb.at[s_rows(2, k, r, 0, groups[2] * half_l)], sqd.at[me], sq_send.at[2, r], sq_recv.at[2, me], dev
        )

    rows_to = ((row_x, to_x), (row_y, to_y), (row_d, to_d))

    def s_add(g):
        size = prow * groups[g] * half_l
        sp_copy(g).wait_recv()
        mine = s_rows(g, k, count=size)
        pb[mine] = pb[mine] + (sp2[...] if g == 2 else pr[pl.ds(g * size, size)])
        if g == 2:
            for r, dev in rows_to:
                sd_copy(r, row, dev).start()
        else:
            for i in (1, 3, 0, 2):
                sq_copy(g, i).start()

    def s_relay(g):
        for i, r, a, j in ((1, row_y, 0, 4), (3, row_x, 1, 5)):
            sq_copy(g, i).wait_recv()
            there = s_rows(g, k, r, a)
            pb[there] = pb[there] + sq_got(g, i)
            sq_copy(g, j).start()

    def z_rows(g):
        return pl.ds(sum(groups[:g]) * half_l, groups[g] * half_l)

    def sn_copy(g, d, way):
        slot = d + 1 - way
        return rc(
            zb.at[d, z_rows(g)], zl.at[slot, z_rows(g)], sn_send.at[g, d], sn_recv.at[g, slot], (up, down)[way]
        )

    def sz_copy(d):
        rows = z_rows(2)
        return rc(zb.at[d, rows], zl.at[z, rows], sn_send.at[2, d], sn_recv.at[2, z], {"col": 2 * d + k})

    def s_turn(g):
        n = groups[g]
        if g == 2:
            there = s_rows(2, k, row, 0, n * half_l)
            for r, dev in rows_to:
                sd_copy(r, r, dev).wait_recv()
            pb[there] = (pb[there] + sqd[row_x]) + (sqd[row_y] + sqd[row_d])
        else:
            for i in (0, 2, 4, 5):
                sq_copy(g, i).wait_recv()
            for a, (i, j) in enumerate(((0, 4), (2, 5))):
                there = s_rows(g, k, row, a)
                pb[there] = pb[there] + sq_got(g, i) + sq_got(g, j)
        at = base(g) + (k * prow + row) * n * half_l
        total = pb[pl.ds(pl.multiple_of(at, 8), n * half_l)]
        wide = 2 * part_u
        for d in range(nz):
            turned = total if d == 0 else pltpu.roll(total, width - d * wide, 1)
            zb[d, z_rows(g)] = turned[:, :128]
        if g == 2:
            for d in range(nz):
                when(z != d, lambda: sz_copy(d).start())
            return

        @pl.when(z == 0)
        def _():
            for d in reversed(range(1, nz)):
                sn_copy(g, d, 0).start()

        @pl.when(z == nz - 1)
        def _():
            for d in range(nz - 1):
                sn_copy(g, d, 1).start()

    def s_take(g, d, slot):
        rows = z_rows(g)
        rc(zl.at[slot, rows], zl.at[slot, rows], sn_send.at[g, d], sn_recv.at[g, slot], to_pair).wait_recv()
        zb[d, rows] = zb[d, rows] + zl[slot, rows]

    def s_line(g, t):
        zb_ = nz - 1 - z

        @pl.when((z >= 1) & (z <= t))
        def _():
            d = z + (nz - 1 - t)
            s_take(g, d, d + 1)
            sn_copy(g, d, 0).start()

        @pl.when((zb_ >= 1) & (zb_ <= t))
        def _():
            d = z - (nz - 1 - t)
            s_take(g, d, d)
            sn_copy(g, d, 1).start()

    def sf_copy(g):
        return rc(zb.at[z, z_rows(g)], zf.at[z_rows(g)], sf_send.at[g], sf_recv.at[g], to_pair)

    def s_last(g):
        if g == 2:
            for there in range(nz):
                when(z != there, lambda: s_take(g, z, there))
        else:
            when(has_down, lambda: s_take(g, z, z + 1))
            when(has_up, lambda: s_take(g, z, z))
        sf_copy(g).start()

    def c_leave(g, i):
        src, dst = (zo.at[g], z_hbm.at[g]) if i == 0 else (co.at[i - 1, g], c_hbm.at[i - 1, g])
        return pltpu.make_async_copy(src, dst, c_sem.at[i, g])

    def s_out(g):
        sf_copy(g).wait_recv()
        mine, theirs = zb[z, z_rows(g)], zf[z_rows(g)]
        for h, both in enumerate((jnp.where(k == 0, mine, theirs), jnp.where(k == 0, theirs, mine))):
            both = jnp.where(k == 0, both, pltpu.roll(both, 128 - part_u, 1))
            for i in range(groups[g]):
                tb[i, pl.ds(h * half_l, half_l)] = both[i * half_l : (i + 1) * half_l]
        for i in range(groups[g]):
            value = tb[i].T[:part_u, :part_l]
            if i == 0:
                zo[g] = value
            else:
                co[i - 1, g] = value
            c_leave(g, i).start()

    def s_sent(g):
        sp_copy(g).wait_send()
        if g == 2:
            for r, dev in rows_to:
                sd_copy(r, row, dev).wait_send()
            for d in range(nz):
                when(z != d, lambda: sz_copy(d).wait_send())
        else:
            for i in range(6):
                sq_copy(g, i).wait_send()
            for d in range(nz):
                when(z < d, lambda: sn_copy(g, d, 0).wait_send())
                when(z > d, lambda: sn_copy(g, d, 1).wait_send())
        sf_copy(g).wait_send()

    def middle_0():
        u_step(1, 1, inside)
        l_fwd(1)

    def middle_1():
        when(inside, lambda: u_own(2))
        l_fwd(2)

    def middle_2():
        u_step(0, 2, at_end)

    tb[...] = jnp.zeros(tb.shape, f32)
    l_start(0)
    u_own(0)
    a_load()
    u_own(1)
    l_fwd(0)
    l_start(1)
    u_step(0, 1)
    when(at_end, lambda: u_own(2))
    l_done(0)
    l_conv(0)
    p_both(0, middle_0)
    pair_add(0, 0)
    pair_add(0, 1)
    l_start(2)
    l_done(1)
    l_conv(1)
    u_step(0, 2, inside)
    p_both(1, middle_1)
    pair_add(1, 0)
    pair_add(1, 1)
    line_t(0, 1)
    u_step(1, 2, inside)
    l_done(2)
    l_conv(2)
    p_both(2, middle_2)
    u_from_ends(2)
    u_step(0, 3)
    u_done(0)
    u_conv(0)
    q_comp(0)
    line_t(0, 2)
    u_from_inside(2)
    u_step(1, 1, at_end)
    u_step(1, 2, at_end)
    u_step(1, 3)
    u_done(1)
    u_conv(1)
    y_relay(0)
    line_t(1, 1)
    q_comp(1)
    when(inside, lambda: line_take(0))
    u_step(2, 2, inside)
    pair_add(2, 0)
    pair_add(2, 1)
    when(at_end, lambda: line_take(0))
    n_sent(0)
    x_out(0)
    y_end(0)
    corner_first()
    step_sums(1)
    s_pair(0)
    y_relay(1)
    s_add(0)
    line_t(1, 2)
    u_step(2, 1, at_end)
    u_step(2, 2, at_end)
    u_step(2, 3)
    u_done(2)
    u_conv(2)
    y_sent(0)
    q_part(2, 0, 3)
    line_t(2, 1)
    s_relay(0)
    line_take(1)
    x_out(1)
    y_end(1)
    step_corner(1)
    n_sent(1)
    step_sums(2)
    s_pair(1)
    line_t(2, 2)
    s_turn(0)
    q_part(2, 3, q_count)
    s_add(1)
    line_take(2)
    x_out(2)
    step_corner(2)
    p_copy(2, 0).wait_send()
    p_copy(2, 1).wait_send()
    put(keep[0], 2, 0)
    s_pair(2)
    s_line(0, 1)
    s_relay(1)
    s_add(2)
    y_relay(2)
    y_own(2)
    s_turn(1)
    s_turn(2)
    s_line(0, 2)
    s_line(1, 1)
    s_line(1, 2)
    s_last(0)
    s_last(2)
    s_last(1)
    s_out(0)
    y_end(2)
    s_out(2)
    s_out(1)

    for s in range(supers):
        x_leave(s).wait()
        y_leave(s).wait()
        for i in range(groups[s]):
            c_leave(s, i).wait()
        for i in range(6):
            l_copy(s, i).wait_send()
        for zs in range(nz):
            for own in (True, False):
                mine = (z == zs) if own else (z != zs)

                @pl.when(mine)
                def _(s=s, zs=zs, own=own):
                    u_copy(s, zs, 2, own).wait_send()

            when((z >= zs) & has_up, lambda s=s, zs=zs: u_copy(s, zs, 0, False).wait_send())
            when((z <= zs) & has_down, lambda s=s, zs=zs: u_copy(s, zs, 1, False).wait_send())
    n_sent(2)
    y_sent(1)
    y_sent(2)
    s_sent(0)
    s_sent(1)
    s_sent(2)


def part_u_is_half(width, prow, pcol):
    return 2 * (width // pcol) == width // prow and (width // prow) % 48 == 0


def fits(shape):
    supers, width, blk, prow, pcol, rows_here, cols_here, slab = shape
    return (
        supers == 3 and prow == 4 and pcol % 4 == 0 and blk == 128 and width % blk == 0
        and slab % 64 == 0 and width == slab + 64 and slab % 128 == 64
        and rows_here % 640 == 0 and cols_here % 640 == 0
        and width % (8 * pcol) == 0 and width // prow <= 128
        and part_u_is_half(width, prow, pcol) and 3 * width <= (pcol // 2) * slab
    )


def sweep(shape, anc_inverse, lower, upper, lower_edge, upper_edge, diag_inverse, mask):
    supers, width, blk, prow, pcol, rows_here, cols_here, slab = shape
    nz = pcol // 2
    part_u = width // pcol
    sums = 3 * supers - 2
    vmem, dma = pltpu.VMEM, pltpu.SemaphoreType.DMA
    in_vmem = pl.BlockSpec(memory_space=pltpu.VMEM)
    in_hbm = pl.BlockSpec(memory_space=pl.ANY)
    out = [
        ((supers, slab, width), in_hbm),
        ((supers, slab, width), in_hbm),
        ((supers, part_u, width // prow), in_hbm),
        ((2, supers - 1, part_u, width // prow), in_hbm),
        ((supers, width, cols_here), in_hbm),
        ((supers, width, rows_here), in_hbm),
    ]
    return pl.pallas_call(
        functools.partial(sweep_kernel, (supers, width, blk, prow, nz, rows_here, cols_here, slab)),
        name="sweep",
        out_shape=[jax.ShapeDtypeStruct(dims, f32) for dims, _ in out],
        in_specs=[in_hbm, in_hbm, in_hbm, in_vmem, in_vmem, in_hbm, pl.BlockSpec(memory_space=pltpu.SMEM)],
        out_specs=[spec for _, spec in out],
        scratch_shapes=[
            vmem((rows_here, cols_here), bf16),
            vmem((rows_here, cols_here), bf16),
            vmem((width, cols_here), bf16),
            vmem((width, cols_here), bf16),
            vmem((width, rows_here), bf16),
            vmem((width, rows_here), bf16),
            vmem((2, width, cols_here // 2), f32),
            vmem(((supers + 1) * nz * slab, width), f32),
            vmem((nz * slab, width), f32),
            vmem((2, nz + 1, slab, width), f32),
            vmem((2, cols_here, width), f32),
            vmem((supers, 6, slab // 2, width), f32),
            vmem((supers, width, width), bf16),
            vmem((supers, width, width), bf16),
            vmem((supers - 1, width, width), bf16),
            vmem((supers - 1, width, width), bf16),
            vmem((width, width), bf16),
            vmem((width, width), bf16),
            vmem((2, width, width), f32),
            vmem((prow * width // (2 * prow), width), f32),
            vmem((6, (sums - 1) * width // (4 * prow), width), f32),
            vmem((prow, width // (2 * prow), width), f32),
            vmem((supers, 128, 128), f32),
            vmem((nz, sums * part_u, 128), f32),
            vmem((nz + 1, sums * part_u, 128), f32),
            vmem((sums * part_u, 128), f32),
            vmem((supers, slab, width), f32),
            vmem((supers, slab, width), f32),
            vmem((supers, part_u, width // prow), f32),
            vmem((2, supers - 1, part_u, width // prow), f32),
            dma((2 * nz,)),
            dma((2,)),
            dma,
            dma((supers, 6)),
            dma((supers, 6)),
            dma((supers, nz, 3)),
            dma((supers, nz)),
            dma((supers, nz)),
            dma((supers, 2)),
            dma((supers, 2)),
            dma((supers, nz)),
            dma((supers, nz + 1)),
            dma((supers, 6)),
            dma((supers, 6)),
            dma((supers,)),
            dma((supers,)),
            dma((supers, 6)),
            dma((supers, 6)),
            dma((supers, nz)),
            dma((supers, nz + 1)),
            dma((supers,)),
            dma((supers,)),
            pltpu.SemaphoreType.REGULAR,
            pltpu.SemaphoreType.REGULAR,
            pltpu.SemaphoreType.REGULAR((supers,)),
            dma((2, supers)),
            dma((3, supers)),
        ],
        compiler_params=pltpu.CompilerParams(
            collective_id=0, has_side_effects=True, vmem_limit_bytes=67043328
        ),
    )(anc_inverse, lower, upper, lower_edge, upper_edge, diag_inverse, mask)


def place(x, y, corner, cross):
    arrays = (x, y, corner, cross)
    pieces = [(a, i) for a, array in enumerate(arrays[:2]) for i in range(array.shape[0])] + [(2, None), (3, None)]

    def body(*refs):
        srcs, dsts, kept, (get, put) = refs[:4], refs[4:8], refs[8:12], refs[12:]

        def view(ref, i):
            return ref if i is None else ref.at[i]

        def copies(n):
            a, i = pieces[n]
            src, mid, dst = (view(r[a], i) for r in (srcs, kept, dsts))
            return pltpu.make_async_copy(src, mid, get.at[n]), pltpu.make_async_copy(mid, dst, put.at[n])

        for n in range(len(pieces)):
            copies(n)[0].start()
        for n in range(len(pieces)):
            copies(n)[0].wait()
            copies(n)[1].start()
        for n in range(len(pieces)):
            copies(n)[1].wait()

    return pl.pallas_call(
        body,
        name="place",
        out_shape=[jax.ShapeDtypeStruct(one.shape, f32) for one in arrays],
        in_specs=[pl.BlockSpec(memory_space=pl.ANY)] * 4,
        out_specs=[pl.BlockSpec(memory_space=pl.ANY)] * 4,
        scratch_shapes=[pltpu.VMEM(one.shape, f32) for one in arrays]
        + [pltpu.SemaphoreType.DMA((len(pieces),))] * 2,
    )(*arrays)


def per_device(anc_inverse, lower_anc, upper_anc, lower_edge, upper_edge, diag_inverse, tile_mask):
    rows_here, cols_here = anc_inverse.shape
    prow, pcol = lax.axis_size("row"), lax.axis_size("col")
    supers, width = diag_inverse.shape[0], diag_inverse.shape[1]
    blk = width // tile_mask.shape[2]
    shape = (supers, width, blk, prow, pcol, rows_here, cols_here, cols_here // prow)
    args = (anc_inverse, lower_anc, upper_anc, lower_edge, upper_edge, diag_inverse, tile_mask)
    if not fits(shape):
        return general(*args)
    x, y, corner, cross, _, _ = sweep(
        shape,
        anc_inverse,
        jnp.transpose(lower_anc, (1, 2, 0)),
        jnp.transpose(upper_anc, (1, 2, 0)),
        lower_edge,
        upper_edge,
        diag_inverse,
        jnp.transpose(tile_mask, (0, 2, 1)),
    )
    x, y, corner, cross = place(x, y, corner, cross)
    return (
        jnp.transpose(x, (1, 0, 2)),
        jnp.transpose(y, (1, 0, 2))[None, None],
        jnp.transpose(corner, (0, 2, 1)),
        jnp.transpose(cross, (0, 1, 3, 2)),
    )


precise = lax.Precision.HIGH


def contract(left, right, left_dim, right_dim):
    return lax.dot_general(
        left,
        right,
        (((left_dim,), (right_dim,)), ((), ())),
        precision=precise,
        preferred_element_type=jnp.float32,
    )


def row_major(array):
    return with_layout_constraint(array, Layout(major_to_minor=(0, 1)))


def partner(index, step, count):
    if count & (count - 1) == 0:
        return index ^ step
    return (step - index) % count


def exchange(piece_for, axis):
    count = lax.axis_size(axis)
    index = lax.axis_index(axis)
    got = []
    for step in range(count):
        peer = partner(index, step, count)
        piece = piece_for(peer)
        pairs = [(i, partner(i, step, count)) for i in range(count)]
        if any(i != j for i, j in pairs):
            piece = lax.ppermute(piece, axis, pairs)
        got.append((peer, piece))
    return got


def mask_factor(factor, tile_mask, first_row, first_col, blk):
    rows, supers, cols = factor.shape
    blocks = rows // blk
    window = lax.dynamic_slice_in_dim(tile_mask, first_row // blk, blocks, 1).astype(jnp.float32)
    tile_cols = window.shape[2]
    tile_of_col = (first_col + jnp.arange(cols)) // blk
    pick = (tile_of_col[None, :] == jnp.arange(tile_cols)[:, None]).astype(jnp.float32)
    chosen = sum(window[:, :, t, None] * pick[t] for t in range(tile_cols))
    chosen = jnp.transpose(chosen, (1, 0, 2))
    masked = factor.reshape(blocks, blk, supers, cols) * chosen[:, None]
    return jnp.transpose(masked.reshape(rows, supers, cols), (1, 2, 0))


def general(anc_inverse, lower_anc, upper_anc, lower_edge, upper_edge, diag_inverse, tile_mask):
    rows_here, cols_here = anc_inverse.shape
    prow = lax.axis_size("row")
    pcol = lax.axis_size("col")
    supers, width = diag_inverse.shape[0], diag_inverse.shape[1]
    blk = width // tile_mask.shape[2]
    row = lax.axis_index("row")
    col = lax.axis_index("col")
    part_lower = width // prow
    part_upper = width // pcol

    upper_t = mask_factor(upper_anc, tile_mask, row * rows_here, col * part_upper, blk)
    lower_t = mask_factor(lower_anc, tile_mask, col * cols_here, row * part_lower, blk)

    upper_t = lax.all_gather(upper_t, "col", axis=0)
    lower_full = jnp.zeros((supers, prow, part_lower, cols_here), jnp.float32)
    for peer, piece in exchange(lambda _: lower_t, "row"):
        lower_full = lax.dynamic_update_slice(lower_full, piece[:, None], (0, peer, 0, 0))
    lower_full = lower_full.reshape(supers, width, cols_here)
    lower_comb = [-lower_full[0]]
    for s in range(1, supers):
        lower_comb.append(-lower_full[s] - contract(lower_edge[s - 1], lower_comb[-1], 0, 0))
    cols_part = [row_major(contract(anc_inverse, one, 1, 1)) for one in lower_comb]
    cols_mine = [lax.psum_scatter(one, "col", scatter_dimension=0, tiled=True) for one in cols_part]

    upper_full = [upper_t[:, s].reshape(width, rows_here) for s in range(supers)]
    upper_comb = [-upper_full[0]]
    for s in range(1, supers):
        upper_comb.append(-upper_full[s] - contract(upper_edge[s - 1], upper_comb[-1], 1, 0))
    rows_part = [row_major(contract(anc_inverse, one, 0, 1)) for one in upper_comb]

    first = jnp.logical_and(row == 0, col == 0)
    corner = []
    cross_cols = []
    cross_rows = []
    for s in range(supers):
        upper_here = contract(upper_full[s], cols_part[s], 1, 0)
        now = jnp.where(first, diag_inverse[s], 0.0) - upper_here
        if s > 0:
            upper_prev = contract(upper_full[s], cols_part[s - 1], 1, 0)
            lower_prev = lax.dot_general(
                rows_part[s - 1],
                lower_full[s],
                (((0,), (1,)), ((), ())),
                precision=precise,
                preferred_element_type=jnp.float32,
            )
            cross_col = -(lower_prev + contract(corner[-1], lower_edge[s - 1], 1, 0))
            cross_row = -(upper_prev + contract(upper_edge[s - 1], corner[-1], 1, 0))
            now = now - contract(upper_edge[s - 1], cross_col, 1, 0)
            cross_cols.append(cross_col)
            cross_rows.append(cross_row)
        corner.append(now)
    sums = jnp.stack(corner + cross_cols + cross_rows)
    count = sums.shape[0]

    row_slab = cols_here // prow
    rows_mine = [
        sum(
            piece
            for _, piece in exchange(
                lambda peer: lax.dynamic_slice_in_dim(one, peer * row_slab, row_slab, 0), "row"
            )
        )
        for one in rows_part
    ]
    sums, rows_mine = lax.optimization_barrier((sums, rows_mine))
    sums = sum(
        piece
        for _, piece in exchange(
            lambda peer: lax.dynamic_slice_in_dim(sums, peer * part_lower, part_lower, 1), "row"
        )
    )
    sums = jnp.transpose(sums.reshape(count * part_lower, width))
    sums, cols_mine = lax.optimization_barrier((sums, cols_mine))
    sums = lax.psum_scatter(sums, "col", scatter_dimension=0, tiled=True)
    sums = jnp.transpose(sums).reshape(count, part_lower, part_upper)

    x_blocks = jnp.stack(cols_mine, axis=1)
    y_blocks = jnp.stack(rows_mine, axis=1)[None, None]
    z_blocks = sums[:supers]
    cross_blocks = sums[supers:].reshape(2, supers - 1, part_lower, part_upper)
    return (x_blocks, y_blocks, z_blocks, cross_blocks)


def solution(mesh):
    return jax.shard_map(
        per_device,
        mesh=mesh,
        in_specs=(
            P("row", "col"),
            P("col", None, "row"),
            P("row", None, "col"),
            P(),
            P(),
            P(),
            P(),
        ),
        out_specs=(
            P(("row", "col"), None, None),
            P("col", "row", None, None, None),
            P(None, "row", "col"),
            P(None, None, "row", "col"),
        ),
        check_vma=False,
    )
```

```python
import functools

import jax
import jax.numpy as jnp
from jax import lax
from jax.experimental import pallas as pl
from jax.experimental.pallas import tpu as pltpu
from jax.experimental.layout import Layout, with_layout_constraint
from jax.sharding import PartitionSpec as P


f32 = jnp.float32
bf16 = jnp.bfloat16


def halves(value):
    hi = value.astype(bf16)
    return hi, (value - hi.astype(f32)).astype(bf16)


def dot3(left, right, left_dim, right_dim):
    dims = (((left_dim,), (right_dim,)), ((), ()))

    def one(a, b):
        return lax.dot_general(a, b, dims, preferred_element_type=f32)

    return one(left[0], right[0]) + (one(left[0], right[1]) + one(left[1], right[0]))


def sweep_kernel(
    shape,
    a_ref, l_ref, u_ref, e_ref, f_ref, d_ref, mask_ref,
    x_hbm, y_hbm, z_hbm, c_hbm, lbuf, ubuf,
    ah, al, lh, ll, uh, ul, stage, pb, pr, ln, qb, yr, uw_h, uw_l, lw_h, lw_l, win_h, win_l, keep,
    sp2, sq, sqd, tb, zb, zl, zf, xo, yo, zo, co,
    a_sem, st_sem, d_sem, l_send, l_recv, u_send, u_recv, up_recv, p_send, p_recv, n_send, n_recv,
    y_send, y_recv, sp_send, sp_recv, sq_send, sq_recv, sn_send, sn_recv, sf_send, sf_recv,
    free_up, free_down, free_pair, o_sem, c_sem,
):
    supers, width, blk, prow, nz, rows_here, cols_here, slab = shape
    pcol = 2 * nz
    part_l, part_u = width // prow, width // pcol
    row = lax.axis_index("row")
    col = lax.axis_index("col")
    z, k = col // 2, col % 2
    other = 1 - k
    y, x = row // 2, row % 2
    row_x, row_y, row_d = y * 2 + 1 - x, (1 - y) * 2 + x, (1 - y) * 2 + 1 - x
    to_x, to_y, to_d = {"row": row_x}, {"row": row_y}, {"row": row_d}
    to_pair = {"col": col + 1 - 2 * k}
    up, down = {"col": col + 2}, {"col": col - 2}
    has_up, has_down = z < nz - 1, z > 0
    at_end, inside = (z == 0) | (z == nz - 1), (z > 0) & (z < nz - 1)

    def when(cond, body):
        pl.when(cond)(body)

    def rc(src, dst, ss, rs, dev):
        return pltpu.make_async_remote_copy(
            src_ref=src, dst_ref=dst, send_sem=ss, recv_sem=rs,
            device_id=dev, device_id_type=pl.DeviceIdType.MESH,
        )

    barrier = pltpu.get_barrier_semaphore()

    def greet(dev):
        pl.semaphore_signal(barrier, inc=1, device_id=dev, device_id_type=pl.DeviceIdType.MESH)

    for dev in (to_x, to_y, to_d, to_pair):
        greet(dev)
    for there in range(nz):
        when(z != there, lambda: greet({"col": 2 * there + k}))
    pl.semaphore_wait(barrier, 4 + nz - 1)

    half_l = part_l // 2

    def l_piece(s, r, h):
        return lbuf.at[s, pl.ds(pl.multiple_of(r * part_l + h * half_l, 8), half_l)]

    def l_own(s, h):
        return l_ref.at[s, pl.ds(h * half_l, half_l)]

    def l_copy(s, i):
        src, dst, dev = (
            (l_own(s, 1), l_piece(s, row, 1), to_x),
            (l_own(s, 0), l_piece(s, row, 0), to_y),
            (l_own(s, 0), l_piece(s, row, 0), to_x),
            (l_own(s, 1), l_piece(s, row, 1), to_y),
            (l_piece(s, row_x, 1), l_piece(s, row_x, 1), to_y),
            (l_piece(s, row_y, 0), l_piece(s, row_y, 0), to_x),
        )[i]
        return rc(src, dst, l_send.at[s, i], l_recv.at[s, i], dev)

    def l_take(s, i):
        r, h = ((row_x, 1), (row_y, 0), (row_x, 0), (row_y, 1), (row_d, 1), (row_d, 0))[i]
        rc(l_piece(s, r, h), l_piece(s, r, h), l_send.at[s, i], l_recv.at[s, i], to_pair).wait_recv()

    def l_start(s):
        for i in range(4):
            l_copy(s, i).start()

    def l_fwd(s):
        l_take(s, 0)
        l_copy(s, 4).start()
        l_take(s, 1)
        l_copy(s, 5).start()

    def l_done(s):
        for i in range(2, 6):
            l_take(s, i)

    def u_piece(s, c):
        return ubuf.at[s, pl.ds(pl.multiple_of(c * part_u, 8), part_u)]

    def u_copy(s, zs, way, own):
        mine = u_piece(s, zs * 2 + k)
        src = u_ref.at[s] if own else mine
        recv = up_recv if way == 2 else u_recv
        return rc(src, mine, u_send.at[s, zs, way], recv.at[s, zs], (up, down, to_pair)[way])

    def u_own(s):
        when(has_up, lambda: u_copy(s, z, 0, True).start())
        when(has_down, lambda: u_copy(s, z, 1, True).start())
        u_copy(s, z, 2, True).start()

    def u_low(s, t, cond):
        @pl.when((z >= t) & cond)
        def _():
            u_copy(s, z - t, 1, False).wait_recv()
            when(has_up, lambda: u_copy(s, z - t, 0, False).start())
            u_copy(s, z - t, 2, False).start()

    def u_high(s, t, cond):
        @pl.when((z + t < nz) & cond)
        def _():
            u_copy(s, z + t, 0, False).wait_recv()
            when(has_down, lambda: u_copy(s, z + t, 1, False).start())
            u_copy(s, z + t, 2, False).start()

    def u_step(s, t, cond=None):
        cond = z >= 0 if cond is None else cond
        u_low(s, t, cond)
        u_high(s, t, cond)

    def u_from_ends(s):
        u_low(s, 1, inside & (z == 1))
        u_high(s, 1, inside & (z == nz - 2))

    def u_from_inside(s):
        u_low(s, 1, inside & (z > 1))
        u_high(s, 1, inside & (z < nz - 2))

    def u_done(s):
        for zs in range(nz):
            piece = u_piece(s, zs * 2 + other)
            rc(piece, piece, u_send.at[s, zs, 2], up_recv.at[s, zs], to_pair).wait_recv()

    lanes = stage.shape[2]
    tiles = lanes // blk

    def load(buf, own_ref, s, count, me, part, q):
        here = pl.ds(q * lanes, lanes)

        @pl.loop(0, count)
        def _(p):
            there = stage.at[q % 2, pl.ds(pl.multiple_of(p * part, 8), part)]

            @pl.when(p != me)
            def _():
                pltpu.make_async_copy(
                    buf.at[s, pl.ds(pl.multiple_of(p * part, 8), part), here], there, st_sem.at[q % 2]
                ).start()

            @pl.when(p == me)
            def _():
                pltpu.make_async_copy(own_ref.at[s, :, here], there, st_sem.at[q % 2]).start()

    def convert(buf, own_ref, s, count, me, part, total, first_tile, out_h, out_l):
        load(buf, own_ref, s, count, me, part, 0)
        for q in range(total // lanes):
            if q + 1 < total // lanes:
                load(buf, own_ref, s, count, me, part, q + 1)
            pltpu.make_async_copy(stage.at[q % 2], stage.at[q % 2], st_sem.at[q % 2]).wait()

            @pl.loop(0, tiles)
            def _(t):
                src = pl.ds(pl.multiple_of(t * blk, 128), blk)
                dst = pl.ds(pl.multiple_of(q * lanes + t * blk, 128), blk)
                for j in range(width // blk):
                    keep_it = mask_ref[s, j, first_tile + q * tiles + t].astype(f32)
                    rows = pl.ds(j * blk, blk)
                    hi, lo = halves(stage[q % 2, rows, src] * keep_it)
                    out_h[rows, dst] = hi
                    out_l[rows, dst] = lo

    def window(index):
        start = index * slab
        odd = start % 128
        return pl.ds(pl.multiple_of(start - odd, 128), width), odd

    def l_conv(s):
        convert(lbuf, l_ref, s, prow, row, part_l, cols_here, col * (cols_here // blk), lh, ll)
        if s > 0:
            where, _ = window(row)
            lw_h[s - 1] = lh[:, where]
            lw_l[s - 1] = ll[:, where]

    def u_conv(s):
        convert(ubuf, u_ref, s, pcol, col, part_u, rows_here, row * (rows_here // blk), uh, ul)
        where, _ = window(col)
        uw_h[s] = uh[:, where]
        uw_l[s] = ul[:, where]

    a_lanes = 256
    a_cols = cols_here // a_lanes
    a_slots = 2 * nz

    def a_copy(n, slot):
        i, j = n // a_cols, n % a_cols
        return pltpu.make_async_copy(
            a_ref.at[pl.ds(pl.multiple_of(i * slab, 8), slab), pl.ds(pl.multiple_of(j * a_lanes, 128), a_lanes)],
            pb.at[pl.ds(pl.multiple_of(slot * slab, 64), slab), pl.ds(0, a_lanes)],
            a_sem.at[slot],
        )

    def a_load():
        count = (rows_here // slab) * a_cols
        for n in range(a_slots - 1):
            a_copy(n, n).start()

        @pl.loop(0, count)
        def _(n):
            slot = n % a_slots

            @pl.when(n + a_slots - 1 < count)
            def _():
                a_copy(n + a_slots - 1, (n + a_slots - 1) % a_slots).start()

            a_copy(n, slot).wait()
            i, j = n // a_cols, n % a_cols
            across = pl.ds(pl.multiple_of(j * a_lanes, 128), a_lanes)
            step = 64
            for b in range(slab // step):
                hi, lo = halves(pb[pl.ds(pl.multiple_of(slot * slab + b * step, 64), step), pl.ds(0, a_lanes)])
                down_to = pl.ds(pl.multiple_of(i * slab + b * step, 64), step)
                ah[down_to, across] = hi
                al[down_to, across] = lo

    hz = nz // 2
    h_rows = rows_here // 2

    def far(i):
        flip = (z < hz).astype(jnp.int32)
        return (flip + i) % 2

    def p_rows(s, d, n=1):
        return pl.ds(pl.multiple_of((s * nz + d) * slab, 64), n * slab)

    def p_copy(s, hh):
        return rc(
            pb.at[p_rows(supers, hh * hz, hz)], pr.at[p_rows(0, hh * hz, hz)],
            p_send.at[s, hh], p_recv.at[s, hh], to_pair,
        )

    def p_both(s, middle):
        @pl.loop(0, 2)
        def _(i):
            when(i == 1, middle)
            hh = far(i)
            if s > 0:
                p_copy(s - 1, hh).wait_send()
            rows = pl.ds(pl.multiple_of(hh * h_rows, 128), h_rows)
            got = dot3((lh[...], ll[...]), (ah[rows], al[rows]), 1, 1).T
            for q in range(2 * hz):
                spot = jnp.where(k == q % 2, s, supers)
                pb[p_rows(spot, hh * hz + q // 2)] = got[q * slab : (q + 1) * slab]
            if s > 0:
                when(i == 0, lambda: pl.semaphore_wait(free_pair.at[s - 1], 1))
            p_copy(s, hh).start()

    def n_copy(s, d, way):
        slot = d + 1 - way
        return rc(pb.at[p_rows(s, d)], ln.at[s % 2, slot], n_send.at[s, d], n_recv.at[s, slot], (up, down)[way])

    def n_take(s, d, slot):
        rc(ln.at[s % 2, slot], ln.at[s % 2, slot], n_send.at[s, d], n_recv.at[s, slot], to_pair).wait_recv()
        pb[p_rows(s, d)] = pb[p_rows(s, d)] + ln[s % 2, slot]

    def tell(sem, dev):
        pl.semaphore_signal(sem, inc=1, device_id=dev, device_id_type=pl.DeviceIdType.MESH)

    def line_wait():
        when(has_up, lambda: pl.semaphore_wait(free_up, 1))
        when(has_down, lambda: pl.semaphore_wait(free_down, 1))

    def pair_add(s, i):
        if s == 2 and i == 0:
            when(at_end, line_wait)
        hh = far(i)
        p_copy(s, hh).wait_recv()
        for q in range(hz):
            d = hh * hz + q
            pb[p_rows(s, d)] = pb[p_rows(s, d)] + pr[p_rows(0, d)]
        if i == 1:
            tell(free_pair.at[s], to_pair)
        lo, hi = (1 - i) * hz, (2 - i) * hz

        @pl.when(z == 0)
        def _():
            for d in reversed(range(max(lo, 1), hi)):
                n_copy(s, d, 0).start()

        lo, hi = i * hz, (i + 1) * hz

        @pl.when(z == nz - 1)
        def _():
            for d in range(lo, min(hi, nz - 1)):
                n_copy(s, d, 1).start()

    def line_t(s, t):
        zb_ = nz - 1 - z
        if s == 2 and t == 1:
            when(inside, line_wait)

        @pl.when((z >= 1) & (z <= t))
        def _():
            d = z + (nz - 1 - t)
            n_take(s, d, d + 1)
            n_copy(s, d, 0).start()

        @pl.when((zb_ >= 1) & (zb_ <= t))
        def _():
            d = z - (nz - 1 - t)
            n_take(s, d, d)
            n_copy(s, d, 1).start()

    def line_take(s):
        when(has_down, lambda: n_take(s, z, z + 1))
        when(has_up, lambda: n_take(s, z, z))
        if s == 0:
            when(has_down, lambda: tell(free_up, down))
            when(has_up, lambda: tell(free_down, up))

    def x_leave(s):
        return pltpu.make_async_copy(xo.at[s], x_hbm.at[s], o_sem.at[0, s])

    def y_leave(s):
        return pltpu.make_async_copy(yo.at[s], y_hbm.at[s], o_sem.at[1, s])

    def x_out(s):
        total = -pb[p_rows(s, z)]
        if s > 0:
            total = total - dot3(halves(xo[s - 1]), halves(e_ref[s - 1]), 1, 0)
        xo[s] = total
        x_leave(s).start()

    def n_sent(s):
        for d in range(nz):
            when(z < d, lambda d=d: n_copy(s, d, 0).wait_send())
            when(z > d, lambda d=d: n_copy(s, d, 1).wait_send())

    half_y = slab // 2
    q_cols = 256

    def q_rows(r, h):
        return pl.ds(pl.multiple_of(r * slab + h * half_y, 8), half_y)

    def q_slab(s, r, h):
        return qb.at[s % 2, q_rows(r, h)]

    def y_copy(s, i):
        src, dev = (
            (q_slab(s, row_x, 0), to_x),
            (q_slab(s, row_d, 0), to_x),
            (q_slab(s, row_y, 1), to_y),
            (q_slab(s, row_d, 1), to_y),
            (q_slab(s, row_y, 0), to_y),
            (q_slab(s, row_x, 1), to_x),
        )[i]
        return rc(src, yr.at[s, i], y_send.at[s, i], y_recv.at[s, i], dev)

    q_count = cols_here // q_cols

    def q_part(s, start, stop):
        @pl.loop(start, stop)
        def _(i):
            @pl.when(i == 2)
            def _():
                y_copy(s, 1).start()
                y_copy(s, 3).start()

            across = pl.ds(pl.multiple_of((row_d + i) % q_count * q_cols, 128), q_cols)
            got = dot3((uh[...], ul[...]), (ah[:, across], al[:, across]), 1, 0)
            qb[s % 2, across] = got.T

    def y_own(s):
        y_copy(s, 0).start()
        y_copy(s, 2).start()

    def q_comp(s):
        q_part(s, 0, q_count)
        y_own(s)

    def y_relay(s):
        y_copy(s, 1).wait_recv()
        qb[s % 2, q_rows(row_y, 0)] = qb[s % 2, q_rows(row_y, 0)] + yr[s, 1]
        y_copy(s, 4).start()
        y_copy(s, 3).wait_recv()
        qb[s % 2, q_rows(row_x, 1)] = qb[s % 2, q_rows(row_x, 1)] + yr[s, 3]
        y_copy(s, 5).start()

    def y_end(s):
        for i in (0, 2, 4, 5):
            y_copy(s, i).wait_recv()
        for h, (i, j) in enumerate(((0, 4), (2, 5))):
            yo[s, pl.ds(h * half_y, half_y)] = -(qb[s % 2, q_rows(row, h)] + yr[s, i] + yr[s, j])
        if s > 0:
            yo[s] = yo[s] - dot3(halves(yo[s - 1]), halves(f_ref[s - 1]), 1, 1)
        y_leave(s).start()

    def y_sent(s):
        for i in range(6):
            y_copy(s, i).wait_send()

    first = ((row == 0) & (col == 0)).astype(f32)

    def fill(value, index):
        _, odd = window(index)
        hi, lo = halves(value)
        win_h[...] = jnp.zeros(win_h.shape, bf16)
        win_l[...] = jnp.zeros(win_l.shape, bf16)
        rows = pl.ds(pl.multiple_of(odd, 64), slab)
        win_h[rows] = hi
        win_l[rows] = lo

    def with_upper(s):
        return dot3((uw_h[s], uw_l[s]), (win_h[...], win_l[...]), 1, 0)

    def d_copy(s):
        return pltpu.make_async_copy(d_ref.at[s], keep.at[0], d_sem)

    def put(value, g, i):
        n = groups[g]
        for r in range(prow):
            for h in range(2):
                at = base(g) + ((h * prow + r) * n + i) * half_l
                pb[pl.ds(at, half_l)] = value[r * part_l + h * half_l : r * part_l + (h + 1) * half_l]

    groups = (3, 3, 1)

    def base(g):
        return (0, nz * slab, supers * nz * slab)[g]

    def corner_first():
        d_copy(0).start()
        fill(xo[0], col)
        got = with_upper(0)
        d_copy(0).wait()
        keep[0] = keep[0] * first - got

    def step_sums(s):
        edge_f = halves(f_ref[s - 1])
        corner = keep[0]
        put(corner, s - 1, 0)
        corner = halves(corner)
        fill(xo[s - 1], col)
        put(-(with_upper(s) + dot3(edge_f, corner, 1, 0)), s - 1, 2)
        fill(yo[s - 1], row)
        turned = dot3((lw_h[s - 1], lw_l[s - 1]), (win_h[...], win_l[...]), 1, 0)
        keep[1] = -(turned.T + dot3(corner, halves(e_ref[s - 1]), 1, 0))
        put(keep[1], s - 1, 1)

    def step_corner(s):
        d_copy(s).start()
        fill(xo[s], col)
        got = with_upper(s) + dot3(halves(f_ref[s - 1]), halves(keep[1]), 1, 0)
        d_copy(s).wait()
        keep[0] = keep[0] * first - got

    def s_rows(g, h, r=0, a=0, count=None):
        n = groups[g]
        at = base(g) + (h * prow + r) * n * half_l + a * n * half_l // 2
        return pl.ds(pl.multiple_of(at, 8), count or n * half_l // 2)

    def sp_copy(g):
        size = prow * groups[g] * half_l
        into = sp2 if g == 2 else pr.at[pl.ds(g * size, size)]
        return rc(pb.at[s_rows(g, other, count=size)], into, sp_send.at[g], sp_recv.at[g], to_pair)

    def s_pair(g):
        if g == 0:
            pl.semaphore_wait(free_pair.at[supers - 1], 1)
        sp_copy(g).start()

    def sq_copy(g, i):
        size = groups[g] * half_l // 2
        r, a, dev = (
            (row_x, 0, to_x), (row_d, 0, to_x), (row_y, 1, to_y), (row_d, 1, to_y), (row_y, 0, to_y), (row_x, 1, to_x),
        )[i]
        into = sq.at[i, pl.ds(sum(groups[:g]) * half_l // 2, size)]
        return rc(pb.at[s_rows(g, k, r, a)], into, sq_send.at[g, i], sq_recv.at[g, i], dev)

    def sq_got(g, i):
        return sq[i, pl.ds(sum(groups[:g]) * half_l // 2, groups[g] * half_l // 2)]

    def sd_copy(r, me, dev):
        return rc(
            pb.at[s_rows(2, k, r, 0, groups[2] * half_l)], sqd.at[me], sq_send.at[2, r], sq_recv.at[2, me], dev
        )

    rows_to = ((row_x, to_x), (row_y, to_y), (row_d, to_d))

    def s_add(g):
        size = prow * groups[g] * half_l
        sp_copy(g).wait_recv()
        mine = s_rows(g, k, count=size)
        pb[mine] = pb[mine] + (sp2[...] if g == 2 else pr[pl.ds(g * size, size)])
        if g == 2:
            for r, dev in rows_to:
                sd_copy(r, row, dev).start()
        else:
            for i in (1, 3, 0, 2):
                sq_copy(g, i).start()

    def s_relay(g):
        for i, r, a, j in ((1, row_y, 0, 4), (3, row_x, 1, 5)):
            sq_copy(g, i).wait_recv()
            there = s_rows(g, k, r, a)
            pb[there] = pb[there] + sq_got(g, i)
            sq_copy(g, j).start()

    def z_rows(g):
        return pl.ds(sum(groups[:g]) * half_l, groups[g] * half_l)

    def sn_copy(g, d, way):
        slot = d + 1 - way
        return rc(
            zb.at[d, z_rows(g)], zl.at[slot, z_rows(g)], sn_send.at[g, d], sn_recv.at[g, slot], (up, down)[way]
        )

    def sz_copy(d):
        rows = z_rows(2)
        return rc(zb.at[d, rows], zl.at[z, rows], sn_send.at[2, d], sn_recv.at[2, z], {"col": 2 * d + k})

    def s_turn(g):
        n = groups[g]
        if g == 2:
            there = s_rows(2, k, row, 0, n * half_l)
            for r, dev in rows_to:
                sd_copy(r, r, dev).wait_recv()
            pb[there] = (pb[there] + sqd[row_x]) + (sqd[row_y] + sqd[row_d])
        else:
            for i in (0, 2, 4, 5):
                sq_copy(g, i).wait_recv()
            for a, (i, j) in enumerate(((0, 4), (2, 5))):
                there = s_rows(g, k, row, a)
                pb[there] = pb[there] + sq_got(g, i) + sq_got(g, j)
        at = base(g) + (k * prow + row) * n * half_l
        total = pb[pl.ds(pl.multiple_of(at, 8), n * half_l)]
        wide = 2 * part_u
        for d in range(nz):
            turned = total if d == 0 else pltpu.roll(total, width - d * wide, 1)
            zb[d, z_rows(g)] = turned[:, :128]
        if g == 2:
            for d in range(nz):
                when(z != d, lambda: sz_copy(d).start())
            return

        @pl.when(z == 0)
        def _():
            for d in reversed(range(1, nz)):
                sn_copy(g, d, 0).start()

        @pl.when(z == nz - 1)
        def _():
            for d in range(nz - 1):
                sn_copy(g, d, 1).start()

    def s_take(g, d, slot):
        rows = z_rows(g)
        rc(zl.at[slot, rows], zl.at[slot, rows], sn_send.at[g, d], sn_recv.at[g, slot], to_pair).wait_recv()
        zb[d, rows] = zb[d, rows] + zl[slot, rows]

    def s_line(g, t):
        zb_ = nz - 1 - z

        @pl.when((z >= 1) & (z <= t))
        def _():
            d = z + (nz - 1 - t)
            s_take(g, d, d + 1)
            sn_copy(g, d, 0).start()

        @pl.when((zb_ >= 1) & (zb_ <= t))
        def _():
            d = z - (nz - 1 - t)
            s_take(g, d, d)
            sn_copy(g, d, 1).start()

    def sf_copy(g):
        return rc(zb.at[z, z_rows(g)], zf.at[z_rows(g)], sf_send.at[g], sf_recv.at[g], to_pair)

    def s_last(g):
        if g == 2:
            for there in range(nz):
                when(z != there, lambda: s_take(g, z, there))
        else:
            when(has_down, lambda: s_take(g, z, z + 1))
            when(has_up, lambda: s_take(g, z, z))
        sf_copy(g).start()

    def c_leave(g, i):
        src, dst = (zo.at[g], z_hbm.at[g]) if i == 0 else (co.at[i - 1, g], c_hbm.at[i - 1, g])
        return pltpu.make_async_copy(src, dst, c_sem.at[i, g])

    def s_out(g):
        sf_copy(g).wait_recv()
        mine, theirs = zb[z, z_rows(g)], zf[z_rows(g)]
        for h, both in enumerate((jnp.where(k == 0, mine, theirs), jnp.where(k == 0, theirs, mine))):
            both = jnp.where(k == 0, both, pltpu.roll(both, 128 - part_u, 1))
            for i in range(groups[g]):
                tb[i, pl.ds(h * half_l, half_l)] = both[i * half_l : (i + 1) * half_l]
        for i in range(groups[g]):
            value = tb[i].T[:part_u, :part_l]
            if i == 0:
                zo[g] = value
            else:
                co[i - 1, g] = value
            c_leave(g, i).start()

    def s_sent(g):
        sp_copy(g).wait_send()
        if g == 2:
            for r, dev in rows_to:
                sd_copy(r, row, dev).wait_send()
            for d in range(nz):
                when(z != d, lambda: sz_copy(d).wait_send())
        else:
            for i in range(6):
                sq_copy(g, i).wait_send()
            for d in range(nz):
                when(z < d, lambda: sn_copy(g, d, 0).wait_send())
                when(z > d, lambda: sn_copy(g, d, 1).wait_send())
        sf_copy(g).wait_send()

    def middle_0():
        u_step(1, 1, inside)
        l_fwd(1)

    def middle_1():
        when(inside, lambda: u_own(2))
        l_fwd(2)

    def middle_2():
        u_step(0, 2, at_end)

    tb[...] = jnp.zeros(tb.shape, f32)
    l_start(0)
    u_own(0)
    a_load()
    u_own(1)
    l_fwd(0)
    l_start(1)
    u_step(0, 1)
    when(at_end, lambda: u_own(2))
    l_done(0)
    l_conv(0)
    p_both(0, middle_0)
    pair_add(0, 0)
    pair_add(0, 1)
    l_start(2)
    l_done(1)
    l_conv(1)
    u_step(0, 2, inside)
    p_both(1, middle_1)
    pair_add(1, 0)
    pair_add(1, 1)
    line_t(0, 1)
    u_step(1, 2, inside)
    l_done(2)
    l_conv(2)
    p_both(2, middle_2)
    u_from_ends(2)
    u_step(0, 3)
    u_done(0)
    u_conv(0)
    q_comp(0)
    line_t(0, 2)
    u_from_inside(2)
    u_step(1, 1, at_end)
    u_step(1, 2, at_end)
    u_step(1, 3)
    u_done(1)
    u_conv(1)
    y_relay(0)
    line_t(1, 1)
    q_comp(1)
    when(inside, lambda: line_take(0))
    u_step(2, 2, inside)
    pair_add(2, 0)
    pair_add(2, 1)
    when(at_end, lambda: line_take(0))
    n_sent(0)
    x_out(0)
    y_end(0)
    corner_first()
    step_sums(1)
    s_pair(0)
    y_relay(1)
    s_add(0)
    line_t(1, 2)
    u_step(2, 1, at_end)
    u_step(2, 2, at_end)
    u_step(2, 3)
    u_done(2)
    u_conv(2)
    y_sent(0)
    q_part(2, 0, 3)
    line_t(2, 1)
    s_relay(0)
    y_end(1)
    line_take(1)
    x_out(1)
    step_corner(1)
    n_sent(1)
    step_sums(2)
    s_pair(1)
    line_t(2, 2)
    s_turn(0)
    q_part(2, 3, q_count)
    s_add(1)
    line_take(2)
    x_out(2)
    step_corner(2)
    p_copy(2, 0).wait_send()
    p_copy(2, 1).wait_send()
    put(keep[0], 2, 0)
    s_pair(2)
    s_line(0, 1)
    s_relay(1)
    s_add(2)
    y_relay(2)
    y_own(2)
    s_turn(1)
    s_turn(2)
    s_line(0, 2)
    s_line(1, 1)
    s_line(1, 2)
    s_last(0)
    s_last(2)
    s_last(1)
    s_out(0)
    y_end(2)
    s_out(2)
    s_out(1)

    for s in range(supers):
        x_leave(s).wait()
        y_leave(s).wait()
        for i in range(groups[s]):
            c_leave(s, i).wait()
        for i in range(6):
            l_copy(s, i).wait_send()
        for zs in range(nz):
            for own in (True, False):
                mine = (z == zs) if own else (z != zs)

                @pl.when(mine)
                def _(s=s, zs=zs, own=own):
                    u_copy(s, zs, 2, own).wait_send()

            when((z >= zs) & has_up, lambda s=s, zs=zs: u_copy(s, zs, 0, False).wait_send())
            when((z <= zs) & has_down, lambda s=s, zs=zs: u_copy(s, zs, 1, False).wait_send())
    n_sent(2)
    y_sent(1)
    y_sent(2)
    s_sent(0)
    s_sent(1)
    s_sent(2)


def part_u_is_half(width, prow, pcol):
    return 2 * (width // pcol) == width // prow and (width // prow) % 48 == 0


def fits(shape):
    supers, width, blk, prow, pcol, rows_here, cols_here, slab = shape
    return (
        supers == 3 and prow == 4 and pcol % 4 == 0 and blk == 128 and width % blk == 0
        and slab % 64 == 0 and width == slab + 64 and slab % 128 == 64
        and rows_here % 640 == 0 and cols_here % 640 == 0
        and width % (8 * pcol) == 0 and width // prow <= 128
        and part_u_is_half(width, prow, pcol) and 3 * width <= (pcol // 2) * slab
    )


def sweep(shape, anc_inverse, lower, upper, lower_edge, upper_edge, diag_inverse, mask):
    supers, width, blk, prow, pcol, rows_here, cols_here, slab = shape
    nz = pcol // 2
    part_u = width // pcol
    sums = 3 * supers - 2
    vmem, dma = pltpu.VMEM, pltpu.SemaphoreType.DMA
    in_vmem = pl.BlockSpec(memory_space=pltpu.VMEM)
    in_hbm = pl.BlockSpec(memory_space=pl.ANY)
    out = [
        ((supers, slab, width), in_hbm),
        ((supers, slab, width), in_hbm),
        ((supers, part_u, width // prow), in_hbm),
        ((2, supers - 1, part_u, width // prow), in_hbm),
        ((supers, width, cols_here), in_hbm),
        ((supers, width, rows_here), in_hbm),
    ]
    return pl.pallas_call(
        functools.partial(sweep_kernel, (supers, width, blk, prow, nz, rows_here, cols_here, slab)),
        name="sweep",
        out_shape=[jax.ShapeDtypeStruct(dims, f32) for dims, _ in out],
        in_specs=[in_hbm, in_hbm, in_hbm, in_vmem, in_vmem, in_hbm, pl.BlockSpec(memory_space=pltpu.SMEM)],
        out_specs=[spec for _, spec in out],
        scratch_shapes=[
            vmem((rows_here, cols_here), bf16),
            vmem((rows_here, cols_here), bf16),
            vmem((width, cols_here), bf16),
            vmem((width, cols_here), bf16),
            vmem((width, rows_here), bf16),
            vmem((width, rows_here), bf16),
            vmem((2, width, cols_here // 2), f32),
            vmem(((supers + 1) * nz * slab, width), f32),
            vmem((nz * slab, width), f32),
            vmem((2, nz + 1, slab, width), f32),
            vmem((2, cols_here, width), f32),
            vmem((supers, 6, slab // 2, width), f32),
            vmem((supers, width, width), bf16),
            vmem((supers, width, width), bf16),
            vmem((supers - 1, width, width), bf16),
            vmem((supers - 1, width, width), bf16),
            vmem((width, width), bf16),
            vmem((width, width), bf16),
            vmem((2, width, width), f32),
            vmem((prow * width // (2 * prow), width), f32),
            vmem((6, (sums - 1) * width // (4 * prow), width), f32),
            vmem((prow, width // (2 * prow), width), f32),
            vmem((supers, 128, 128), f32),
            vmem((nz, sums * part_u, 128), f32),
            vmem((nz + 1, sums * part_u, 128), f32),
            vmem((sums * part_u, 128), f32),
            vmem((supers, slab, width), f32),
            vmem((supers, slab, width), f32),
            vmem((supers, part_u, width // prow), f32),
            vmem((2, supers - 1, part_u, width // prow), f32),
            dma((2 * nz,)),
            dma((2,)),
            dma,
            dma((supers, 6)),
            dma((supers, 6)),
            dma((supers, nz, 3)),
            dma((supers, nz)),
            dma((supers, nz)),
            dma((supers, 2)),
            dma((supers, 2)),
            dma((supers, nz)),
            dma((supers, nz + 1)),
            dma((supers, 6)),
            dma((supers, 6)),
            dma((supers,)),
            dma((supers,)),
            dma((supers, 6)),
            dma((supers, 6)),
            dma((supers, nz)),
            dma((supers, nz + 1)),
            dma((supers,)),
            dma((supers,)),
            pltpu.SemaphoreType.REGULAR,
            pltpu.SemaphoreType.REGULAR,
            pltpu.SemaphoreType.REGULAR((supers,)),
            dma((2, supers)),
            dma((3, supers)),
        ],
        compiler_params=pltpu.CompilerParams(
            collective_id=0, has_side_effects=True, vmem_limit_bytes=67043328
        ),
    )(anc_inverse, lower, upper, lower_edge, upper_edge, diag_inverse, mask)


def place(x, y, corner, cross):
    arrays = (x, y, corner, cross)
    pieces = [(a, i) for a, array in enumerate(arrays[:2]) for i in range(array.shape[0])] + [(2, None), (3, None)]

    def body(*refs):
        srcs, dsts, kept, (get, put) = refs[:4], refs[4:8], refs[8:12], refs[12:]

        def view(ref, i):
            return ref if i is None else ref.at[i]

        def copies(n):
            a, i = pieces[n]
            src, mid, dst = (view(r[a], i) for r in (srcs, kept, dsts))
            return pltpu.make_async_copy(src, mid, get.at[n]), pltpu.make_async_copy(mid, dst, put.at[n])

        for n in range(len(pieces)):
            copies(n)[0].start()
        for n in range(len(pieces)):
            copies(n)[0].wait()
            copies(n)[1].start()
        for n in range(len(pieces)):
            copies(n)[1].wait()

    return pl.pallas_call(
        body,
        name="place",
        out_shape=[jax.ShapeDtypeStruct(one.shape, f32) for one in arrays],
        in_specs=[pl.BlockSpec(memory_space=pl.ANY)] * 4,
        out_specs=[pl.BlockSpec(memory_space=pl.ANY)] * 4,
        scratch_shapes=[pltpu.VMEM(one.shape, f32) for one in arrays]
        + [pltpu.SemaphoreType.DMA((len(pieces),))] * 2,
    )(*arrays)


def per_device(anc_inverse, lower_anc, upper_anc, lower_edge, upper_edge, diag_inverse, tile_mask):
    rows_here, cols_here = anc_inverse.shape
    prow, pcol = lax.axis_size("row"), lax.axis_size("col")
    supers, width = diag_inverse.shape[0], diag_inverse.shape[1]
    blk = width // tile_mask.shape[2]
    shape = (supers, width, blk, prow, pcol, rows_here, cols_here, cols_here // prow)
    args = (anc_inverse, lower_anc, upper_anc, lower_edge, upper_edge, diag_inverse, tile_mask)
    if not fits(shape):
        return general(*args)
    x, y, corner, cross, _, _ = sweep(
        shape,
        anc_inverse,
        jnp.transpose(lower_anc, (1, 2, 0)),
        jnp.transpose(upper_anc, (1, 2, 0)),
        lower_edge,
        upper_edge,
        diag_inverse,
        jnp.transpose(tile_mask, (0, 2, 1)),
    )
    x, y, corner, cross = place(x, y, corner, cross)
    return (
        jnp.transpose(x, (1, 0, 2)),
        jnp.transpose(y, (1, 0, 2))[None, None],
        jnp.transpose(corner, (0, 2, 1)),
        jnp.transpose(cross, (0, 1, 3, 2)),
    )


precise = lax.Precision.HIGH


def contract(left, right, left_dim, right_dim):
    return lax.dot_general(
        left,
        right,
        (((left_dim,), (right_dim,)), ((), ())),
        precision=precise,
        preferred_element_type=jnp.float32,
    )


def row_major(array):
    return with_layout_constraint(array, Layout(major_to_minor=(0, 1)))


def partner(index, step, count):
    if count & (count - 1) == 0:
        return index ^ step
    return (step - index) % count


def exchange(piece_for, axis):
    count = lax.axis_size(axis)
    index = lax.axis_index(axis)
    got = []
    for step in range(count):
        peer = partner(index, step, count)
        piece = piece_for(peer)
        pairs = [(i, partner(i, step, count)) for i in range(count)]
        if any(i != j for i, j in pairs):
            piece = lax.ppermute(piece, axis, pairs)
        got.append((peer, piece))
    return got


def mask_factor(factor, tile_mask, first_row, first_col, blk):
    rows, supers, cols = factor.shape
    blocks = rows // blk
    window = lax.dynamic_slice_in_dim(tile_mask, first_row // blk, blocks, 1).astype(jnp.float32)
    tile_cols = window.shape[2]
    tile_of_col = (first_col + jnp.arange(cols)) // blk
    pick = (tile_of_col[None, :] == jnp.arange(tile_cols)[:, None]).astype(jnp.float32)
    chosen = sum(window[:, :, t, None] * pick[t] for t in range(tile_cols))
    chosen = jnp.transpose(chosen, (1, 0, 2))
    masked = factor.reshape(blocks, blk, supers, cols) * chosen[:, None]
    return jnp.transpose(masked.reshape(rows, supers, cols), (1, 2, 0))


def general(anc_inverse, lower_anc, upper_anc, lower_edge, upper_edge, diag_inverse, tile_mask):
    rows_here, cols_here = anc_inverse.shape
    prow = lax.axis_size("row")
    pcol = lax.axis_size("col")
    supers, width = diag_inverse.shape[0], diag_inverse.shape[1]
    blk = width // tile_mask.shape[2]
    row = lax.axis_index("row")
    col = lax.axis_index("col")
    part_lower = width // prow
    part_upper = width // pcol

    upper_t = mask_factor(upper_anc, tile_mask, row * rows_here, col * part_upper, blk)
    lower_t = mask_factor(lower_anc, tile_mask, col * cols_here, row * part_lower, blk)

    upper_t = lax.all_gather(upper_t, "col", axis=0)
    lower_full = jnp.zeros((supers, prow, part_lower, cols_here), jnp.float32)
    for peer, piece in exchange(lambda _: lower_t, "row"):
        lower_full = lax.dynamic_update_slice(lower_full, piece[:, None], (0, peer, 0, 0))
    lower_full = lower_full.reshape(supers, width, cols_here)
    lower_comb = [-lower_full[0]]
    for s in range(1, supers):
        lower_comb.append(-lower_full[s] - contract(lower_edge[s - 1], lower_comb[-1], 0, 0))
    cols_part = [row_major(contract(anc_inverse, one, 1, 1)) for one in lower_comb]
    cols_mine = [lax.psum_scatter(one, "col", scatter_dimension=0, tiled=True) for one in cols_part]

    upper_full = [upper_t[:, s].reshape(width, rows_here) for s in range(supers)]
    upper_comb = [-upper_full[0]]
    for s in range(1, supers):
        upper_comb.append(-upper_full[s] - contract(upper_edge[s - 1], upper_comb[-1], 1, 0))
    rows_part = [row_major(contract(anc_inverse, one, 0, 1)) for one in upper_comb]

    first = jnp.logical_and(row == 0, col == 0)
    corner = []
    cross_cols = []
    cross_rows = []
    for s in range(supers):
        upper_here = contract(upper_full[s], cols_part[s], 1, 0)
        now = jnp.where(first, diag_inverse[s], 0.0) - upper_here
        if s > 0:
            upper_prev = contract(upper_full[s], cols_part[s - 1], 1, 0)
            lower_prev = lax.dot_general(
                rows_part[s - 1],
                lower_full[s],
                (((0,), (1,)), ((), ())),
                precision=precise,
                preferred_element_type=jnp.float32,
            )
            cross_col = -(lower_prev + contract(corner[-1], lower_edge[s - 1], 1, 0))
            cross_row = -(upper_prev + contract(upper_edge[s - 1], corner[-1], 1, 0))
            now = now - contract(upper_edge[s - 1], cross_col, 1, 0)
            cross_cols.append(cross_col)
            cross_rows.append(cross_row)
        corner.append(now)
    sums = jnp.stack(corner + cross_cols + cross_rows)
    count = sums.shape[0]

    row_slab = cols_here // prow
    rows_mine = [
        sum(
            piece
            for _, piece in exchange(
                lambda peer: lax.dynamic_slice_in_dim(one, peer * row_slab, row_slab, 0), "row"
            )
        )
        for one in rows_part
    ]
    sums, rows_mine = lax.optimization_barrier((sums, rows_mine))
    sums = sum(
        piece
        for _, piece in exchange(
            lambda peer: lax.dynamic_slice_in_dim(sums, peer * part_lower, part_lower, 1), "row"
        )
    )
    sums = jnp.transpose(sums.reshape(count * part_lower, width))
    sums, cols_mine = lax.optimization_barrier((sums, cols_mine))
    sums = lax.psum_scatter(sums, "col", scatter_dimension=0, tiled=True)
    sums = jnp.transpose(sums).reshape(count, part_lower, part_upper)

    x_blocks = jnp.stack(cols_mine, axis=1)
    y_blocks = jnp.stack(rows_mine, axis=1)[None, None]
    z_blocks = sums[:supers]
    cross_blocks = sums[supers:].reshape(2, supers - 1, part_lower, part_upper)
    return (x_blocks, y_blocks, z_blocks, cross_blocks)


def solution(mesh):
    return jax.shard_map(
        per_device,
        mesh=mesh,
        in_specs=(
            P("row", "col"),
            P("col", None, "row"),
            P("row", None, "col"),
            P(),
            P(),
            P(),
            P(),
        ),
        out_specs=(
            P(("row", "col"), None, None),
            P("col", "row", None, None, None),
            P(None, "row", "col"),
            P(None, None, "row", "col"),
        ),
        check_vma=False,
    )
```
